32 devices in a mesh: seq: 2 (over core), wa: 4 (over y, x), wb: 4 (over z).
Axes of the slice: x: 2, y: 2, z: 4, core: 2. Of those that a mesh axis runs over, the one named last changes fastest.
Arguments:
- long_x: bfloat16 [256, 2048], P('seq', 'wb'), may hold values from -6 to 6
- short_x: bfloat16 [2, 64, 2048], P('seq', None, 'wb'), may hold values from -6 to 6
- short_len: int32 [2], P('seq'), may hold values from 1 to 64, as said below
- w_in: bfloat16 [2048, 4096], P('wb', 'wa'), may hold values from -0.125 to 0.125
- w_outgate: bfloat16 [2048, 4096], P(None, ('wa', 'wb')), may hold values from -0.125 to 0.125
- w_gates: bfloat16 [2048, 8], replicated, may hold values from -1 to 1
- conv_weight: float32 [4, 4096], P(None, 'wa'), may hold values from -3 to 3
- w_query: float32 [1024, 4, 4], P('wa'), may hold values from -3 to 3
- w_key: float32 [1024, 4, 4], P('wa'), may hold values from -3 to 3
- w_value: float32 [1024, 4, 4], P('wa'), may hold values from -3 to 3
- igate_bias: float32 [4], replicated, may hold values from -3 to 3
- fgate_bias: float32 [4], replicated, may hold values from 3 to 9
- norm_gain: float32 [4096], P(('wa', 'wb')), may hold values from 0.5 to 1.5
- skip_gain: float32 [4096], P(('wa', 'wb')), may hold values from 0.5 to 1.5
- w_down: bfloat16 [4096, 2048], P(('wa', 'wb')), may hold values from -0.125 to 0.125
Outputs:
- long_y: bfloat16 [256, 2048], P('seq', ('wa', 'wb'))
- short_y: bfloat16 [2, 64, 2048], P('seq', None, ('wa', 'wb'))
- cache_c: float32 [2, 4, 1024, 1024], P('seq', 'wa', 'wb')
- cache_n: float32 [2, 4, 1024], P('seq', 'wa')
- cache_m: float32 [2, 4], P('seq', 'wa')
- cache_conv: bfloat16 [2, 3, 4096], P('seq', None, 'wa')
The draws below stay inside these ranges and needn't reach their ends.
Inputs may be any that keep to these rules, and one draw needn't show every extreme that they name: `short_len`: every slot holds 1 or more valid rows, and some slot exactly 64.
All inputs are finite; a program needn't handle non-finite values.
Results may differ from the reference program's by a relative error of at most 0.024.
Values may be sent and summed in bfloat16 or wider, within the bound.
A program may use at most 128 MiB of HBM per device.

```python
import jax
import jax.numpy as jnp
from jax import lax

D = 2048
INNER = 4096
H = 4
KC = 4
BS = 4
LONG_DEV = 128
SHORT_MAX = 64
LONG_LEN = 256
N_SEQ = 2


def draw_short_len(key, part):
    folded = jax.random.fold_in(key, 11)
    first_key, second_key = jax.random.split(folded, 2)
    lengths = jax.random.randint(second_key, (N_SEQ,), 1, SHORT_MAX + 1)
    fullest = jax.random.randint(first_key, (), 0, N_SEQ)
    lengths = jnp.where(jnp.arange(N_SEQ) == fullest, SHORT_MAX, lengths)
    return lengths.astype(jnp.int32)


def gate_matrix(key):
    folded = jax.random.fold_in(key, 23)
    raw = jnp.clip(jax.random.normal(folded, (D, 2 * H), jnp.float32), -4.0, 4.0)
    return raw * D ** (-0.5)


def draw_w_gates(key, part):
    return gate_matrix(key).astype(jnp.bfloat16)


def draw_long_x(key, part):
    base = jnp.clip(jax.random.normal(jax.random.fold_in(key, 31), (LONG_LEN, D), jnp.float32), -6.0, 6.0)
    return base.astype(jnp.bfloat16)


def draw_short_x(key, part):
    base = jnp.clip(jax.random.normal(jax.random.fold_in(key, 41), (N_SEQ, SHORT_MAX, D), jnp.float32), -6.0, 6.0)
    return base.astype(jnp.bfloat16)


def raised(values, own_key, source, target, shards_of, factor):
    def block_of(axis_at):
        return (jnp.arange(values.shape[axis_at]) // (values.shape[axis_at] // shards_of)).reshape((-1,) + (1,) * (values.ndim - 1 - axis_at))

    near = jax.random.permutation(own_key, shards_of)[block_of(target)]
    far = (block_of(target) + shards_of // 2) % shards_of
    return jnp.where((block_of(source) == near) | (block_of(source) == far), factor * values, values)


def block_levels(rng, dims, cuts, least, top_value):
    gain = 1.0
    for dim, blocks in cuts:
        draws = jax.random.uniform(jax.random.fold_in(jax.random.fold_in(rng, 6), dim), (blocks,), jnp.float32, least / len(cuts), top_value / len(cuts))
        gain = gain * jnp.repeat(jnp.exp(draws), dims[dim] // blocks).reshape((-1,) + (1,) * (len(dims) - 1 - dim))
    return gain


def noise(stream_key, shape, width, reach, shards=(), held_as=jnp.bfloat16):
    factor_of = block_levels(stream_key, shape, shards, -0.22, 0.18) if shards else 1.0
    drawn = jax.random.normal(stream_key, shape, jnp.float32) * width * factor_of
    return jnp.minimum(jnp.maximum(drawn, -reach), reach).astype(held_as)


def bell_draw_with(own_key, extent, width, bound, cuts, heavy, dtype=jnp.bfloat16):
    values = width * jax.random.normal(own_key, extent, jnp.float32)
    if cuts:
        values = values * block_levels(own_key, extent, cuts, -0.22, 0.18)
    return jnp.clip(raised(values, jax.random.fold_in(own_key, 3), *heavy), -bound, bound).astype(dtype)


def setup_inputs(seed: int = 0) -> dict:
    keys = jax.random.split(jax.random.key(seed), 16)
    long_x = draw_long_x(jax.random.fold_in(keys[15], 71), 0)
    short_x = draw_short_x(jax.random.fold_in(keys[15], 71), 0)
    short_len = draw_short_len(jax.random.fold_in(keys[15], 71), 0)
    w_in = noise(keys[3], (D, INNER), D ** -0.5, 0.125, ((0, 4), (1, 4)))
    w_outgate = noise(keys[4], (D, INNER), D ** -0.5, 0.125, ((1, 16),))
    w_gates = draw_w_gates(jax.random.fold_in(keys[15], 71), 0)
    conv_weight = noise(keys[6], (KC, INNER), KC ** -0.5, 3.0, ((1, 4),), jnp.float32)
    w_query = noise(keys[7], (INNER // BS, BS, BS), BS ** -0.5, 3.0, ((0, 4),), jnp.float32)
    w_key = noise(keys[8], (INNER // BS, BS, BS), BS ** -0.5, 3.0, ((0, 4),), jnp.float32)
    w_value = noise(keys[9], (INNER // BS, BS, BS), BS ** -0.5, 3.0, ((0, 4),), jnp.float32)
    igate_bias = noise(keys[10], (H,), 1.0, 3.0, (), jnp.float32)
    fgate_bias = jnp.clip(jax.random.uniform(keys[11], (H,), jnp.float32, 3.0, 9.0), 3.0, 9.0)
    norm_gain = jnp.clip(1.0 + 0.1 * jax.random.normal(keys[12], (INNER,), jnp.float32), 0.5, 1.5)
    skip_gain = jnp.clip(0.5 + 1.0 * jax.random.uniform(keys[13], (INNER,), jnp.float32) ** block_levels(keys[13], (INNER,), ((0, 16),), -0.2, 0.2), 0.5, 1.5)
    w_down = bell_draw_with(keys[14], (INNER, D), INNER ** -0.5, 0.125, ((0, 16),), (0, 1, 16, 2.0))
    return {"long_x": long_x, "short_x": short_x, "short_len": short_len, "w_in": w_in, "w_outgate": w_outgate, "w_gates": w_gates, "conv_weight": conv_weight, "w_query": w_query, "w_key": w_key, "w_value": w_value, "igate_bias": igate_bias, "fgate_bias": fgate_bias, "norm_gain": norm_gain, "skip_gain": skip_gain, "w_down": w_down}


NEG_FILL = -1e+30
EPSILON = 1e-05
exact_mode = lax.Precision.HIGHEST

def block_diagonal(inputs, blocks):
    row_count = inputs.shape[0]
    grouped = inputs.reshape(row_count, blocks.shape[0], blocks.shape[1])
    combined = jnp.einsum('rni,nio->rno', grouped, blocks, precision=exact_mode)
    return combined.reshape(row_count, -1)

def causal_conv(mlstm_in, previous, conv_weight):
    extended = jnp.concatenate([previous.astype(jnp.float32), mlstm_in.astype(jnp.float32)], axis=0)
    row_count = mlstm_in.shape[0]
    running = jnp.zeros(mlstm_in.shape, jnp.float32)
    for offset in range(conv_weight.shape[0]):
        running = running + conv_weight[offset] * extended[offset:offset + row_count]
    return running

def block_hidden(queries, key_rows, value_rows, in_gate, log_forget, is_valid, carried):
    scaling = key_rows.shape[1] ** (-0.5)
    row_count = queries.shape[0]
    forget_sum = jnp.cumsum(jnp.where(is_valid, log_forget, 0.0))
    positions = jnp.arange(row_count)
    causal = (positions[:, None] >= positions[None, :]) & is_valid[None, :]
    log_weight = jnp.where(causal, forget_sum[:, None] - forget_sum[None, :] + in_gate[None, :], NEG_FILL)
    row_max = lax.optimization_barrier(jnp.max(log_weight, axis=1))
    if carried is not None:
        carry_log = forget_sum + carried[2]
        row_max = jnp.maximum(row_max, carry_log)
    weights = jnp.where(causal, jnp.exp(log_weight - row_max[:, None]), 0.0)
    scores = jnp.dot(queries, key_rows.T, preferred_element_type=jnp.float32) * scaling
    mixing = scores * weights
    denominator = lax.optimization_barrier(jnp.sum(mixing, axis=1))
    numerator = jnp.dot(mixing.astype(jnp.bfloat16), value_rows, preferred_element_type=jnp.float32)
    if carried is not None:
        carry_weight = jnp.exp(carry_log - row_max)
        query_wide = queries.astype(jnp.float32)
        numerator = numerator + carry_weight[:, None] * jnp.dot(query_wide, carried[0].T, precision=exact_mode)
        denominator = denominator + carry_weight * jnp.dot(query_wide, carried[1], precision=exact_mode)
    return numerator / jnp.maximum(jnp.abs(denominator), jnp.exp(-row_max))[:, None]

def block_state(key_rows, value_rows, in_gate, log_forget, is_valid):
    scaling = key_rows.shape[1] ** (-0.5)
    forget_sum = jnp.cumsum(jnp.where(is_valid, log_forget, 0.0))
    forget_total = forget_sum[-1]
    end_log = jnp.where(is_valid, forget_total - forget_sum + in_gate, NEG_FILL)
    end_max = jnp.max(end_log)
    end_weight = jnp.where(is_valid, jnp.exp(end_log - end_max), 0.0)
    key_wide = key_rows.astype(jnp.float32) * scaling
    matrix_state = jnp.dot((value_rows.astype(jnp.float32) * end_weight[:, None]).T, key_wide, precision=exact_mode)
    normalizer = jnp.dot(end_weight, key_wide, precision=exact_mode)
    return (matrix_state, normalizer, end_max, forget_total)

def merge_states(earlier, latter):
    state_a, normal_a, max_a, forget_a = earlier
    state_b, normal_b, max_b, forget_b = latter
    shifted = max_a + forget_b
    joined = jnp.maximum(shifted, max_b)
    weight_a = jnp.exp(shifted - joined)
    weight_b = jnp.exp(max_b - joined)
    return (weight_a * state_a + weight_b * state_b, weight_a * normal_a + weight_b * normal_b, joined, forget_a + forget_b)

def edge_rows(rows, length, rim):
    select = (jnp.arange(rows.shape[0])[None, :] == length - rim + jnp.arange(rim)[:, None]).astype(jnp.float32)
    return jnp.dot(select, rows.astype(jnp.float32), precision=exact_mode).astype(jnp.bfloat16)

def head_major(rows, heads):
    return rows.reshape(rows.shape[0], heads, -1).transpose(1, 0, 2)

def reference(long_x, short_x, short_len, w_in, w_outgate, w_gates, conv_weight, w_query, w_key, w_value, igate_bias, fgate_bias, norm_gain, skip_gain, w_down):
    heads = igate_bias.shape[0]
    rim = conv_weight.shape[0] - 1
    inner = w_in.shape[1]
    head_width = inner // heads

    def prepare(inputs, segments):
        mlstm_in = jnp.dot(inputs, w_in, preferred_element_type=jnp.float32).astype(jnp.bfloat16)
        gate_out = jnp.dot(inputs, w_outgate, preferred_element_type=jnp.float32)
        gate_pre = jnp.dot(inputs, w_gates, preferred_element_type=jnp.float32)
        in_gate = gate_pre[:, :heads] + igate_bias
        log_forget = jax.nn.log_sigmoid(gate_pre[:, heads:] + fgate_bias)
        pieces = mlstm_in.reshape(segments, -1, inner)
        empty_rim = jnp.zeros((rim, inner), jnp.bfloat16)
        conv_out = jax.vmap(causal_conv, in_axes=(0, None, None))(pieces, empty_rim, conv_weight)
        activated = jax.nn.silu(conv_out.reshape(-1, inner))
        queries = block_diagonal(activated, w_query).astype(jnp.bfloat16)
        key_rows = block_diagonal(activated, w_key).astype(jnp.bfloat16)
        value_rows = block_diagonal(mlstm_in.astype(jnp.float32), w_value).astype(jnp.bfloat16)
        return (mlstm_in, gate_out, activated, queries, key_rows, value_rows, in_gate, log_forget)

    def finish(hidden, activated, gate_out, row_valid):
        mean = lax.optimization_barrier(jnp.mean(hidden, axis=2, keepdims=True))
        square = lax.optimization_barrier(jnp.mean(hidden * hidden, axis=2, keepdims=True))
        normed = (hidden - mean) * lax.rsqrt(square - mean * mean + EPSILON)
        flat = normed.transpose(1, 0, 2).reshape(hidden.shape[1], -1) * norm_gain
        gated = ((flat + skip_gain * activated) * jax.nn.silu(gate_out) * row_valid[:, None]).astype(jnp.bfloat16)
        return jnp.dot(gated, w_down, preferred_element_type=jnp.float32).astype(jnp.bfloat16)
    long_in, long_gate, long_act, long_q, long_k, long_v, long_i, long_f = prepare(long_x, 1)

    def to_blocks(rows):
        return head_major(rows, heads).reshape(heads, N_SEQ, LONG_DEV, -1).transpose(1, 0, 2, 3)

    def gate_blocks(rows):
        return rows.reshape(N_SEQ, LONG_DEV, heads).transpose(0, 2, 1)
    all_valid = jnp.ones((LONG_DEV,), bool)
    hidden_map = jax.vmap(block_hidden, in_axes=(0, 0, 0, 0, 0, None, 0))
    state_map = jax.vmap(block_state, in_axes=(0, 0, 0, 0, None))

    def long_step(carry, block):
        block_q, block_k, block_v, block_i, block_f = block
        hidden = hidden_map(block_q, block_k, block_v, block_i, block_f, all_valid, carry)
        local = state_map(block_k, block_v, block_i, block_f, all_valid)
        return (jax.vmap(merge_states)(carry, local), hidden)
    start = (jnp.zeros((heads, head_width, head_width), jnp.float32), jnp.zeros((heads, head_width), jnp.float32), jnp.full((heads,), NEG_FILL, jnp.float32), jnp.zeros((heads,), jnp.float32))
    blocks = (to_blocks(long_q), to_blocks(long_k), to_blocks(long_v), gate_blocks(long_i), gate_blocks(long_f))
    long_final, long_hidden = lax.scan(long_step, start, blocks)
    long_hidden = long_hidden.transpose(1, 0, 2, 3).reshape(heads, N_SEQ * LONG_DEV, head_width)
    long_y = finish(long_hidden, long_act, long_gate, jnp.ones((N_SEQ * LONG_DEV,), jnp.float32))
    flat_short = short_x.reshape(N_SEQ * SHORT_MAX, -1)
    short_in, short_gate, short_act, short_q, short_k, short_v, short_i, short_f = prepare(flat_short, N_SEQ)

    def slot_blocks(rows):
        return head_major(rows, heads).reshape(heads, N_SEQ, SHORT_MAX, -1).transpose(1, 0, 2, 3)

    def slot_gates(rows):
        return rows.reshape(N_SEQ, SHORT_MAX, heads).transpose(0, 2, 1)
    free_map = jax.vmap(block_hidden, in_axes=(0, 0, 0, 0, 0, None, None))

    def slot_work(slot):
        slot_q, slot_k, slot_v, slot_i, slot_f, length = slot
        slot_valid = jnp.arange(SHORT_MAX) < length
        hidden = free_map(slot_q, slot_k, slot_v, slot_i, slot_f, slot_valid, None)
        local = state_map(slot_k, slot_v, slot_i, slot_f, slot_valid)
        return (hidden, local)
    short_hidden, short_states = lax.map(slot_work, (slot_blocks(short_q), slot_blocks(short_k), slot_blocks(short_v), slot_gates(short_i), slot_gates(short_f), short_len))
    short_hidden = short_hidden.transpose(1, 0, 2, 3).reshape(heads, N_SEQ * SHORT_MAX, head_width)
    row_valid = (jnp.arange(SHORT_MAX)[None, :] < short_len[:, None]).reshape(-1).astype(jnp.float32)
    short_y = finish(short_hidden, short_act, short_gate, row_valid).reshape(N_SEQ, SHORT_MAX, -1)
    short_edges = jax.vmap(edge_rows, in_axes=(0, 0, None))(short_in.reshape(N_SEQ, SHORT_MAX, inner), short_len, rim)
    long_edge = long_in[N_SEQ * LONG_DEV - rim:]
    is_last = jnp.arange(N_SEQ) == N_SEQ - 1
    cache_c = jnp.where(is_last[:, None, None, None], long_final[0][None], short_states[0])
    cache_n = jnp.where(is_last[:, None, None], long_final[1][None], short_states[1])
    cache_m = jnp.where(is_last[:, None], long_final[2][None], short_states[2])
    cache_conv = jnp.where(is_last[:, None, None], long_edge[None], short_edges)
    return (long_y, short_y, cache_c, cache_n, cache_m, cache_conv)
```

```python
import functools

import jax
import jax.numpy as jnp
from jax import lax
from jax.experimental import pallas as pl
from jax.experimental.pallas import tpu as pltpu
from jax.sharding import PartitionSpec as P

MESH = pl.DeviceIdType.MESH
NEG_FILL = -1e30
EPSILON = 1e-05
exact_mode = lax.Precision.HIGHEST


def passed_along(array, axis, by):
    devices = lax.axis_size(axis)
    pairs = [(i, i + by) for i in range(devices) if 0 <= i + by < devices]
    return lax.ppermute(array, axis, pairs)


def entering(array, axis, combine, identity):
    devices, index = (lax.axis_size(axis), lax.axis_index(axis))
    everything = jax.tree.map(lambda part: lax.all_gather(part, axis), array)
    start = jax.tree.map(
        lambda part, zero: jnp.broadcast_to(jnp.asarray(zero, part.dtype), part.shape),
        array,
        identity,
    )

    def turn(k, before):
        reached = k < index
        new = combine(before, jax.tree.map(lambda part: part[k], everything))
        return jax.tree.map(lambda a, b: jnp.where(reached, a, b), new, before)

    return lax.fori_loop(0, devices, turn, start)


def block_diagonal(inputs, blocks):
    row_count = inputs.shape[0]
    grouped = inputs.reshape(row_count, blocks.shape[0], blocks.shape[1])
    combined = jnp.einsum("rni,nio->rno", grouped, blocks, precision=exact_mode)
    return combined.reshape(row_count, -1)


def causal_conv(mlstm_in, previous, conv_weight):
    extended = jnp.concatenate([previous.astype(jnp.float32), mlstm_in.astype(jnp.float32)], axis=0)
    row_count = mlstm_in.shape[0]
    running = jnp.zeros(mlstm_in.shape, jnp.float32)
    for offset in range(conv_weight.shape[0]):
        running = running + conv_weight[offset] * extended[offset : offset + row_count]
    return running


def running_sum(row):
    at = jnp.arange(row.shape[0])
    return jnp.sum(jnp.where(at[:, None] >= at[None, :], row[None, :], 0.0), axis=1)


def block_hidden(queries, key_rows, value_rows, in_gate, log_forget, is_valid, carried):
    scaling = key_rows.shape[1] ** (-0.5)
    row_count = queries.shape[0]
    forget_sum = running_sum(jnp.where(is_valid, log_forget, 0.0))
    positions = jnp.arange(row_count)
    causal = (positions[:, None] >= positions[None, :]) & is_valid[None, :]
    log_weight = jnp.where(
        causal, forget_sum[:, None] - forget_sum[None, :] + in_gate[None, :], NEG_FILL
    )
    row_max = jnp.max(log_weight, axis=1)
    if carried is not None:
        carry_log = forget_sum + carried[2]
        row_max = jnp.maximum(row_max, carry_log)
    weights = jnp.where(causal, jnp.exp(log_weight - row_max[:, None]), 0.0)
    scores = jnp.dot(queries, key_rows.T, preferred_element_type=jnp.float32) * scaling
    mixing = scores * weights
    denominator = jnp.sum(mixing, axis=1)
    numerator = jnp.dot(mixing.astype(jnp.bfloat16), value_rows, preferred_element_type=jnp.float32)
    if carried is not None:
        carry_weight = jnp.exp(carry_log - row_max)
        query_wide = queries.astype(jnp.float32)
        numerator = numerator + carry_weight[:, None] * jnp.dot(
            query_wide, carried[0].T, precision=exact_mode
        )
        denominator = denominator + carry_weight * jnp.dot(
            query_wide, carried[1], precision=exact_mode
        )
    return numerator / jnp.maximum(jnp.abs(denominator), jnp.exp(-row_max))[:, None]


def block_state(key_rows, value_rows, in_gate, log_forget, is_valid):
    scaling = key_rows.shape[1] ** (-0.5)
    forget_sum = running_sum(jnp.where(is_valid, log_forget, 0.0))
    forget_total = forget_sum[-1]
    end_log = jnp.where(is_valid, forget_total - forget_sum + in_gate, NEG_FILL)
    end_max = jnp.max(end_log)
    end_weight = jnp.where(is_valid, jnp.exp(end_log - end_max), 0.0)
    key_wide = key_rows.astype(jnp.float32) * scaling
    matrix_state = jnp.dot(
        (value_rows.astype(jnp.float32) * end_weight[:, None]).T, key_wide, precision=exact_mode
    )
    normalizer = jnp.dot(end_weight, key_wide, precision=exact_mode)
    return (matrix_state, normalizer, end_max, forget_total)


def merge_states(earlier, latter):
    state_a, normal_a, max_a, forget_a = earlier
    state_b, normal_b, max_b, forget_b = latter
    shifted = max_a + forget_b
    joined = jnp.maximum(shifted, max_b)
    weight_a = jnp.exp(shifted - joined)
    weight_b = jnp.exp(max_b - joined)
    return (
        weight_a * state_a + weight_b * state_b,
        weight_a * normal_a + weight_b * normal_b,
        joined,
        forget_a + forget_b,
    )


def edge_rows(rows, length, rim):
    select = (jnp.arange(rows.shape[0])[None, :] == length - rim + jnp.arange(rim)[:, None]).astype(
        jnp.float32
    )
    return jnp.dot(select, rows.astype(jnp.float32), precision=exact_mode).astype(jnp.bfloat16)


def body(
    long_x,
    short_x,
    short_len,
    w_in,
    w_outgate,
    w_gates,
    conv_weight,
    w_query,
    w_key,
    w_value,
    igate_bias,
    fgate_bias,
    norm_gain,
    skip_gain,
    w_down,
):
    long_rows = long_x.shape[0]
    slot_rows = short_x.shape[1]
    heads = igate_bias.shape[0]
    head_width = w_in.shape[1]
    value_width = w_outgate.shape[1]
    block_size = w_value.shape[1]
    rim = conv_weight.shape[0] - 1
    head_index = lax.axis_index("wa")
    column_index = lax.axis_index("wb")
    local_rows = jnp.concatenate([long_x, short_x[0]], axis=0)
    gathered = lax.all_gather(local_rows, "wb", axis=1, tiled=True)
    mlstm_full = jnp.dot(
        gathered, lax.all_gather(w_in, "wb", axis=0, tiled=True), preferred_element_type=jnp.float32
    )
    mlstm_in = mlstm_full.astype(jnp.bfloat16)
    gate_out = jnp.dot(gathered, w_outgate, preferred_element_type=jnp.float32)
    gate_pre = jnp.dot(gathered, w_gates, preferred_element_type=jnp.float32)
    pick = (jnp.arange(heads) == head_index).astype(jnp.float32)
    in_gate = jnp.sum(gate_pre[:, :heads] * pick, axis=1) + jnp.sum(igate_bias * pick)
    log_forget = jax.nn.log_sigmoid(
        jnp.sum(gate_pre[:, heads:] * pick, axis=1) + jnp.sum(fgate_bias * pick)
    )
    long_in = mlstm_in[:long_rows]
    slot_in = mlstm_in[long_rows:]
    previous = passed_along(long_in[long_rows - rim :], "seq", 1)
    long_conv = causal_conv(long_in, previous, conv_weight)
    slot_conv = causal_conv(slot_in, jnp.zeros((rim, head_width), jnp.bfloat16), conv_weight)
    activated = jax.nn.silu(jnp.concatenate([long_conv, slot_conv], axis=0))
    queries = block_diagonal(activated, w_query).astype(jnp.bfloat16)
    key_rows = block_diagonal(activated, w_key).astype(jnp.bfloat16)
    value_blocks = lax.dynamic_slice_in_dim(
        w_value, column_index * (value_width // block_size), value_width // block_size, 0
    )
    value_cols = lax.dynamic_slice_in_dim(mlstm_in, column_index * value_width, value_width, 1)
    value_rows = block_diagonal(value_cols.astype(jnp.float32), value_blocks).astype(jnp.bfloat16)
    long_valid = jnp.ones((long_rows,), bool)
    local_state = block_state(
        key_rows[:long_rows],
        value_rows[:long_rows],
        in_gate[:long_rows],
        log_forget[:long_rows],
        long_valid,
    )
    local_tuple = (
        local_state[0],
        local_state[1],
        jnp.reshape(local_state[2], (1,)),
        jnp.reshape(local_state[3], (1,)),
    )
    identity = (
        jnp.zeros_like(local_state[0]),
        jnp.zeros_like(local_state[1]),
        jnp.full((1,), NEG_FILL, jnp.float32),
        jnp.zeros((1,), jnp.float32),
    )
    prefix = entering(local_tuple, "seq", merge_states, identity)
    carried = (prefix[0], prefix[1], prefix[2][0])
    long_hidden = block_hidden(
        queries[:long_rows],
        key_rows[:long_rows],
        value_rows[:long_rows],
        in_gate[:long_rows],
        log_forget[:long_rows],
        long_valid,
        carried,
    )
    final = merge_states(prefix, local_tuple)
    slot_valid = jnp.arange(slot_rows) < short_len[0]
    slot_hidden = block_hidden(
        queries[long_rows:],
        key_rows[long_rows:],
        value_rows[long_rows:],
        in_gate[long_rows:],
        log_forget[long_rows:],
        slot_valid,
        None,
    )
    slot_state = block_state(
        key_rows[long_rows:],
        value_rows[long_rows:],
        in_gate[long_rows:],
        log_forget[long_rows:],
        slot_valid,
    )
    hidden = jnp.concatenate([long_hidden, slot_hidden], axis=0)
    sums = lax.psum((jnp.sum(hidden, axis=1), jnp.sum(hidden * hidden, axis=1)), "wb")
    mean = sums[0] / head_width
    square = sums[1] / head_width
    normed = (
        (hidden - mean[:, None]) * lax.rsqrt(square - mean * mean + EPSILON)[:, None] * norm_gain
    )
    act_cols = lax.dynamic_slice_in_dim(activated, column_index * value_width, value_width, 1)
    row_valid = jnp.concatenate([long_valid, slot_valid], axis=0).astype(jnp.float32)
    gated = ((normed + skip_gain * act_cols) * jax.nn.silu(gate_out) * row_valid[:, None]).astype(
        jnp.bfloat16
    )
    terms = jnp.dot(gated, w_down, preferred_element_type=jnp.float32)
    mixed = lax.psum_scatter(
        terms.astype(jnp.bfloat16), ("wa", "wb"), scatter_dimension=1, tiled=True
    )
    long_y = mixed[:long_rows]
    short_y = mixed[long_rows:][None]
    slot_edge = edge_rows(slot_in, short_len[0], rim)
    is_last = lax.axis_index("seq") == lax.axis_size("seq") - 1
    cache_c = jnp.where(is_last, final[0], slot_state[0])[None, None]
    cache_n = jnp.where(is_last, final[1], slot_state[1])[None, None]
    cache_m = jnp.reshape(jnp.where(is_last, final[2][0], slot_state[2]), (1, 1))
    cache_conv = jnp.where(is_last, long_in[long_rows - rim :], slot_edge)[None]
    return (long_y, short_y, cache_c, cache_n, cache_m, cache_conv)


def flipped(index, mask):
    out, bit = index, 1
    while bit <= mask:
        if mask & bit:
            out = out + bit - 2 * bit * lax.rem(lax.div(index, bit), 2)
        bit *= 2
    return out


def mega_kernel(
    nwa, nwb, nseq,
    len_hbm, ib_hbm, fb_hbm,
    lx_ref, sx_ref, w_in_hbm, wg_hbm, cw_hbm, wq_hbm, wk_hbm, wv_hbm, gain_hbm, skip_hbm, w_og_hbm, w_down_hbm,
    ly_ref, sy_ref, c_ref, n_ref, m_ref, cc_ref,
    xg, psend, precv, gsend, grecv, mg, tail, ext, act, qs, kb, vb, esend, erecv, hs,
    ga, wd, yacc, zsend, zrecv, wsq, wlo,
    w_in_ref, wg_ref, cw_ref, wq_ref, wk_ref, wv_ref, gain_ref, skip_ref, w_og_ref,
    len_ref, ib_ref, fb_ref,
    p_ss, p_rs, g_ss, g_rs, m_ss, m_rs, x_ss, x_rs, xa_ss, xa_rs, e_ss, e_rs,
    t_ss, t_rs, k_ss, k_rs, v_ss, v_rs, o_ss, o_rs, z_ss, z_rs, d_ss, d_rs, f_ss, f_rs, w_sem,
):
    f32, bf16 = jnp.float32, jnp.bfloat16
    seq, wa, wb = lax.axis_index("seq"), lax.axis_index("wa"), lax.axis_index("wb")
    rl, rs = lx_ref.shape[0], sx_ref.shape[0]
    rows = rl + rs
    kd = lx_ref.shape[1]
    gw = mg.shape[2]
    na, nb = nwa - 1, nwb - 1
    other = lax.rem(seq + 1, nseq)
    loads = []

    def load(src, dst):
        copy = pltpu.make_async_copy(src, dst, w_sem.at[len(loads)])
        copy.start()
        loads.append(copy)
        return copy

    group_a = [flipped(wa, j) for j in range(nwa)]
    group_b = [flipped(wb, i) for i in range(nwb)]
    half = wd.shape[1] // 2
    quarter = wd.shape[2]

    def quarter_of(owner):
        return pl.ds(pl.multiple_of(owner * quarter, 128), quarter)

    first = [load(lx_ref, xg.at[0, 0:rl, :]), load(sx_ref, xg.at[0, rl:rows, :])]
    first += [load(wg_hbm, wg_ref), load(w_in_hbm, w_in_ref)]
    small = [(wq_hbm, wq_ref), (wk_hbm, wk_ref), (wv_hbm, wv_ref), (cw_hbm, cw_ref)]
    small += [(len_hbm, len_ref), (ib_hbm, ib_ref), (fb_hbm, fb_ref)]
    small = [load(src, dst) for src, dst in small]
    late = [load(src, dst) for src, dst in ((gain_hbm, gain_ref), (skip_hbm, skip_ref))]
    late += [load(w_og_hbm, w_og_ref), load(w_down_hbm.at[:, quarter_of(wa)], wd.at[0])]

    barrier = pltpu.get_barrier_semaphore()
    peers_a = [(seq, group_a[j], wb) for j in range(1, nwa)]
    peers_b = [(seq, wa, group_b[i]) for i in range(1, nwb)]
    cross_b = [(other, wa, group_b[i]) for i in range(nwb)]
    peer = cross_b[0]
    everyone = peers_a + peers_b + cross_b
    for p in everyone:
        pl.semaphore_signal(barrier, inc=1, device_id=p, device_id_type=MESH)
    sent = []

    def send(src, dst, ssem, rsem, device):
        copy = pltpu.make_async_remote_copy(
            src_ref=src, dst_ref=dst, send_sem=ssem, recv_sem=rsem,
            device_id=device, device_id_type=MESH,
        )
        copy.start()
        sent.append(copy)
        return copy

    def dot(a, b, dims=((1,), (0,))):
        return lax.dot_general(a, b, (dims, ((), ())), preferred_element_type=f32)

    def columns_of(owner):
        return pl.ds(pl.multiple_of(owner * gw, 128), gw)

    far_first = list(range(nb, 0, -1))
    for c in first:
        c.wait()
    x = xg[0]
    for i in far_first:
        psend[i - 1] = dot(x, w_in_ref[:, columns_of(group_b[i])]).astype(bf16)
    gp = dot(wg_ref[:, pl.ds(pl.multiple_of(wb * kd, 128), kd)], x, ((1,), (1,)))
    gsend[...] = jnp.zeros_like(gsend)
    gsend[:, 0:rows] = gp
    pl.semaphore_wait(barrier, len(everyone))
    copies_p, copies_g, copies_x = [None] * nb, [None] * nb, [None] * nb
    for i in far_first:
        at = i - 1
        copies_p[at] = send(psend.at[at], precv.at[at], p_ss.at[at], p_rs.at[at], peers_b[at])
    part = rows // nwa
    share = pl.ds(pl.multiple_of(wa * part, 16), part)
    for i in far_first:
        at = i - 1
        copies_g[at] = send(gsend, grecv.at[at], g_ss.at[at], g_rs.at[at], peers_b[at])
    for i in far_first:
        at = i - 1
        copies_x[at] = send(
            xg.at[0, share, :], xg.at[i, share, :], x_ss.at[at], x_rs.at[at], peers_b[at]
        )
    mine = pl.ds(pl.multiple_of(seq * half, 16), half)
    copies_d = []
    for j in range(1, nwa):
        copies_d.append(
            send(
                w_down_hbm.at[mine, quarter_of(group_a[j])], wd.at[j, mine, :],
                d_ss.at[j - 1], d_rs.at[j - 1], peers_a[j - 1],
            )
        )
    own = dot(x, w_in_ref[:, columns_of(wb)])

    def halves(a):
        top = a.astype(bf16)
        return top, (a - top.astype(f32)).astype(bf16)

    row_sq = lax.broadcasted_iota(jnp.int32, (gw, gw), 0)
    col_sq = lax.broadcasted_iota(jnp.int32, (gw, gw), 1)
    same = row_sq // 4 == col_sq // 4
    inner = lax.rem(row_sq, 4)
    blocks = wq_ref.shape[2]
    outer = lax.rem(lax.broadcasted_iota(jnp.int32, (4, gw), 1), 4) == lax.broadcasted_iota(
        jnp.int32, (4, gw), 0
    )
    block_at = lax.broadcasted_iota(jnp.int32, (blocks, gw), 0)
    block_of = lax.broadcasted_iota(jnp.int32, (blocks, gw), 1) // 4
    for c in small:
        c.wait()
    for n in range(nwb):
        spread = (block_at == group_b[n] * (gw // 4) + block_of).astype(bf16)
        for kind, ref in enumerate((wq_ref, wk_ref, wv_ref)):
            full = jnp.zeros((gw, gw), f32)
            for i in range(4):
                top, rest = halves(ref[i])
                wide = dot(top, spread) + dot(rest, spread)
                coef = jnp.sum(jnp.where(outer, wide, 0.0), axis=0, keepdims=True)
                full = jnp.where(inner == i, coef, full)
            wsq[kind * nwb + n], wlo[kind * nwb + n] = halves(jnp.where(same, full, 0.0))

    for i in range(1, nwb):
        copies_p[i - 1].wait_recv()
        own = own + precv[i - 1].astype(f32)
    mg[0] = own.astype(bf16)
    copies_m, copies_t = [None] * nb, [None] * nwb
    edge = slice(rl - 16, rl)
    for i in [0] + far_first:
        copies_t[i] = send(mg.at[0, edge, :], tail.at[i], t_ss.at[i], t_rs.at[i], cross_b[i])
    for i in far_first:
        at = i - 1
        copies_m[at] = send(mg.at[0], mg.at[i], m_ss.at[at], m_rs.at[at], peers_b[at])

    gates = gsend[:, 0:rows]
    for c in copies_g:
        c.wait_recv()
    sums = [gsend[:, 0:rows]] + [grecv[i][:, 0:rows] for i in range(nb)]
    while len(sums) > 1:
        sums = [sums[i] + sums[i + 1] for i in range(0, len(sums), 2)]
    gates = sums[0]
    heads = gates.shape[0] // 2
    row_id = lax.broadcasted_iota(jnp.int32, gates.shape, 0)
    ig = jnp.sum(jnp.where(row_id == wa, gates, 0.0), axis=0, keepdims=True) + ib_ref[wa]
    fg = jnp.sum(jnp.where(row_id == wa + heads, gates, 0.0), axis=0, keepdims=True) + fb_ref[wa]
    lf = jnp.minimum(fg, 0.0) - jnp.log1p(jnp.exp(-jnp.abs(fg)))
    length = len_ref[0]
    last = seq == nseq - 1

    def block_gates(i_row, f_row, size, limit):
        t = lax.broadcasted_iota(jnp.int32, (size, size), 0)
        s = lax.broadcasted_iota(jnp.int32, (size, size), 1)
        valid = lax.broadcasted_iota(jnp.int32, (1, size), 1) < limit
        f_row = jnp.where(valid, f_row, 0.0)
        b_col = jnp.sum(jnp.where(s <= t, f_row, 0.0), axis=1, keepdims=True)
        b_row = jnp.sum(jnp.where(s == t, b_col, 0.0), axis=0, keepdims=True)
        total = jnp.sum(f_row, axis=1, keepdims=True)
        e_row = jnp.where(valid, total - b_row + i_row, NEG_FILL)
        causal = (s <= t) & (s < limit)
        logw = jnp.where(causal, b_col - b_row + i_row, NEG_FILL)
        return b_col, total, e_row, causal, logw

    def to_col(row):
        size = row.shape[1]
        t = lax.broadcasted_iota(jnp.int32, (size, size), 0)
        s = lax.broadcasted_iota(jnp.int32, (size, size), 1)
        return jnp.sum(jnp.where(s == t, row, 0.0), axis=1, keepdims=True)

    bl, totl, el, causl, logl = block_gates(ig[:, 0:rl], lf[:, 0:rl], rl, rl)
    bs, tots, es, causs, logs = block_gates(ig[:, rl:rows], lf[:, rl:rows], rs, length)
    esend[...] = jnp.broadcast_to(el, esend.shape)
    ce = send(esend, erecv, e_ss.at[0], e_rs.at[0], peer)
    pick_row = lax.broadcasted_iota(jnp.int32, (8, rows), 0)
    pick_at = lax.broadcasted_iota(jnp.int32, (8, rows), 1)
    slot_at = length - 3 + pick_row
    target = jnp.where(last, rl - 3 + pick_row, jnp.where(slot_at >= 0, rl + slot_at, -1))
    pick = (pick_at == target).astype(bf16)
    first_keep = jnp.where(seq > 0, 1.0, 0.0)
    scale = (gw * nwb) ** (-0.5)
    sl = jnp.zeros((rl, rl), f32)
    ss = jnp.zeros((rs, rs), f32)
    copies_k, copies_v, copies_xa, copies_f = [], [], [], []
    for n in range(nwb):
        if n:
            copies_m[n - 1].wait_recv()
        lanes = columns_of(group_b[n])
        m = mg[n]
        v = (dot(m, wsq[2 * nwb + n]) + dot(m, wlo[2 * nwb + n])).astype(bf16)
        vb[n, rl : rl + rows, :] = v
        copies_v.append(
            send(vb.at[n, rl : 2 * rl, :], vb.at[n, 0:rl, :], v_ss.at[n], v_rs.at[n], peer)
        )
        cc_ref[:, lanes] = dot(pick, m)[0:3].astype(bf16)
        wide = m.astype(f32)
        copies_t[n].wait_recv()
        ext[0:8, :] = tail[n].astype(f32)[8:16] * first_keep
        ext[8 : 8 + rl, :] = wide[0:rl]
        ext[8 + rl : 16 + rl, :] = jnp.zeros((8, gw), f32)
        ext[16 + rl : 16 + rows, :] = wide[rl:rows]
        taps = cw_ref[:, lanes]
        for base, start, size in ((5, 0, rl), (13 + rl, rl, rs)):
            conv = jnp.zeros((size, gw), f32)
            for j in range(4):
                conv = conv + taps[j : j + 1] * ext[base + j : base + j + size, :]
            act[n, start : start + size, :] = conv / (1.0 + jnp.exp(-conv))
        top, rest = halves(act[n])
        wk, wq = nwb + n, n
        k = (dot(top, wsq[wk]) + dot(rest, wsq[wk]) + dot(top, wlo[wk])).astype(bf16)
        kb[n, rl : rl + rows, :] = k
        copies_k.append(
            send(kb.at[n, rl : 2 * rl, :], kb.at[n, 0:rl, :], k_ss.at[n], k_rs.at[n], peer)
        )
        q = (dot(top, wsq[wq]) + dot(rest, wsq[wq]) + dot(top, wlo[wq])).astype(bf16)
        qs[n] = q
        sl = sl + dot(q[0:rl], k[0:rl], ((1,), (1,)))
        ss = ss + dot(q[rl:rows], k[rl:rows], ((1,), (1,)))
        if n == 0:
            for i in far_first[::-1]:
                copies_x[i - 1].wait_recv()
                src = xg.at[i, share, :]
                for j in range(na):
                    at = (i - 1) * na + j
                    copies_xa.append(send(src, src, xa_ss.at[at], xa_rs.at[at], peers_a[j]))
            for j in range(na):
                copies_d[j].wait_recv()
                src = wd.at[j + 1, mine, :]
                copies_f.append(send(src, src, f_ss.at[j], f_rs.at[j], peer))

    for c in late:
        c.wait()
    for c in copies_xa:
        c.wait_recv()
    inv = 1.0 / (gw * nwb)
    gain, skip = gain_ref[...], skip_ref[...]
    gate = jnp.zeros((rows, gw), f32)
    for i in range(nwb):
        gate = gate + dot(xg[i], w_og_ref[pl.ds(pl.multiple_of(group_b[i] * kd, 128), kd), :])
    gate = gate / (1.0 + jnp.exp(-gate))
    copies_o = []

    def gated(start, size, hidden, total, square_sum, keep):
        mean = total * inv
        norm = lax.rsqrt(square_sum * inv - mean * mean + EPSILON)
        normed = (hidden - mean) * norm * gain
        out = (normed + skip * act[0, start : start + size, :]) * gate[start : start + size]
        return (out if keep is None else out * keep).astype(bf16)

    def share_out(start, size):
        span = slice(start, start + size)
        row = len(copies_o)
        copies_o.append([])
        for j in range(1, nwa):
            at = row * na + j - 1
            copies_o[-1].append(
                send(ga.at[0, span, :], ga.at[j, span, :], o_ss.at[at], o_rs.at[at], peers_a[j - 1])
            )

    rmax_s = jnp.max(logs, axis=1, keepdims=True)
    mix_s = ss * scale * jnp.where(causs, jnp.exp(logs - rmax_s), 0.0)
    den_s = jnp.sum(mix_s, axis=1, keepdims=True)
    div_s = jnp.maximum(jnp.abs(den_s), jnp.exp(-rmax_s))
    mix_s = mix_s.astype(bf16)
    sum_s = jnp.zeros((rs, 1), f32)
    sq_s = jnp.zeros((rs, 1), f32)
    for n in range(nwb):
        hh = dot(mix_s, vb[n, 2 * rl : rl + rows, :]) / div_s
        if n == 0:
            own_s = hh
        sum_s += jnp.sum(hh, axis=1, keepdims=True)
        sq_s += jnp.sum(hh * hh, axis=1, keepdims=True)
    ok_s = (lax.broadcasted_iota(jnp.int32, (rs, 1), 0) < length).astype(f32)
    ga[0, rl:rows, :] = gated(rl, rs, own_s, sum_s, sq_s, ok_s)
    share_out(rl, rs)

    ce.wait_recv()
    ep = erecv[0:1, :]
    mp = jnp.max(ep, axis=1, keepdims=True)
    carry_m = jnp.where(seq > 0, mp, NEG_FILL)
    carry_log = bl + carry_m
    rmax_l = jnp.maximum(jnp.max(logl, axis=1, keepdims=True), carry_log)
    mix_l = sl * scale * jnp.where(causl, jnp.exp(logl - rmax_l), 0.0)
    for c in copies_k + copies_v:
        c.wait_recv()
    sp = jnp.zeros((rl, rl), f32)
    for n in range(nwb):
        sp = sp + dot(qs[n, 0:rl, :], kb[n, 0:rl, :], ((1,), (1,)))
    mix_p = sp * scale * jnp.exp(ep - mp) * jnp.exp(carry_log - rmax_l)
    den_l = jnp.sum(mix_l, axis=1, keepdims=True) + jnp.sum(mix_p, axis=1, keepdims=True)
    div_l = jnp.maximum(jnp.abs(den_l), jnp.exp(-rmax_l))
    mix = jnp.concatenate([mix_p, mix_l], axis=1).astype(bf16)
    sum_l = jnp.zeros((rl, 1), f32)
    sq_l = jnp.zeros((rl, 1), f32)
    for n in range(nwb):
        hl = dot(mix, vb[n, 0 : 2 * rl, :]) / div_l
        if n == 0:
            hs[...] = hl
        sum_l += jnp.sum(hl, axis=1, keepdims=True)
        sq_l += jnp.sum(hl * hl, axis=1, keepdims=True)
    step = rl // 2
    for start in (0, step):
        span = slice(start, start + step)
        ga[0, span, :] = gated(start, step, hs[span, :], sum_l[span], sq_l[span], None)
        share_out(start, step)

    ml = jnp.max(el, axis=1, keepdims=True)
    shifted = carry_m + totl
    joined = jnp.maximum(shifted, ml)
    ms = jnp.max(es, axis=1, keepdims=True)
    m_ref[...] = jnp.where(last, joined, ms)
    keep_p = jnp.where(last & (seq > 0), 1.0, 0.0)
    keep_l = jnp.where(last, 1.0, 0.0)
    wp = to_col(jnp.exp(ep - mp) * jnp.exp(shifted - joined)) * (keep_p * scale)
    wl = to_col(jnp.exp(el - joined)) * (keep_l * scale)
    ws = to_col(jnp.where(es > 0.5 * NEG_FILL, jnp.exp(es - ms), 0.0)) * ((1.0 - keep_l) * scale)
    weight = jnp.concatenate([wp, wl, ws], axis=0)
    vw = (vb[0].astype(f32) * weight).astype(bf16)
    for n in range(nwb):
        lanes = columns_of(group_b[n])
        keys = kb[n]
        c_ref[:, lanes] = dot(vw, keys, ((0,), (0,)))
        n_ref[:, lanes] = jnp.sum(keys.astype(f32) * weight, axis=0, keepdims=True)

    for c in copies_f:
        c.wait_recv()
    ow = zrecv.shape[2]
    copies_z = []
    spans = [(rl, rs), (0, step), (step, step)]

    def piece_of(owner):
        return pl.ds(pl.multiple_of(owner * ow, 128), ow)

    for row, (start, size) in enumerate(spans):
        span = slice(start, start + size)
        y = dot(ga[0, span, :], wd[0])
        for j in range(1, nwa):
            copies_o[row][j - 1].wait_recv()
            y = y + dot(ga[j, span, :], wd[j])
        yacc[span, :] = y
        copies_z.append([])
        for i in range(1, nwb):
            at = row * nb + i - 1
            zsend[i - 1, span, :] = yacc[span, piece_of(group_b[i])].astype(bf16)
            copies_z[-1].append(
                send(
                    zsend.at[i - 1, span, :], zrecv.at[i - 1, span, :],
                    z_ss.at[at], z_rs.at[at], peers_b[i - 1],
                )
            )
    for row, (start, size) in enumerate(spans):
        span = slice(start, start + size)
        y = yacc[span, piece_of(wb)]
        for i in range(nb):
            copies_z[row][i].wait_recv()
            y = y + zrecv[i, span, :].astype(f32)
        if start == rl:
            sy_ref[...] = y.astype(bf16)
        else:
            ly_ref[span, :] = y.astype(bf16)
    for c in sent:
        c.wait_send()


def fused_body(
    long_x, short_x, short_len, w_in, w_outgate, w_gates, conv_weight, w_query, w_key, w_value,
    igate_bias, fgate_bias, norm_gain, skip_gain, w_down,
):
    nseq, nwa, nwb = (lax.axis_size(a) for a in ("seq", "wa", "wb"))
    f32, bf16 = jnp.float32, jnp.bfloat16
    rl, kd = long_x.shape
    rs = short_x.shape[1]
    rows = rl + rs
    gw = w_outgate.shape[1]
    hw = w_in.shape[1]
    ow = w_down.shape[1] // (nwa * nwb)
    turned = [w.transpose(1, 2, 0) for w in (w_query, w_key, w_value)]
    vm = pl.BlockSpec(memory_space=pltpu.VMEM)
    hbm = pl.BlockSpec(memory_space=pl.ANY)
    nb, na = nwb - 1, nwa - 1
    dma = pltpu.SemaphoreType.DMA
    outs = pl.pallas_call(
        functools.partial(mega_kernel, nwa, nwb, nseq),
        out_shape=(
            jax.ShapeDtypeStruct((rl, ow), bf16),
            jax.ShapeDtypeStruct((rs, ow), bf16),
            jax.ShapeDtypeStruct((gw, hw), f32),
            jax.ShapeDtypeStruct((1, hw), f32),
            jax.ShapeDtypeStruct((1, 1), f32),
            jax.ShapeDtypeStruct((3, hw), bf16),
        ),
        in_specs=[hbm] * 15,
        out_specs=(vm,) * 6,
        scratch_shapes=[
            pltpu.VMEM((nwb, rows, kd), bf16),
            pltpu.VMEM((nb, rows, gw), bf16),
            pltpu.VMEM((nb, rows, gw), bf16),
            pltpu.VMEM((8, 256), f32),
            pltpu.VMEM((nb, 8, 256), f32),
            pltpu.VMEM((nwb, rows, gw), bf16),
            pltpu.VMEM((nwb, 16, gw), bf16),
            pltpu.VMEM((16 + rows, gw), f32),
            pltpu.VMEM((nwb, rows, gw), f32),
            pltpu.VMEM((nwb, rows, gw), bf16),
            pltpu.VMEM((nwb, rl + rows, gw), bf16),
            pltpu.VMEM((nwb, rl + rows, gw), bf16),
            pltpu.VMEM((8, rl), f32),
            pltpu.VMEM((8, rl), f32),
            pltpu.VMEM((rl, gw), f32),
            pltpu.VMEM((nwa, rows, gw), bf16),
            pltpu.VMEM((nwa, gw, nwb * ow), bf16),
            pltpu.VMEM((rows, nwb * ow), f32),
            pltpu.VMEM((nb, rows, ow), bf16),
            pltpu.VMEM((nb, rows, ow), bf16),
            pltpu.VMEM((3 * nwb, gw, gw), bf16),
            pltpu.VMEM((3 * nwb, gw, gw), bf16),
            pltpu.VMEM(w_in.shape, bf16),
            pltpu.VMEM(w_gates.shape[::-1], bf16),
            pltpu.VMEM(conv_weight.shape, f32),
            pltpu.VMEM(turned[0].shape, f32),
            pltpu.VMEM(turned[1].shape, f32),
            pltpu.VMEM(turned[2].shape, f32),
            pltpu.VMEM((1, gw), f32),
            pltpu.VMEM((1, gw), f32),
            pltpu.VMEM(w_outgate.shape, bf16),
            pltpu.SMEM(short_len.shape, jnp.int32),
            pltpu.SMEM(igate_bias.shape, f32),
            pltpu.SMEM(fgate_bias.shape, f32),
        ]
        + [dma((nb,))] * 8
        + [dma((nb * na,))] * 2
        + [dma((1,))] * 2
        + [dma((nwb,))] * 6
        + [dma((3 * na,))] * 2
        + [dma((3 * nb,))] * 2
        + [dma((na,))] * 4
        + [dma((15,))],
        compiler_params=pltpu.CompilerParams(
            collective_id=0, has_side_effects=True, vmem_limit_bytes=60 * 2**20
        ),
        name="mlstm_layer",
    )(
        short_len, igate_bias, fgate_bias, long_x, short_x[0], w_in, w_gates.T,
        conv_weight, *turned, norm_gain[None], skip_gain[None], w_outgate, w_down,
    )
    y, sy, c, n, m, edge = outs
    return (y, sy[None], c[None, None], n[None], m, edge[None])


def solution(mesh):
    in_specs = (
        P("seq", "wb"),
        P("seq", None, "wb"),
        P("seq"),
        P("wb", "wa"),
        P(None, ("wa", "wb")),
        P(),
        P(None, "wa"),
        P("wa", None, None),
        P("wa", None, None),
        P("wa", None, None),
        P(),
        P(),
        P(("wa", "wb")),
        P(("wa", "wb")),
        P(("wa", "wb"), None),
    )
    out_specs = (
        P("seq", ("wa", "wb")),
        P("seq", None, ("wa", "wb")),
        P("seq", "wa", "wb", None),
        P("seq", "wa", None),
        P("seq", "wa"),
        P("seq", None, "wa"),
    )
    even = all(mesh.shape[a] & (mesh.shape[a] - 1) == 0 for a in ("wa", "wb"))
    layer = fused_body if mesh.shape["seq"] == 2 and even else body
    return jax.shard_map(layer, mesh=mesh, in_specs=in_specs, out_specs=out_specs, check_vma=False)
```

```python
import functools

import jax
import jax.numpy as jnp
from jax import lax
from jax.experimental import pallas as pl
from jax.experimental.pallas import tpu as pltpu
from jax.sharding import PartitionSpec as P

MESH = pl.DeviceIdType.MESH
NEG_FILL = -1e30
EPSILON = 1e-05
exact_mode = lax.Precision.HIGHEST


def passed_along(array, axis, by):
    devices = lax.axis_size(axis)
    pairs = [(i, i + by) for i in range(devices) if 0 <= i + by < devices]
    return lax.ppermute(array, axis, pairs)


def entering(array, axis, combine, identity):
    devices, index = (lax.axis_size(axis), lax.axis_index(axis))
    everything = jax.tree.map(lambda part: lax.all_gather(part, axis), array)
    start = jax.tree.map(
        lambda part, zero: jnp.broadcast_to(jnp.asarray(zero, part.dtype), part.shape),
        array,
        identity,
    )

    def turn(k, before):
        reached = k < index
        new = combine(before, jax.tree.map(lambda part: part[k], everything))
        return jax.tree.map(lambda a, b: jnp.where(reached, a, b), new, before)

    return lax.fori_loop(0, devices, turn, start)


def block_diagonal(inputs, blocks):
    row_count = inputs.shape[0]
    grouped = inputs.reshape(row_count, blocks.shape[0], blocks.shape[1])
    combined = jnp.einsum("rni,nio->rno", grouped, blocks, precision=exact_mode)
    return combined.reshape(row_count, -1)


def causal_conv(mlstm_in, previous, conv_weight):
    extended = jnp.concatenate([previous.astype(jnp.float32), mlstm_in.astype(jnp.float32)], axis=0)
    row_count = mlstm_in.shape[0]
    running = jnp.zeros(mlstm_in.shape, jnp.float32)
    for offset in range(conv_weight.shape[0]):
        running = running + conv_weight[offset] * extended[offset : offset + row_count]
    return running


def running_sum(row):
    at = jnp.arange(row.shape[0])
    return jnp.sum(jnp.where(at[:, None] >= at[None, :], row[None, :], 0.0), axis=1)


def block_hidden(queries, key_rows, value_rows, in_gate, log_forget, is_valid, carried):
    scaling = key_rows.shape[1] ** (-0.5)
    row_count = queries.shape[0]
    forget_sum = running_sum(jnp.where(is_valid, log_forget, 0.0))
    positions = jnp.arange(row_count)
    causal = (positions[:, None] >= positions[None, :]) & is_valid[None, :]
    log_weight = jnp.where(
        causal, forget_sum[:, None] - forget_sum[None, :] + in_gate[None, :], NEG_FILL
    )
    row_max = jnp.max(log_weight, axis=1)
    if carried is not None:
        carry_log = forget_sum + carried[2]
        row_max = jnp.maximum(row_max, carry_log)
    weights = jnp.where(causal, jnp.exp(log_weight - row_max[:, None]), 0.0)
    scores = jnp.dot(queries, key_rows.T, preferred_element_type=jnp.float32) * scaling
    mixing = scores * weights
    denominator = jnp.sum(mixing, axis=1)
    numerator = jnp.dot(mixing.astype(jnp.bfloat16), value_rows, preferred_element_type=jnp.float32)
    if carried is not None:
        carry_weight = jnp.exp(carry_log - row_max)
        query_wide = queries.astype(jnp.float32)
        numerator = numerator + carry_weight[:, None] * jnp.dot(
            query_wide, carried[0].T, precision=exact_mode
        )
        denominator = denominator + carry_weight * jnp.dot(
            query_wide, carried[1], precision=exact_mode
        )
    return numerator / jnp.maximum(jnp.abs(denominator), jnp.exp(-row_max))[:, None]


def block_state(key_rows, value_rows, in_gate, log_forget, is_valid):
    scaling = key_rows.shape[1] ** (-0.5)
    forget_sum = running_sum(jnp.where(is_valid, log_forget, 0.0))
    forget_total = forget_sum[-1]
    end_log = jnp.where(is_valid, forget_total - forget_sum + in_gate, NEG_FILL)
    end_max = jnp.max(end_log)
    end_weight = jnp.where(is_valid, jnp.exp(end_log - end_max), 0.0)
    key_wide = key_rows.astype(jnp.float32) * scaling
    matrix_state = jnp.dot(
        (value_rows.astype(jnp.float32) * end_weight[:, None]).T, key_wide, precision=exact_mode
    )
    normalizer = jnp.dot(end_weight, key_wide, precision=exact_mode)
    return (matrix_state, normalizer, end_max, forget_total)


def merge_states(earlier, latter):
    state_a, normal_a, max_a, forget_a = earlier
    state_b, normal_b, max_b, forget_b = latter
    shifted = max_a + forget_b
    joined = jnp.maximum(shifted, max_b)
    weight_a = jnp.exp(shifted - joined)
    weight_b = jnp.exp(max_b - joined)
    return (
        weight_a * state_a + weight_b * state_b,
        weight_a * normal_a + weight_b * normal_b,
        joined,
        forget_a + forget_b,
    )


def edge_rows(rows, length, rim):
    select = (jnp.arange(rows.shape[0])[None, :] == length - rim + jnp.arange(rim)[:, None]).astype(
        jnp.float32
    )
    return jnp.dot(select, rows.astype(jnp.float32), precision=exact_mode).astype(jnp.bfloat16)


def body(
    long_x,
    short_x,
    short_len,
    w_in,
    w_outgate,
    w_gates,
    conv_weight,
    w_query,
    w_key,
    w_value,
    igate_bias,
    fgate_bias,
    norm_gain,
    skip_gain,
    w_down,
):
    long_rows = long_x.shape[0]
    slot_rows = short_x.shape[1]
    heads = igate_bias.shape[0]
    head_width = w_in.shape[1]
    value_width = w_outgate.shape[1]
    block_size = w_value.shape[1]
    rim = conv_weight.shape[0] - 1
    head_index = lax.axis_index("wa")
    column_index = lax.axis_index("wb")
    local_rows = jnp.concatenate([long_x, short_x[0]], axis=0)
    gathered = lax.all_gather(local_rows, "wb", axis=1, tiled=True)
    mlstm_full = jnp.dot(
        gathered, lax.all_gather(w_in, "wb", axis=0, tiled=True), preferred_element_type=jnp.float32
    )
    mlstm_in = mlstm_full.astype(jnp.bfloat16)
    gate_out = jnp.dot(gathered, w_outgate, preferred_element_type=jnp.float32)
    gate_pre = jnp.dot(gathered, w_gates, preferred_element_type=jnp.float32)
    pick = (jnp.arange(heads) == head_index).astype(jnp.float32)
    in_gate = jnp.sum(gate_pre[:, :heads] * pick, axis=1) + jnp.sum(igate_bias * pick)
    log_forget = jax.nn.log_sigmoid(
        jnp.sum(gate_pre[:, heads:] * pick, axis=1) + jnp.sum(fgate_bias * pick)
    )
    long_in = mlstm_in[:long_rows]
    slot_in = mlstm_in[long_rows:]
    previous = passed_along(long_in[long_rows - rim :], "seq", 1)
    long_conv = causal_conv(long_in, previous, conv_weight)
    slot_conv = causal_conv(slot_in, jnp.zeros((rim, head_width), jnp.bfloat16), conv_weight)
    activated = jax.nn.silu(jnp.concatenate([long_conv, slot_conv], axis=0))
    queries = block_diagonal(activated, w_query).astype(jnp.bfloat16)
    key_rows = block_diagonal(activated, w_key).astype(jnp.bfloat16)
    value_blocks = lax.dynamic_slice_in_dim(
        w_value, column_index * (value_width // block_size), value_width // block_size, 0
    )
    value_cols = lax.dynamic_slice_in_dim(mlstm_in, column_index * value_width, value_width, 1)
    value_rows = block_diagonal(value_cols.astype(jnp.float32), value_blocks).astype(jnp.bfloat16)
    long_valid = jnp.ones((long_rows,), bool)
    local_state = block_state(
        key_rows[:long_rows],
        value_rows[:long_rows],
        in_gate[:long_rows],
        log_forget[:long_rows],
        long_valid,
    )
    local_tuple = (
        local_state[0],
        local_state[1],
        jnp.reshape(local_state[2], (1,)),
        jnp.reshape(local_state[3], (1,)),
    )
    identity = (
        jnp.zeros_like(local_state[0]),
        jnp.zeros_like(local_state[1]),
        jnp.full((1,), NEG_FILL, jnp.float32),
        jnp.zeros((1,), jnp.float32),
    )
    prefix = entering(local_tuple, "seq", merge_states, identity)
    carried = (prefix[0], prefix[1], prefix[2][0])
    long_hidden = block_hidden(
        queries[:long_rows],
        key_rows[:long_rows],
        value_rows[:long_rows],
        in_gate[:long_rows],
        log_forget[:long_rows],
        long_valid,
        carried,
    )
    final = merge_states(prefix, local_tuple)
    slot_valid = jnp.arange(slot_rows) < short_len[0]
    slot_hidden = block_hidden(
        queries[long_rows:],
        key_rows[long_rows:],
        value_rows[long_rows:],
        in_gate[long_rows:],
        log_forget[long_rows:],
        slot_valid,
        None,
    )
    slot_state = block_state(
        key_rows[long_rows:],
        value_rows[long_rows:],
        in_gate[long_rows:],
        log_forget[long_rows:],
        slot_valid,
    )
    hidden = jnp.concatenate([long_hidden, slot_hidden], axis=0)
    sums = lax.psum((jnp.sum(hidden, axis=1), jnp.sum(hidden * hidden, axis=1)), "wb")
    mean = sums[0] / head_width
    square = sums[1] / head_width
    normed = (
        (hidden - mean[:, None]) * lax.rsqrt(square - mean * mean + EPSILON)[:, None] * norm_gain
    )
    act_cols = lax.dynamic_slice_in_dim(activated, column_index * value_width, value_width, 1)
    row_valid = jnp.concatenate([long_valid, slot_valid], axis=0).astype(jnp.float32)
    gated = ((normed + skip_gain * act_cols) * jax.nn.silu(gate_out) * row_valid[:, None]).astype(
        jnp.bfloat16
    )
    terms = jnp.dot(gated, w_down, preferred_element_type=jnp.float32)
    mixed = lax.psum_scatter(
        terms.astype(jnp.bfloat16), ("wa", "wb"), scatter_dimension=1, tiled=True
    )
    long_y = mixed[:long_rows]
    short_y = mixed[long_rows:][None]
    slot_edge = edge_rows(slot_in, short_len[0], rim)
    is_last = lax.axis_index("seq") == lax.axis_size("seq") - 1
    cache_c = jnp.where(is_last, final[0], slot_state[0])[None, None]
    cache_n = jnp.where(is_last, final[1], slot_state[1])[None, None]
    cache_m = jnp.reshape(jnp.where(is_last, final[2][0], slot_state[2]), (1, 1))
    cache_conv = jnp.where(is_last, long_in[long_rows - rim :], slot_edge)[None]
    return (long_y, short_y, cache_c, cache_n, cache_m, cache_conv)


def flipped(index, mask):
    out, bit = index, 1
    while bit <= mask:
        if mask & bit:
            out = out + bit - 2 * bit * lax.rem(lax.div(index, bit), 2)
        bit *= 2
    return out


def mega_kernel(
    nwa, nwb, nseq,
    len_hbm, ib_hbm, fb_hbm,
    lx_ref, sx_ref, w_in_hbm, wg_hbm, cw_hbm, wq_hbm, wk_hbm, wv_hbm, gain_hbm, skip_hbm, w_og_hbm, w_down_hbm,
    ly_ref, sy_ref, c_ref, n_ref, m_ref, cc_ref,
    xg, psend, precv, gsend, grecv, mg, tail, ext, act, qs, kb, vb, esend, erecv, hs,
    ga, wd, yacc, zsend, zrecv, wsq, wlo,
    w_in_ref, wg_ref, cw_ref, wq_ref, wk_ref, wv_ref, gain_ref, skip_ref, w_og_ref,
    len_ref, ib_ref, fb_ref,
    p_ss, p_rs, g_ss, g_rs, m_ss, m_rs, x_ss, x_rs, xa_ss, xa_rs, e_ss, e_rs,
    t_ss, t_rs, k_ss, k_rs, v_ss, v_rs, o_ss, o_rs, z_ss, z_rs, d_ss, d_rs, f_ss, f_rs, w_sem,
):
    f32, bf16 = jnp.float32, jnp.bfloat16
    seq, wa, wb = lax.axis_index("seq"), lax.axis_index("wa"), lax.axis_index("wb")
    rl, rs = lx_ref.shape[0], sx_ref.shape[0]
    rows = rl + rs
    kd = lx_ref.shape[1]
    gw = mg.shape[2]
    na, nb = nwa - 1, nwb - 1
    other = lax.rem(seq + 1, nseq)
    loads = []

    def load(src, dst):
        copy = pltpu.make_async_copy(src, dst, w_sem.at[len(loads)])
        copy.start()
        loads.append(copy)
        return copy

    group_a = [flipped(wa, j) for j in range(nwa)]
    group_b = [flipped(wb, i) for i in range(nwb)]
    half = wd.shape[1] // 2
    quarter = wd.shape[2]

    def quarter_of(owner):
        return pl.ds(pl.multiple_of(owner * quarter, 128), quarter)

    first = [load(lx_ref, xg.at[0, 0:rl, :]), load(sx_ref, xg.at[0, rl:rows, :])]
    first += [load(wg_hbm, wg_ref), load(w_in_hbm, w_in_ref)]
    small = [(wq_hbm, wq_ref), (wk_hbm, wk_ref), (wv_hbm, wv_ref), (cw_hbm, cw_ref)]
    small += [(len_hbm, len_ref), (ib_hbm, ib_ref), (fb_hbm, fb_ref)]
    small = [load(src, dst) for src, dst in small]
    late = [load(src, dst) for src, dst in ((gain_hbm, gain_ref), (skip_hbm, skip_ref))]
    late += [load(w_og_hbm, w_og_ref), load(w_down_hbm.at[:, quarter_of(wa)], wd.at[0])]

    barrier = pltpu.get_barrier_semaphore()
    peers_a = [(seq, group_a[j], wb) for j in range(1, nwa)]
    peers_b = [(seq, wa, group_b[i]) for i in range(1, nwb)]
    cross_b = [(other, wa, group_b[i]) for i in range(nwb)]
    peer = cross_b[0]
    everyone = peers_a + peers_b + cross_b
    for p in everyone:
        pl.semaphore_signal(barrier, inc=1, device_id=p, device_id_type=MESH)
    sent = []

    def send(src, dst, ssem, rsem, device):
        copy = pltpu.make_async_remote_copy(
            src_ref=src, dst_ref=dst, send_sem=ssem, recv_sem=rsem,
            device_id=device, device_id_type=MESH,
        )
        copy.start()
        sent.append(copy)
        return copy

    def dot(a, b, dims=((1,), (0,))):
        return lax.dot_general(a, b, (dims, ((), ())), preferred_element_type=f32)

    def columns_of(owner):
        return pl.ds(pl.multiple_of(owner * gw, 128), gw)

    far_first = list(range(nb, 0, -1))
    for c in first:
        c.wait()
    x = xg[0]
    for i in far_first:
        psend[i - 1] = dot(x, w_in_ref[:, columns_of(group_b[i])]).astype(bf16)
    gp = dot(wg_ref[:, pl.ds(pl.multiple_of(wb * kd, 128), kd)], x, ((1,), (1,)))
    gsend[...] = jnp.zeros_like(gsend)
    gsend[:, 0:rows] = gp
    pl.semaphore_wait(barrier, len(everyone))
    copies_p, copies_g, copies_x = [None] * nb, [None] * nb, [None] * nb
    for i in far_first:
        at = i - 1
        copies_p[at] = send(psend.at[at], precv.at[at], p_ss.at[at], p_rs.at[at], peers_b[at])
    part = rows // nwa
    share = pl.ds(pl.multiple_of(wa * part, 16), part)
    for i in far_first:
        at = i - 1
        copies_g[at] = send(gsend, grecv.at[at], g_ss.at[at], g_rs.at[at], peers_b[at])
    for i in far_first:
        at = i - 1
        copies_x[at] = send(
            xg.at[0, share, :], xg.at[i, share, :], x_ss.at[at], x_rs.at[at], peers_b[at]
        )
    mine = pl.ds(pl.multiple_of(seq * half, 16), half)
    copies_d = []
    for j in range(1, nwa):
        copies_d.append(
            send(
                w_down_hbm.at[mine, quarter_of(group_a[j])], wd.at[j, mine, :],
                d_ss.at[j - 1], d_rs.at[j - 1], peers_a[j - 1],
            )
        )
    own = dot(x, w_in_ref[:, columns_of(wb)])

    def halves(a):
        top = a.astype(bf16)
        return top, (a - top.astype(f32)).astype(bf16)

    row_sq = lax.broadcasted_iota(jnp.int32, (gw, gw), 0)
    col_sq = lax.broadcasted_iota(jnp.int32, (gw, gw), 1)
    same = row_sq // 4 == col_sq // 4
    inner = lax.rem(row_sq, 4)
    blocks = wq_ref.shape[2]
    outer = lax.rem(lax.broadcasted_iota(jnp.int32, (4, gw), 1), 4) == lax.broadcasted_iota(
        jnp.int32, (4, gw), 0
    )
    block_at = lax.broadcasted_iota(jnp.int32, (blocks, gw), 0)
    block_of = lax.broadcasted_iota(jnp.int32, (blocks, gw), 1) // 4
    for c in small:
        c.wait()
    for n in range(nwb):
        spread = (block_at == group_b[n] * (gw // 4) + block_of).astype(bf16)
        for kind, ref in enumerate((wq_ref, wk_ref, wv_ref)):
            full = jnp.zeros((gw, gw), f32)
            for i in range(4):
                top, rest = halves(ref[i])
                wide = dot(top, spread) + dot(rest, spread)
                coef = jnp.sum(jnp.where(outer, wide, 0.0), axis=0, keepdims=True)
                full = jnp.where(inner == i, coef, full)
            wsq[kind * nwb + n], wlo[kind * nwb + n] = halves(jnp.where(same, full, 0.0))

    for i in range(1, nwb):
        copies_p[i - 1].wait_recv()
        own = own + precv[i - 1].astype(f32)
    mg[0] = own.astype(bf16)
    copies_m, copies_t = [None] * nb, [None] * nwb
    edge = slice(rl - 16, rl)
    for i in [0] + far_first:
        copies_t[i] = send(mg.at[0, edge, :], tail.at[i], t_ss.at[i], t_rs.at[i], cross_b[i])
    for i in far_first:
        at = i - 1
        copies_m[at] = send(mg.at[0], mg.at[i], m_ss.at[at], m_rs.at[at], peers_b[at])

    gates = gsend[:, 0:rows]
    for c in copies_g:
        c.wait_recv()
    sums = [gsend[:, 0:rows]] + [grecv[i][:, 0:rows] for i in range(nb)]
    while len(sums) > 1:
        sums = [sums[i] + sums[i + 1] for i in range(0, len(sums), 2)]
    gates = sums[0]
    heads = gates.shape[0] // 2
    row_id = lax.broadcasted_iota(jnp.int32, gates.shape, 0)
    ig = jnp.sum(jnp.where(row_id == wa, gates, 0.0), axis=0, keepdims=True) + ib_ref[wa]
    fg = jnp.sum(jnp.where(row_id == wa + heads, gates, 0.0), axis=0, keepdims=True) + fb_ref[wa]
    lf = jnp.minimum(fg, 0.0) - jnp.log1p(jnp.exp(-jnp.abs(fg)))
    length = len_ref[0, 0]
    last = seq == nseq - 1

    def block_gates(i_row, f_row, size, limit):
        t = lax.broadcasted_iota(jnp.int32, (size, size), 0)
        s = lax.broadcasted_iota(jnp.int32, (size, size), 1)
        valid = lax.broadcasted_iota(jnp.int32, (1, size), 1) < limit
        f_row = jnp.where(valid, f_row, 0.0)
        b_col = jnp.sum(jnp.where(s <= t, f_row, 0.0), axis=1, keepdims=True)
        b_row = jnp.sum(jnp.where(s == t, b_col, 0.0), axis=0, keepdims=True)
        total = jnp.sum(f_row, axis=1, keepdims=True)
        e_row = jnp.where(valid, total - b_row + i_row, NEG_FILL)
        causal = (s <= t) & (s < limit)
        logw = jnp.where(causal, b_col - b_row + i_row, NEG_FILL)
        return b_col, total, e_row, causal, logw

    def to_col(row):
        size = row.shape[1]
        t = lax.broadcasted_iota(jnp.int32, (size, size), 0)
        s = lax.broadcasted_iota(jnp.int32, (size, size), 1)
        return jnp.sum(jnp.where(s == t, row, 0.0), axis=1, keepdims=True)

    bl, totl, el, causl, logl = block_gates(ig[:, 0:rl], lf[:, 0:rl], rl, rl)
    bs, tots, es, causs, logs = block_gates(ig[:, rl:rows], lf[:, rl:rows], rs, length)
    esend[...] = jnp.broadcast_to(el, esend.shape)
    ce = send(esend, erecv, e_ss.at[0], e_rs.at[0], peer)
    pick_row = lax.broadcasted_iota(jnp.int32, (8, rows), 0)
    pick_at = lax.broadcasted_iota(jnp.int32, (8, rows), 1)
    slot_at = length - 3 + pick_row
    target = jnp.where(last, rl - 3 + pick_row, jnp.where(slot_at >= 0, rl + slot_at, -1))
    pick = (pick_at == target).astype(bf16)
    first_keep = jnp.where(seq > 0, 1.0, 0.0)
    scale = (gw * nwb) ** (-0.5)
    sl = jnp.zeros((rl, rl), f32)
    ss = jnp.zeros((rs, rs), f32)
    copies_k, copies_v, copies_xa, copies_f = [], [], [], []
    for n in range(nwb):
        if n:
            copies_m[n - 1].wait_recv()
        lanes = columns_of(group_b[n])
        m = mg[n]
        v = (dot(m, wsq[2 * nwb + n]) + dot(m, wlo[2 * nwb + n])).astype(bf16)
        vb[n, rl : rl + rows, :] = v
        copies_v.append(
            send(vb.at[n, rl : 2 * rl, :], vb.at[n, 0:rl, :], v_ss.at[n], v_rs.at[n], peer)
        )
        cc_ref[0, :, lanes] = dot(pick, m)[0:3].astype(bf16)
        wide = m.astype(f32)
        copies_t[n].wait_recv()
        ext[0:8, :] = tail[n].astype(f32)[8:16] * first_keep
        ext[8 : 8 + rl, :] = wide[0:rl]
        ext[8 + rl : 16 + rl, :] = jnp.zeros((8, gw), f32)
        ext[16 + rl : 16 + rows, :] = wide[rl:rows]
        taps = cw_ref[:, lanes]
        for base, start, size in ((5, 0, rl), (13 + rl, rl, rs)):
            conv = jnp.zeros((size, gw), f32)
            for j in range(4):
                conv = conv + taps[j : j + 1] * ext[base + j : base + j + size, :]
            act[n, start : start + size, :] = conv / (1.0 + jnp.exp(-conv))
        top, rest = halves(act[n])
        wk, wq = nwb + n, n
        k = (dot(top, wsq[wk]) + dot(rest, wsq[wk]) + dot(top, wlo[wk])).astype(bf16)
        kb[n, rl : rl + rows, :] = k
        copies_k.append(
            send(kb.at[n, rl : 2 * rl, :], kb.at[n, 0:rl, :], k_ss.at[n], k_rs.at[n], peer)
        )
        q = (dot(top, wsq[wq]) + dot(rest, wsq[wq]) + dot(top, wlo[wq])).astype(bf16)
        qs[n] = q
        sl = sl + dot(q[0:rl], k[0:rl], ((1,), (1,)))
        ss = ss + dot(q[rl:rows], k[rl:rows], ((1,), (1,)))
        if n == 0:
            for i in far_first[::-1]:
                copies_x[i - 1].wait_recv()
                src = xg.at[i, share, :]
                for j in range(na):
                    at = (i - 1) * na + j
                    copies_xa.append(send(src, src, xa_ss.at[at], xa_rs.at[at], peers_a[j]))
            for j in range(na):
                copies_d[j].wait_recv()
                src = wd.at[j + 1, mine, :]
                copies_f.append(send(src, src, f_ss.at[j], f_rs.at[j], peer))

    for c in late:
        c.wait()
    for c in copies_xa:
        c.wait_recv()
    inv = 1.0 / (gw * nwb)
    gain, skip = gain_ref[...], skip_ref[...]
    gate = jnp.zeros((rows, gw), f32)
    for i in range(nwb):
        gate = gate + dot(xg[i], w_og_ref[pl.ds(pl.multiple_of(group_b[i] * kd, 128), kd), :])
    gate = gate / (1.0 + jnp.exp(-gate))
    copies_o = []

    def gated(start, size, hidden, total, square_sum, keep):
        mean = total * inv
        norm = lax.rsqrt(square_sum * inv - mean * mean + EPSILON)
        normed = (hidden - mean) * norm * gain
        out = (normed + skip * act[0, start : start + size, :]) * gate[start : start + size]
        return (out if keep is None else out * keep).astype(bf16)

    def share_out(start, size):
        span = slice(start, start + size)
        row = len(copies_o)
        copies_o.append([])
        for j in range(1, nwa):
            at = row * na + j - 1
            copies_o[-1].append(
                send(ga.at[0, span, :], ga.at[j, span, :], o_ss.at[at], o_rs.at[at], peers_a[j - 1])
            )

    rmax_s = jnp.max(logs, axis=1, keepdims=True)
    mix_s = ss * scale * jnp.where(causs, jnp.exp(logs - rmax_s), 0.0)
    den_s = jnp.sum(mix_s, axis=1, keepdims=True)
    div_s = jnp.maximum(jnp.abs(den_s), jnp.exp(-rmax_s))
    mix_s = mix_s.astype(bf16)
    sum_s = jnp.zeros((rs, 1), f32)
    sq_s = jnp.zeros((rs, 1), f32)
    for n in range(nwb):
        hh = dot(mix_s, vb[n, 2 * rl : rl + rows, :]) / div_s
        if n == 0:
            own_s = hh
        sum_s += jnp.sum(hh, axis=1, keepdims=True)
        sq_s += jnp.sum(hh * hh, axis=1, keepdims=True)
    ok_s = (lax.broadcasted_iota(jnp.int32, (rs, 1), 0) < length).astype(f32)
    ga[0, rl:rows, :] = gated(rl, rs, own_s, sum_s, sq_s, ok_s)
    share_out(rl, rs)

    ce.wait_recv()
    ep = erecv[0:1, :]
    mp = jnp.max(ep, axis=1, keepdims=True)
    carry_m = jnp.where(seq > 0, mp, NEG_FILL)
    carry_log = bl + carry_m
    rmax_l = jnp.maximum(jnp.max(logl, axis=1, keepdims=True), carry_log)
    mix_l = sl * scale * jnp.where(causl, jnp.exp(logl - rmax_l), 0.0)
    for c in copies_k + copies_v:
        c.wait_recv()
    sp = jnp.zeros((rl, rl), f32)
    for n in range(nwb):
        sp = sp + dot(qs[n, 0:rl, :], kb[n, 0:rl, :], ((1,), (1,)))
    mix_p = sp * scale * jnp.exp(ep - mp) * jnp.exp(carry_log - rmax_l)
    den_l = jnp.sum(mix_l, axis=1, keepdims=True) + jnp.sum(mix_p, axis=1, keepdims=True)
    div_l = jnp.maximum(jnp.abs(den_l), jnp.exp(-rmax_l))
    mix = jnp.concatenate([mix_p, mix_l], axis=1).astype(bf16)
    sum_l = jnp.zeros((rl, 1), f32)
    sq_l = jnp.zeros((rl, 1), f32)
    for n in range(nwb):
        hl = dot(mix, vb[n, 0 : 2 * rl, :]) / div_l
        if n == 0:
            hs[...] = hl
        sum_l += jnp.sum(hl, axis=1, keepdims=True)
        sq_l += jnp.sum(hl * hl, axis=1, keepdims=True)
    step = rl // 2
    for start in (0, step):
        span = slice(start, start + step)
        ga[0, span, :] = gated(start, step, hs[span, :], sum_l[span], sq_l[span], None)
        share_out(start, step)

    ml = jnp.max(el, axis=1, keepdims=True)
    shifted = carry_m + totl
    joined = jnp.maximum(shifted, ml)
    ms = jnp.max(es, axis=1, keepdims=True)
    m_ref[...] = jnp.where(last, joined, ms)
    keep_p = jnp.where(last & (seq > 0), 1.0, 0.0)
    keep_l = jnp.where(last, 1.0, 0.0)
    wp = to_col(jnp.exp(ep - mp) * jnp.exp(shifted - joined)) * (keep_p * scale)
    wl = to_col(jnp.exp(el - joined)) * (keep_l * scale)
    ws = to_col(jnp.where(es > 0.5 * NEG_FILL, jnp.exp(es - ms), 0.0)) * ((1.0 - keep_l) * scale)
    weight = jnp.concatenate([wp, wl, ws], axis=0)
    vw = (vb[0].astype(f32) * weight).astype(bf16)
    for n in range(nwb):
        lanes = columns_of(group_b[n])
        keys = kb[n]
        c_ref[0, 0, :, lanes] = dot(vw, keys, ((0,), (0,)))
        n_ref[0, :, lanes] = jnp.sum(keys.astype(f32) * weight, axis=0, keepdims=True)

    for c in copies_f:
        c.wait_recv()
    ow = zrecv.shape[2]
    copies_z = []
    spans = [(rl, rs), (0, step), (step, step)]

    def piece_of(owner):
        return pl.ds(pl.multiple_of(owner * ow, 128), ow)

    for row, (start, size) in enumerate(spans):
        span = slice(start, start + size)
        y = dot(ga[0, span, :], wd[0])
        for j in range(1, nwa):
            copies_o[row][j - 1].wait_recv()
            y = y + dot(ga[j, span, :], wd[j])
        yacc[span, :] = y
        copies_z.append([])
        for i in range(1, nwb):
            at = row * nb + i - 1
            zsend[i - 1, span, :] = yacc[span, piece_of(group_b[i])].astype(bf16)
            copies_z[-1].append(
                send(
                    zsend.at[i - 1, span, :], zrecv.at[i - 1, span, :],
                    z_ss.at[at], z_rs.at[at], peers_b[i - 1],
                )
            )
    for row, (start, size) in enumerate(spans):
        span = slice(start, start + size)
        y = yacc[span, piece_of(wb)]
        for i in range(nb):
            copies_z[row][i].wait_recv()
            y = y + zrecv[i, span, :].astype(f32)
        if start == rl:
            sy_ref[0] = y.astype(bf16)
        else:
            ly_ref[span, :] = y.astype(bf16)
    for c in sent:
        c.wait_send()


def write_kernel(*refs):
    sources, targets, sem = refs[:6], refs[6:12], refs[12]
    copies = [
        pltpu.make_async_copy(src, dst, sem.at[i])
        for i, (src, dst) in enumerate(zip(sources, targets))
    ]
    for c in copies:
        c.start()
    for c in copies:
        c.wait()


def fused_body(
    long_x, short_x, short_len, w_in, w_outgate, w_gates, conv_weight, w_query, w_key, w_value,
    igate_bias, fgate_bias, norm_gain, skip_gain, w_down,
):
    nseq, nwa, nwb = (lax.axis_size(a) for a in ("seq", "wa", "wb"))
    f32, bf16 = jnp.float32, jnp.bfloat16
    rl, kd = long_x.shape
    rs = short_x.shape[1]
    rows = rl + rs
    gw = w_outgate.shape[1]
    hw = w_in.shape[1]
    ow = w_down.shape[1] // (nwa * nwb)
    turned = [w.transpose(1, 2, 0) for w in (w_query, w_key, w_value)]
    vm = pl.BlockSpec(memory_space=pltpu.VMEM)
    hbm = pl.BlockSpec(memory_space=pl.ANY)
    nb, na = nwb - 1, nwa - 1
    dma = pltpu.SemaphoreType.DMA
    shapes = (
        jax.ShapeDtypeStruct((rl, ow), bf16),
        jax.ShapeDtypeStruct((1, rs, ow), bf16),
        jax.ShapeDtypeStruct((1, 1, gw, hw), f32),
        jax.ShapeDtypeStruct((1, 1, hw), f32),
        jax.ShapeDtypeStruct((1, 1), f32),
        jax.ShapeDtypeStruct((1, 3, hw), bf16),
    )
    inputs = (
        short_len[:, None], igate_bias, fgate_bias, long_x, short_x[0], w_in, w_gates.T,
        conv_weight, *turned, norm_gain[None], skip_gain[None], w_outgate, w_down,
    )
    outs = pl.pallas_call(
        functools.partial(mega_kernel, nwa, nwb, nseq),
        out_shape=tuple(pltpu.VMEM(a.shape, a.dtype) for a in shapes),
        in_specs=[pl.BlockSpec(memory_space=pltpu.HBM)] * 15,
        out_specs=(vm,) * 6,
        scratch_shapes=[
            pltpu.VMEM((nwb, rows, kd), bf16),
            pltpu.VMEM((nb, rows, gw), bf16),
            pltpu.VMEM((nb, rows, gw), bf16),
            pltpu.VMEM((8, 256), f32),
            pltpu.VMEM((nb, 8, 256), f32),
            pltpu.VMEM((nwb, rows, gw), bf16),
            pltpu.VMEM((nwb, 16, gw), bf16),
            pltpu.VMEM((16 + rows, gw), f32),
            pltpu.VMEM((nwb, rows, gw), f32),
            pltpu.VMEM((nwb, rows, gw), bf16),
            pltpu.VMEM((nwb, rl + rows, gw), bf16),
            pltpu.VMEM((nwb, rl + rows, gw), bf16),
            pltpu.VMEM((8, rl), f32),
            pltpu.VMEM((8, rl), f32),
            pltpu.VMEM((rl, gw), f32),
            pltpu.VMEM((nwa, rows, gw), bf16),
            pltpu.VMEM((nwa, gw, nwb * ow), bf16),
            pltpu.VMEM((rows, nwb * ow), f32),
            pltpu.VMEM((nb, rows, ow), bf16),
            pltpu.VMEM((nb, rows, ow), bf16),
            pltpu.VMEM((3 * nwb, gw, gw), bf16),
            pltpu.VMEM((3 * nwb, gw, gw), bf16),
            pltpu.VMEM(w_in.shape, bf16),
            pltpu.VMEM(w_gates.shape[::-1], bf16),
            pltpu.VMEM(conv_weight.shape, f32),
            pltpu.VMEM(turned[0].shape, f32),
            pltpu.VMEM(turned[1].shape, f32),
            pltpu.VMEM(turned[2].shape, f32),
            pltpu.VMEM((1, gw), f32),
            pltpu.VMEM((1, gw), f32),
            pltpu.VMEM(w_outgate.shape, bf16),
            pltpu.SMEM((1, 1), jnp.int32),
            pltpu.SMEM(igate_bias.shape, f32),
            pltpu.SMEM(fgate_bias.shape, f32),
        ]
        + [dma((nb,))] * 8
        + [dma((nb * na,))] * 2
        + [dma((1,))] * 2
        + [dma((nwb,))] * 6
        + [dma((3 * na,))] * 2
        + [dma((3 * nb,))] * 2
        + [dma((na,))] * 4
        + [dma((15,))],
        compiler_params=pltpu.CompilerParams(
            collective_id=0, has_side_effects=True, vmem_limit_bytes=48 * 2**20
        ),
        name="mlstm_layer",
    )(*(a if a.size == 1 else pltpu.with_memory_space_constraint(a, pltpu.HBM) for a in inputs))
    return pl.pallas_call(
        write_kernel,
        out_shape=shapes,
        in_specs=[vm] * 6,
        out_specs=(pl.BlockSpec(memory_space=pltpu.HBM),) * 6,
        scratch_shapes=[dma((6,))],
        name="write_out",
    )(*(pltpu.with_memory_space_constraint(out, pltpu.VMEM) for out in outs))


def solution(mesh):
    in_specs = (
        P("seq", "wb"),
        P("seq", None, "wb"),
        P("seq"),
        P("wb", "wa"),
        P(None, ("wa", "wb")),
        P(),
        P(None, "wa"),
        P("wa", None, None),
        P("wa", None, None),
        P("wa", None, None),
        P(),
        P(),
        P(("wa", "wb")),
        P(("wa", "wb")),
        P(("wa", "wb"), None),
    )
    out_specs = (
        P("seq", ("wa", "wb")),
        P("seq", None, ("wa", "wb")),
        P("seq", "wa", "wb", None),
        P("seq", "wa", None),
        P("seq", "wa"),
        P("seq", None, "wa"),
    )
    even = all(mesh.shape[a] & (mesh.shape[a] - 1) == 0 for a in ("wa", "wb"))
    layer = fused_body if mesh.shape["seq"] == 2 and even else body
    return jax.shard_map(layer, mesh=mesh, in_specs=in_specs, out_specs=out_specs, check_vma=False)
```

```python
import functools

import jax
import jax.numpy as jnp
from jax import lax
from jax.experimental import pallas as pl
from jax.experimental.pallas import tpu as pltpu
from jax.sharding import PartitionSpec as P

MESH = pl.DeviceIdType.MESH
NEG_FILL = -1e30
EPSILON = 1e-05
exact_mode = lax.Precision.HIGHEST


def passed_along(array, axis, by):
    devices = lax.axis_size(axis)
    pairs = [(i, i + by) for i in range(devices) if 0 <= i + by < devices]
    return lax.ppermute(array, axis, pairs)


def entering(array, axis, combine, identity):
    devices, index = (lax.axis_size(axis), lax.axis_index(axis))
    everything = jax.tree.map(lambda part: lax.all_gather(part, axis), array)
    start = jax.tree.map(
        lambda part, zero: jnp.broadcast_to(jnp.asarray(zero, part.dtype), part.shape),
        array,
        identity,
    )

    def turn(k, before):
        reached = k < index
        new = combine(before, jax.tree.map(lambda part: part[k], everything))
        return jax.tree.map(lambda a, b: jnp.where(reached, a, b), new, before)

    return lax.fori_loop(0, devices, turn, start)


def block_diagonal(inputs, blocks):
    row_count = inputs.shape[0]
    grouped = inputs.reshape(row_count, blocks.shape[0], blocks.shape[1])
    combined = jnp.einsum("rni,nio->rno", grouped, blocks, precision=exact_mode)
    return combined.reshape(row_count, -1)


def causal_conv(mlstm_in, previous, conv_weight):
    extended = jnp.concatenate([previous.astype(jnp.float32), mlstm_in.astype(jnp.float32)], axis=0)
    row_count = mlstm_in.shape[0]
    running = jnp.zeros(mlstm_in.shape, jnp.float32)
    for offset in range(conv_weight.shape[0]):
        running = running + conv_weight[offset] * extended[offset : offset + row_count]
    return running


def running_sum(row):
    at = jnp.arange(row.shape[0])
    return jnp.sum(jnp.where(at[:, None] >= at[None, :], row[None, :], 0.0), axis=1)


def block_hidden(queries, key_rows, value_rows, in_gate, log_forget, is_valid, carried):
    scaling = key_rows.shape[1] ** (-0.5)
    row_count = queries.shape[0]
    forget_sum = running_sum(jnp.where(is_valid, log_forget, 0.0))
    positions = jnp.arange(row_count)
    causal = (positions[:, None] >= positions[None, :]) & is_valid[None, :]
    log_weight = jnp.where(
        causal, forget_sum[:, None] - forget_sum[None, :] + in_gate[None, :], NEG_FILL
    )
    row_max = jnp.max(log_weight, axis=1)
    if carried is not None:
        carry_log = forget_sum + carried[2]
        row_max = jnp.maximum(row_max, carry_log)
    weights = jnp.where(causal, jnp.exp(log_weight - row_max[:, None]), 0.0)
    scores = jnp.dot(queries, key_rows.T, preferred_element_type=jnp.float32) * scaling
    mixing = scores * weights
    denominator = jnp.sum(mixing, axis=1)
    numerator = jnp.dot(mixing.astype(jnp.bfloat16), value_rows, preferred_element_type=jnp.float32)
    if carried is not None:
        carry_weight = jnp.exp(carry_log - row_max)
        query_wide = queries.astype(jnp.float32)
        numerator = numerator + carry_weight[:, None] * jnp.dot(
            query_wide, carried[0].T, precision=exact_mode
        )
        denominator = denominator + carry_weight * jnp.dot(
            query_wide, carried[1], precision=exact_mode
        )
    return numerator / jnp.maximum(jnp.abs(denominator), jnp.exp(-row_max))[:, None]


def block_state(key_rows, value_rows, in_gate, log_forget, is_valid):
    scaling = key_rows.shape[1] ** (-0.5)
    forget_sum = running_sum(jnp.where(is_valid, log_forget, 0.0))
    forget_total = forget_sum[-1]
    end_log = jnp.where(is_valid, forget_total - forget_sum + in_gate, NEG_FILL)
    end_max = jnp.max(end_log)
    end_weight = jnp.where(is_valid, jnp.exp(end_log - end_max), 0.0)
    key_wide = key_rows.astype(jnp.float32) * scaling
    matrix_state = jnp.dot(
        (value_rows.astype(jnp.float32) * end_weight[:, None]).T, key_wide, precision=exact_mode
    )
    normalizer = jnp.dot(end_weight, key_wide, precision=exact_mode)
    return (matrix_state, normalizer, end_max, forget_total)


def merge_states(earlier, latter):
    state_a, normal_a, max_a, forget_a = earlier
    state_b, normal_b, max_b, forget_b = latter
    shifted = max_a + forget_b
    joined = jnp.maximum(shifted, max_b)
    weight_a = jnp.exp(shifted - joined)
    weight_b = jnp.exp(max_b - joined)
    return (
        weight_a * state_a + weight_b * state_b,
        weight_a * normal_a + weight_b * normal_b,
        joined,
        forget_a + forget_b,
    )


def edge_rows(rows, length, rim):
    select = (jnp.arange(rows.shape[0])[None, :] == length - rim + jnp.arange(rim)[:, None]).astype(
        jnp.float32
    )
    return jnp.dot(select, rows.astype(jnp.float32), precision=exact_mode).astype(jnp.bfloat16)


def body(
    long_x,
    short_x,
    short_len,
    w_in,
    w_outgate,
    w_gates,
    conv_weight,
    w_query,
    w_key,
    w_value,
    igate_bias,
    fgate_bias,
    norm_gain,
    skip_gain,
    w_down,
):
    long_rows = long_x.shape[0]
    slot_rows = short_x.shape[1]
    heads = igate_bias.shape[0]
    head_width = w_in.shape[1]
    value_width = w_outgate.shape[1]
    block_size = w_value.shape[1]
    rim = conv_weight.shape[0] - 1
    head_index = lax.axis_index("wa")
    column_index = lax.axis_index("wb")
    local_rows = jnp.concatenate([long_x, short_x[0]], axis=0)
    gathered = lax.all_gather(local_rows, "wb", axis=1, tiled=True)
    mlstm_full = jnp.dot(
        gathered, lax.all_gather(w_in, "wb", axis=0, tiled=True), preferred_element_type=jnp.float32
    )
    mlstm_in = mlstm_full.astype(jnp.bfloat16)
    gate_out = jnp.dot(gathered, w_outgate, preferred_element_type=jnp.float32)
    gate_pre = jnp.dot(gathered, w_gates, preferred_element_type=jnp.float32)
    pick = (jnp.arange(heads) == head_index).astype(jnp.float32)
    in_gate = jnp.sum(gate_pre[:, :heads] * pick, axis=1) + jnp.sum(igate_bias * pick)
    log_forget = jax.nn.log_sigmoid(
        jnp.sum(gate_pre[:, heads:] * pick, axis=1) + jnp.sum(fgate_bias * pick)
    )
    long_in = mlstm_in[:long_rows]
    slot_in = mlstm_in[long_rows:]
    previous = passed_along(long_in[long_rows - rim :], "seq", 1)
    long_conv = causal_conv(long_in, previous, conv_weight)
    slot_conv = causal_conv(slot_in, jnp.zeros((rim, head_width), jnp.bfloat16), conv_weight)
    activated = jax.nn.silu(jnp.concatenate([long_conv, slot_conv], axis=0))
    queries = block_diagonal(activated, w_query).astype(jnp.bfloat16)
    key_rows = block_diagonal(activated, w_key).astype(jnp.bfloat16)
    value_blocks = lax.dynamic_slice_in_dim(
        w_value, column_index * (value_width // block_size), value_width // block_size, 0
    )
    value_cols = lax.dynamic_slice_in_dim(mlstm_in, column_index * value_width, value_width, 1)
    value_rows = block_diagonal(value_cols.astype(jnp.float32), value_blocks).astype(jnp.bfloat16)
    long_valid = jnp.ones((long_rows,), bool)
    local_state = block_state(
        key_rows[:long_rows],
        value_rows[:long_rows],
        in_gate[:long_rows],
        log_forget[:long_rows],
        long_valid,
    )
    local_tuple = (
        local_state[0],
        local_state[1],
        jnp.reshape(local_state[2], (1,)),
        jnp.reshape(local_state[3], (1,)),
    )
    identity = (
        jnp.zeros_like(local_state[0]),
        jnp.zeros_like(local_state[1]),
        jnp.full((1,), NEG_FILL, jnp.float32),
        jnp.zeros((1,), jnp.float32),
    )
    prefix = entering(local_tuple, "seq", merge_states, identity)
    carried = (prefix[0], prefix[1], prefix[2][0])
    long_hidden = block_hidden(
        queries[:long_rows],
        key_rows[:long_rows],
        value_rows[:long_rows],
        in_gate[:long_rows],
        log_forget[:long_rows],
        long_valid,
        carried,
    )
    final = merge_states(prefix, local_tuple)
    slot_valid = jnp.arange(slot_rows) < short_len[0]
    slot_hidden = block_hidden(
        queries[long_rows:],
        key_rows[long_rows:],
        value_rows[long_rows:],
        in_gate[long_rows:],
        log_forget[long_rows:],
        slot_valid,
        None,
    )
    slot_state = block_state(
        key_rows[long_rows:],
        value_rows[long_rows:],
        in_gate[long_rows:],
        log_forget[long_rows:],
        slot_valid,
    )
    hidden = jnp.concatenate([long_hidden, slot_hidden], axis=0)
    sums = lax.psum((jnp.sum(hidden, axis=1), jnp.sum(hidden * hidden, axis=1)), "wb")
    mean = sums[0] / head_width
    square = sums[1] / head_width
    normed = (
        (hidden - mean[:, None]) * lax.rsqrt(square - mean * mean + EPSILON)[:, None] * norm_gain
    )
    act_cols = lax.dynamic_slice_in_dim(activated, column_index * value_width, value_width, 1)
    row_valid = jnp.concatenate([long_valid, slot_valid], axis=0).astype(jnp.float32)
    gated = ((normed + skip_gain * act_cols) * jax.nn.silu(gate_out) * row_valid[:, None]).astype(
        jnp.bfloat16
    )
    terms = jnp.dot(gated, w_down, preferred_element_type=jnp.float32)
    mixed = lax.psum_scatter(
        terms.astype(jnp.bfloat16), ("wa", "wb"), scatter_dimension=1, tiled=True
    )
    long_y = mixed[:long_rows]
    short_y = mixed[long_rows:][None]
    slot_edge = edge_rows(slot_in, short_len[0], rim)
    is_last = lax.axis_index("seq") == lax.axis_size("seq") - 1
    cache_c = jnp.where(is_last, final[0], slot_state[0])[None, None]
    cache_n = jnp.where(is_last, final[1], slot_state[1])[None, None]
    cache_m = jnp.reshape(jnp.where(is_last, final[2][0], slot_state[2]), (1, 1))
    cache_conv = jnp.where(is_last, long_in[long_rows - rim :], slot_edge)[None]
    return (long_y, short_y, cache_c, cache_n, cache_m, cache_conv)


def flipped(index, mask):
    out, bit = index, 1
    while bit <= mask:
        if mask & bit:
            out = out + bit - 2 * bit * lax.rem(lax.div(index, bit), 2)
        bit *= 2
    return out


def mega_kernel(
    nwa, nwb, nseq,
    len_hbm, ib_hbm, fb_hbm,
    lx_ref, sx_ref, w_in_hbm, wg_hbm, cw_hbm, wq_hbm, wk_hbm, wv_hbm, gain_hbm, skip_hbm, w_og_hbm, w_down_hbm,
    ly_ref, sy_ref, c_ref, n_ref, m_ref, cc_ref,
    xg, own_ref, psend, precv, gsend, grecv, mg, tail, ext, act, qs, kb, vb, esend, erecv, hs,
    ga, wd, yacc, zsend, zrecv, wsq, wlo,
    w_in_ref, wg_ref, cw_ref, wq_ref, wk_ref, wv_ref, gain_ref, skip_ref, w_og_ref,
    len_ref, ib_ref, fb_ref,
    p_ss, p_rs, g_ss, g_rs, m_ss, m_rs, x_ss, x_rs, xa_ss, xa_rs, e_ss, e_rs,
    t_ss, t_rs, k_ss, k_rs, v_ss, v_rs, o_ss, o_rs, z_ss, z_rs, d_ss, d_rs, f_ss, f_rs, w_sem,
):
    f32, bf16 = jnp.float32, jnp.bfloat16
    seq, wa, wb = lax.axis_index("seq"), lax.axis_index("wa"), lax.axis_index("wb")
    rl, rs = lx_ref.shape[0], sx_ref.shape[0]
    rows = rl + rs
    kd = lx_ref.shape[1]
    gw = mg.shape[2]
    na, nb = nwa - 1, nwb - 1
    other = lax.rem(seq + 1, nseq)
    loads = []

    def load(src, dst):
        copy = pltpu.make_async_copy(src, dst, w_sem.at[len(loads)])
        copy.start()
        loads.append(copy)
        return copy

    group_a = [flipped(wa, j) for j in range(nwa)]
    group_b = [flipped(wb, i) for i in range(nwb)]
    half = wd.shape[1] // 2
    quarter = wd.shape[2]

    def quarter_of(owner):
        return pl.ds(pl.multiple_of(owner * quarter, 128), quarter)

    first = [load(lx_ref, xg.at[0, 0:rl, :]), load(sx_ref, xg.at[0, rl:rows, :])]
    first += [load(wg_hbm, wg_ref), load(w_in_hbm, w_in_ref)]
    small = [(wq_hbm, wq_ref), (wk_hbm, wk_ref), (wv_hbm, wv_ref), (cw_hbm, cw_ref)]
    small += [(len_hbm, len_ref), (ib_hbm, ib_ref), (fb_hbm, fb_ref)]
    small = [load(src, dst) for src, dst in small]
    late = [load(src, dst) for src, dst in ((gain_hbm, gain_ref), (skip_hbm, skip_ref))]
    late += [load(w_og_hbm, w_og_ref), load(w_down_hbm.at[:, quarter_of(wa)], wd.at[0])]

    barrier = pltpu.get_barrier_semaphore()
    peers_a = [(seq, group_a[j], wb) for j in range(1, nwa)]
    peers_b = [(seq, wa, group_b[i]) for i in range(1, nwb)]
    cross_b = [(other, wa, group_b[i]) for i in range(nwb)]
    peer = cross_b[0]
    everyone = peers_a + peers_b + cross_b
    for p in everyone:
        pl.semaphore_signal(barrier, inc=1, device_id=p, device_id_type=MESH)
    sent = []

    def send(src, dst, ssem, rsem, device):
        copy = pltpu.make_async_remote_copy(
            src_ref=src, dst_ref=dst, send_sem=ssem, recv_sem=rsem,
            device_id=device, device_id_type=MESH,
        )
        copy.start()
        sent.append(copy)
        return copy

    def edge_copy(i):
        return pltpu.make_async_remote_copy(
            src_ref=mg.at[0, rl - 16 : rl, :], dst_ref=tail.at[i], send_sem=t_ss.at[i],
            recv_sem=t_rs.at[i], device_id=cross_b[i], device_id_type=MESH,
        )

    def dot(a, b, dims=((1,), (0,))):
        return lax.dot_general(a, b, (dims, ((), ())), preferred_element_type=f32)

    def columns_of(owner):
        return pl.ds(pl.multiple_of(owner * gw, 128), gw)

    far_first = list(range(nb, 0, -1))

    @pl.when(seq == 0)
    def _():
        tail[...] = jnp.zeros_like(tail)

    for c in first:
        c.wait()
    x = xg[0]
    for i in far_first:
        psend[i - 1] = dot(x, w_in_ref[:, columns_of(group_b[i])]).astype(bf16)
    gp = dot(wg_ref[:, pl.ds(pl.multiple_of(wb * kd, 128), kd)], x, ((1,), (1,)))
    row_id = lax.broadcasted_iota(jnp.int32, gp.shape, 0)
    gsend[...] = jnp.zeros_like(gsend)
    for at, head in ((0, wa), (2, wa + gp.shape[0] // 2)):
        row = jnp.sum(jnp.where(row_id == head, gp, 0.0), axis=0, keepdims=True)
        gsend[at : at + 1, 0:rl] = row[:, 0:rl]
        gsend[at + 1 : at + 2, 0:rs] = row[:, rl:rows]
    pl.semaphore_wait(barrier, len(everyone))
    copies_p, copies_g, copies_x = [], [None] * nb, [None] * nb
    part = rows // nwa
    share = pl.ds(pl.multiple_of(wa * part, 16), part)
    cuts = [(0, rl), (rl, rows)]

    def send_x():
        for i in (2, 1):
            at = i - 1
            copies_x[at] = send(
                xg.at[0, share, :], xg.at[i, share, :], x_ss.at[at], x_rs.at[at], peers_b[at]
            )

    for c, (start, end) in enumerate(cuts):
        if c == 1:
            send_x()
        copies_p.append([None] * nb)
        for i in far_first:
            at, span = i - 1, slice(start, end)
            copies_p[c][at] = send(
                psend.at[at, span, :], precv.at[at, span, :],
                p_ss.at[c * nb + at], p_rs.at[c * nb + at], peers_b[at],
            )
        if c == 0:
            for i in far_first:
                at = i - 1
                copies_g[at] = send(gsend, grecv.at[at], g_ss.at[at], g_rs.at[at], peers_b[at])
    if 1 >= len(cuts):
        send_x()
    mine = pl.ds(pl.multiple_of(seq * half, 16), half)
    copies_d = []
    for j in range(1, nwa):
        copies_d.append(
            send(
                w_down_hbm.at[mine, quarter_of(group_a[j])], wd.at[j, mine, :],
                d_ss.at[j - 1], d_rs.at[j - 1], peers_a[j - 1],
            )
        )
    own_ref[...] = dot(x, w_in_ref[:, columns_of(wb)])

    def halves(a):
        top = a.astype(bf16)
        return top, (a - top.astype(f32)).astype(bf16)

    row_sq = lax.broadcasted_iota(jnp.int32, (gw, gw), 0)
    col_sq = lax.broadcasted_iota(jnp.int32, (gw, gw), 1)
    same = row_sq // 4 == col_sq // 4
    inner = lax.rem(row_sq, 4)
    blocks = wq_ref.shape[2]
    outer = lax.rem(lax.broadcasted_iota(jnp.int32, (4, gw), 1), 4) == lax.broadcasted_iota(
        jnp.int32, (4, gw), 0
    )
    block_at = lax.broadcasted_iota(jnp.int32, (blocks, gw), 0)
    block_of = lax.broadcasted_iota(jnp.int32, (blocks, gw), 1) // 4
    for c in small:
        c.wait()
    for n in range(nwb):
        spread = (block_at == group_b[n] * (gw // 4) + block_of).astype(bf16)
        for kind, ref in enumerate((wq_ref, wk_ref, wv_ref)):
            full = jnp.zeros((gw, gw), f32)
            for i in range(4):
                top, rest = halves(ref[i])
                wide = dot(top, spread) + dot(rest, spread)
                coef = jnp.sum(jnp.where(outer, wide, 0.0), axis=0, keepdims=True)
                full = jnp.where(inner == i, coef, full)
            wsq[kind * nwb + n], wlo[kind * nwb + n] = halves(jnp.where(same, full, 0.0))

    copies_m = []
    copies_xa = []

    def relay_x():
        copies_x[1].wait_recv()
        copies_x[2] = send(
            xg.at[2, share, :], xg.at[3, share, :], x_ss.at[2], x_rs.at[2], peers_b[0]
        )

    def spread_x(i):
        if i != 2:
            copies_x[i - 1].wait_recv()
        src = xg.at[i, share, :]
        for j in range(na):
            at = (i - 1) * na + j
            copies_xa.append(send(src, src, xa_ss.at[at], xa_rs.at[at], peers_a[j]))

    for c, (start, end) in enumerate(cuts):
        if c == 1:
            relay_x()
        span = slice(start, end)
        total = own_ref[span, :]
        for i in far_first:
            copies_p[c][i - 1].wait_recv()
            total = total + precv[i - 1, span, :].astype(f32)
        mg[0, span, :] = total.astype(bf16)
        if start < rl <= end:

            @pl.when(seq == 0)
            def _():
                for i in [0] + far_first:
                    edge_copy(i).start()

        copies_m.append([None] * nb)
        for i in far_first:
            at = i - 1
            copies_m[c][at] = send(
                mg.at[0, span, :], mg.at[i, span, :],
                m_ss.at[c * nb + at], m_rs.at[c * nb + at], peers_b[at],
            )

    for c in copies_g:
        c.wait_recv()
    sums = [gsend[...]] + [grecv[i] for i in range(nb)]
    while len(sums) > 1:
        sums = [sums[i] + sums[i + 1] for i in range(0, len(sums), 2)]
    gates = sums[0]
    ig = gates[0:2] + ib_ref[wa]
    fg = gates[2:4] + fb_ref[wa]
    lf = jnp.minimum(fg, 0.0) - jnp.log1p(jnp.exp(-jnp.abs(fg)))
    length = len_ref[0, 0]
    last = seq == nseq - 1

    def block_gates(i_row, f_row, size, limit):
        t = lax.broadcasted_iota(jnp.int32, (size, size), 0)
        s = lax.broadcasted_iota(jnp.int32, (size, size), 1)
        valid = lax.broadcasted_iota(jnp.int32, (1, size), 1) < limit
        f_row = jnp.where(valid, f_row, 0.0)
        b_col = jnp.sum(jnp.where(s <= t, f_row, 0.0), axis=1, keepdims=True)
        b_row = jnp.sum(jnp.where(s == t, b_col, 0.0), axis=0, keepdims=True)
        total = jnp.sum(f_row, axis=1, keepdims=True)
        e_row = jnp.where(valid, total - b_row + i_row, NEG_FILL)
        causal = (s <= t) & (s < limit)
        logw = jnp.where(causal, b_col - b_row + i_row, NEG_FILL)
        return b_col, total, e_row, causal, logw

    def to_col(row):
        size = row.shape[1]
        t = lax.broadcasted_iota(jnp.int32, (size, size), 0)
        s = lax.broadcasted_iota(jnp.int32, (size, size), 1)
        return jnp.sum(jnp.where(s == t, row, 0.0), axis=1, keepdims=True)

    bl, totl, el, causl, logl = block_gates(ig[0:1, 0:rl], lf[0:1, 0:rl], rl, rl)
    bs, tots, es, causs, logs = block_gates(ig[1:2, 0:rs], lf[1:2, 0:rs], rs, length)
    esend[...] = jnp.broadcast_to(el, esend.shape)
    ce = send(esend, erecv, e_ss.at[0], e_rs.at[0], peer)
    pick_row = lax.broadcasted_iota(jnp.int32, (8, rows), 0)
    pick_at = lax.broadcasted_iota(jnp.int32, (8, rows), 1)
    slot_at = length - 3 + pick_row
    target = jnp.where(last, rl - 3 + pick_row, jnp.where(slot_at >= 0, rl + slot_at, -1))
    pick = (pick_at == target).astype(bf16)
    first_keep = jnp.where(seq > 0, 1.0, 0.0)
    scale = (gw * nwb) ** (-0.5)
    sl = jnp.zeros((rl, rl), f32)
    ss = jnp.zeros((rs, rs), f32)
    copies_k, copies_v, copies_f = [], [], []
    for n in range(nwb):
        if n:
            for row in copies_m:
                row[n - 1].wait_recv()
        lanes = columns_of(group_b[n])
        m = mg[n]
        v = (dot(m, wsq[2 * nwb + n]) + dot(m, wlo[2 * nwb + n])).astype(bf16)
        vb[n, rl : rl + rows, :] = v
        copies_v.append(
            send(vb.at[n, rl : 2 * rl, :], vb.at[n, 0:rl, :], v_ss.at[n], v_rs.at[n], peer)
        )
        cc_ref[0, :, lanes] = dot(pick, m)[0:3].astype(bf16)
        wide = m.astype(f32)

        @pl.when(seq > 0)
        def _():
            edge_copy(n).wait_recv()

        ext[0:8, :] = tail[n].astype(f32)[8:16] * first_keep
        ext[8 : 8 + rl, :] = wide[0:rl]
        ext[8 + rl : 16 + rl, :] = jnp.zeros((8, gw), f32)
        ext[16 + rl : 16 + rows, :] = wide[rl:rows]
        taps = cw_ref[:, lanes]
        for base, start, size in ((5, 0, rl), (13 + rl, rl, rs)):
            conv = jnp.zeros((size, gw), f32)
            for j in range(4):
                conv = conv + taps[j : j + 1] * ext[base + j : base + j + size, :]
            act[n, start : start + size, :] = conv / (1.0 + jnp.exp(-conv))
        top, rest = halves(act[n])
        wk, wq = nwb + n, n
        k = (dot(top, wsq[wk]) + dot(rest, wsq[wk]) + dot(top, wlo[wk])).astype(bf16)
        kb[n, rl : rl + rows, :] = k
        copies_k.append(
            send(kb.at[n, rl : 2 * rl, :], kb.at[n, 0:rl, :], k_ss.at[n], k_rs.at[n], peer)
        )
        q = (dot(top, wsq[wq]) + dot(rest, wsq[wq]) + dot(top, wlo[wq])).astype(bf16)
        qs[n] = q
        sl = sl + dot(q[0:rl], k[0:rl], ((1,), (1,)))
        ss = ss + dot(q[rl:rows], k[rl:rows], ((1,), (1,)))
        if n == 0:
            if len(cuts) <= 1:
                relay_x()
            for i in (2, 1, 3):
                spread_x(i)
            for j in range(na):
                copies_d[j].wait_recv()
                src = wd.at[j + 1, mine, :]
                copies_f.append(send(src, src, f_ss.at[j], f_rs.at[j], peer))

    for c in late:
        c.wait()
    for c in copies_xa:
        c.wait_recv()
    inv = 1.0 / (gw * nwb)
    gain, skip = gain_ref[...], skip_ref[...]
    gate = jnp.zeros((rows, gw), f32)
    for i in range(nwb):
        gate = gate + dot(xg[i], w_og_ref[pl.ds(pl.multiple_of(group_b[i] * kd, 128), kd), :])
    gate = gate / (1.0 + jnp.exp(-gate))
    copies_o = []

    def gated(start, size, hidden, total, square_sum, keep):
        mean = total * inv
        norm = lax.rsqrt(square_sum * inv - mean * mean + EPSILON)
        normed = (hidden - mean) * norm * gain
        out = (normed + skip * act[0, start : start + size, :]) * gate[start : start + size]
        return (out if keep is None else out * keep).astype(bf16)

    def share_out(start, size):
        span = slice(start, start + size)
        row = len(copies_o)
        copies_o.append([])
        for j in range(1, nwa):
            at = row * na + j - 1
            copies_o[-1].append(
                send(ga.at[0, span, :], ga.at[j, span, :], o_ss.at[at], o_rs.at[at], peers_a[j - 1])
            )

    rmax_s = jnp.max(logs, axis=1, keepdims=True)
    mix_s = ss * scale * jnp.where(causs, jnp.exp(logs - rmax_s), 0.0)
    den_s = jnp.sum(mix_s, axis=1, keepdims=True)
    div_s = jnp.maximum(jnp.abs(den_s), jnp.exp(-rmax_s))
    mix_s = mix_s.astype(bf16)
    sum_s = jnp.zeros((rs, 1), f32)
    sq_s = jnp.zeros((rs, 1), f32)
    for n in range(nwb):
        hh = dot(mix_s, vb[n, 2 * rl : rl + rows, :]) / div_s
        if n == 0:
            own_s = hh
        sum_s += jnp.sum(hh, axis=1, keepdims=True)
        sq_s += jnp.sum(hh * hh, axis=1, keepdims=True)
    ok_s = (lax.broadcasted_iota(jnp.int32, (rs, 1), 0) < length).astype(f32)
    ga[0, rl:rows, :] = gated(rl, rs, own_s, sum_s, sq_s, ok_s)
    share_out(rl, rs)

    ce.wait_recv()
    ep = erecv[0:1, :]
    mp = jnp.max(ep, axis=1, keepdims=True)
    carry_m = jnp.where(seq > 0, mp, NEG_FILL)
    carry_log = bl + carry_m
    rmax_l = jnp.maximum(jnp.max(logl, axis=1, keepdims=True), carry_log)
    mix_l = sl * scale * jnp.where(causl, jnp.exp(logl - rmax_l), 0.0)
    for c in copies_k + copies_v:
        c.wait_recv()
    sp = jnp.zeros((rl, rl), f32)
    for n in range(nwb):
        sp = sp + dot(qs[n, 0:rl, :], kb[n, 0:rl, :], ((1,), (1,)))
    mix_p = sp * scale * jnp.exp(ep - mp) * jnp.exp(carry_log - rmax_l)
    den_l = jnp.sum(mix_l, axis=1, keepdims=True) + jnp.sum(mix_p, axis=1, keepdims=True)
    div_l = jnp.maximum(jnp.abs(den_l), jnp.exp(-rmax_l))
    mix = jnp.concatenate([mix_p, mix_l], axis=1).astype(bf16)
    sum_l = jnp.zeros((rl, 1), f32)
    sq_l = jnp.zeros((rl, 1), f32)
    for n in range(nwb):
        hl = dot(mix, vb[n, 0 : 2 * rl, :]) / div_l
        if n == 0:
            hs[...] = hl
        sum_l += jnp.sum(hl, axis=1, keepdims=True)
        sq_l += jnp.sum(hl * hl, axis=1, keepdims=True)
    step = rl // 2
    for start in (0, step):
        span = slice(start, start + step)
        ga[0, span, :] = gated(start, step, hs[span, :], sum_l[span], sq_l[span], None)
        share_out(start, step)

    ml = jnp.max(el, axis=1, keepdims=True)
    shifted = carry_m + totl
    joined = jnp.maximum(shifted, ml)
    ms = jnp.max(es, axis=1, keepdims=True)
    m_ref[...] = jnp.where(last, joined, ms)
    keep_p = jnp.where(last & (seq > 0), 1.0, 0.0)
    keep_l = jnp.where(last, 1.0, 0.0)
    wp = to_col(jnp.exp(ep - mp) * jnp.exp(shifted - joined)) * (keep_p * scale)
    wl = to_col(jnp.exp(el - joined)) * (keep_l * scale)
    ws = to_col(jnp.where(es > 0.5 * NEG_FILL, jnp.exp(es - ms), 0.0)) * ((1.0 - keep_l) * scale)
    weight = jnp.concatenate([wp, wl, ws], axis=0)
    vw = (vb[0].astype(f32) * weight).astype(bf16)
    for n in range(nwb):
        lanes = columns_of(group_b[n])
        keys = kb[n]
        c_ref[0, 0, :, lanes] = dot(vw, keys, ((0,), (0,)))
        n_ref[0, :, lanes] = jnp.sum(keys.astype(f32) * weight, axis=0, keepdims=True)

    for c in copies_f:
        c.wait_recv()
    ow = zrecv.shape[2]
    copies_z = []
    spans = [(rl, rs), (0, step), (step, step)]

    def piece_of(owner):
        return pl.ds(pl.multiple_of(owner * ow, 128), ow)

    for row, (start, size) in enumerate(spans):
        span = slice(start, start + size)
        y = dot(ga[0, span, :], wd[0])
        for j in range(1, nwa):
            copies_o[row][j - 1].wait_recv()
            y = y + dot(ga[j, span, :], wd[j])
        yacc[span, :] = y
        copies_z.append([])
        for i in range(1, nwb):
            at = row * nb + i - 1
            zsend[i - 1, span, :] = yacc[span, piece_of(group_b[i])].astype(bf16)
            copies_z[-1].append(
                send(
                    zsend.at[i - 1, span, :], zrecv.at[i - 1, span, :],
                    z_ss.at[at], z_rs.at[at], peers_b[i - 1],
                )
            )
    for row, (start, size) in enumerate(spans):
        span = slice(start, start + size)
        y = yacc[span, piece_of(wb)]
        for i in range(nb):
            copies_z[row][i].wait_recv()
            y = y + zrecv[i, span, :].astype(f32)
        if start == rl:
            sy_ref[0] = y.astype(bf16)
        else:
            ly_ref[span, :] = y.astype(bf16)
    for c in sent:
        c.wait_send()

    @pl.when(seq == 0)
    def _():
        for i in range(nwb):
            edge_copy(i).wait_send()


def write_kernel(*refs):
    sources, targets, sem = refs[:6], refs[6:12], refs[12]
    copies = [
        pltpu.make_async_copy(src, dst, sem.at[i])
        for i, (src, dst) in enumerate(zip(sources, targets))
    ]
    for c in copies:
        c.start()
    for c in copies:
        c.wait()


def fused_body(
    long_x, short_x, short_len, w_in, w_outgate, w_gates, conv_weight, w_query, w_key, w_value,
    igate_bias, fgate_bias, norm_gain, skip_gain, w_down,
):
    nseq, nwa, nwb = (lax.axis_size(a) for a in ("seq", "wa", "wb"))
    f32, bf16 = jnp.float32, jnp.bfloat16
    rl, kd = long_x.shape
    rs = short_x.shape[1]
    rows = rl + rs
    gw = w_outgate.shape[1]
    hw = w_in.shape[1]
    ow = w_down.shape[1] // (nwa * nwb)
    turned = [w.transpose(1, 2, 0) for w in (w_query, w_key, w_value)]
    vm = pl.BlockSpec(memory_space=pltpu.VMEM)
    hbm = pl.BlockSpec(memory_space=pl.ANY)
    nb, na = nwb - 1, nwa - 1
    dma = pltpu.SemaphoreType.DMA
    shapes = (
        jax.ShapeDtypeStruct((rl, ow), bf16),
        jax.ShapeDtypeStruct((1, rs, ow), bf16),
        jax.ShapeDtypeStruct((1, 1, gw, hw), f32),
        jax.ShapeDtypeStruct((1, 1, hw), f32),
        jax.ShapeDtypeStruct((1, 1), f32),
        jax.ShapeDtypeStruct((1, 3, hw), bf16),
    )
    inputs = (
        short_len[:, None], igate_bias, fgate_bias, long_x, short_x[0], w_in, w_gates.T,
        conv_weight, *turned, norm_gain[None], skip_gain[None], w_outgate, w_down,
    )
    outs = pl.pallas_call(
        functools.partial(mega_kernel, nwa, nwb, nseq),
        out_shape=tuple(pltpu.VMEM(a.shape, a.dtype) for a in shapes),
        in_specs=[pl.BlockSpec(memory_space=pltpu.HBM)] * 15,
        out_specs=(vm,) * 6,
        scratch_shapes=[
            pltpu.VMEM((nwb, rows, kd), bf16),
            pltpu.VMEM((rows, gw), f32),
            pltpu.VMEM((nb, rows, gw), bf16),
            pltpu.VMEM((nb, rows, gw), bf16),
            pltpu.VMEM((8, max(rl, rs)), f32),
            pltpu.VMEM((nb, 8, max(rl, rs)), f32),
            pltpu.VMEM((nwb, rows, gw), bf16),
            pltpu.VMEM((nwb, 16, gw), bf16),
            pltpu.VMEM((16 + rows, gw), f32),
            pltpu.VMEM((nwb, rows, gw), f32),
            pltpu.VMEM((nwb, rows, gw), bf16),
            pltpu.VMEM((nwb, rl + rows, gw), bf16),
            pltpu.VMEM((nwb, rl + rows, gw), bf16),
            pltpu.VMEM((8, rl), f32),
            pltpu.VMEM((8, rl), f32),
            pltpu.VMEM((rl, gw), f32),
            pltpu.VMEM((nwa, rows, gw), bf16),
            pltpu.VMEM((nwa, gw, nwb * ow), bf16),
            pltpu.VMEM((rows, nwb * ow), f32),
            pltpu.VMEM((nb, rows, ow), bf16),
            pltpu.VMEM((nb, rows, ow), bf16),
            pltpu.VMEM((3 * nwb, gw, gw), bf16),
            pltpu.VMEM((3 * nwb, gw, gw), bf16),
            pltpu.VMEM(w_in.shape, bf16),
            pltpu.VMEM(w_gates.shape[::-1], bf16),
            pltpu.VMEM(conv_weight.shape, f32),
            pltpu.VMEM(turned[0].shape, f32),
            pltpu.VMEM(turned[1].shape, f32),
            pltpu.VMEM(turned[2].shape, f32),
            pltpu.VMEM((1, gw), f32),
            pltpu.VMEM((1, gw), f32),
            pltpu.VMEM(w_outgate.shape, bf16),
            pltpu.SMEM((1, 1), jnp.int32),
            pltpu.SMEM(igate_bias.shape, f32),
            pltpu.SMEM(fgate_bias.shape, f32),
        ]
        + [dma((3 * nb,))] * 2
        + [dma((nb,))] * 2
        + [dma((3 * nb,))] * 2
        + [dma((nb,))] * 2
        + [dma((nb * na,))] * 2
        + [dma((1,))] * 2
        + [dma((nwb,))] * 6
        + [dma((3 * na,))] * 2
        + [dma((3 * nb,))] * 2
        + [dma((na,))] * 4
        + [dma((15,))],
        compiler_params=pltpu.CompilerParams(
            collective_id=0, has_side_effects=True, vmem_limit_bytes=48 * 2**20
        ),
        name="mlstm_layer",
    )(*(a if a.size == 1 else pltpu.with_memory_space_constraint(a, pltpu.HBM) for a in inputs))
    return pl.pallas_call(
        write_kernel,
        out_shape=shapes,
        in_specs=[vm] * 6,
        out_specs=(pl.BlockSpec(memory_space=pltpu.HBM),) * 6,
        scratch_shapes=[dma((6,))],
        name="write_out",
    )(*(pltpu.with_memory_space_constraint(out, pltpu.VMEM) for out in outs))


def solution(mesh):
    in_specs = (
        P("seq", "wb"),
        P("seq", None, "wb"),
        P("seq"),
        P("wb", "wa"),
        P(None, ("wa", "wb")),
        P(),
        P(None, "wa"),
        P("wa", None, None),
        P("wa", None, None),
        P("wa", None, None),
        P(),
        P(),
        P(("wa", "wb")),
        P(("wa", "wb")),
        P(("wa", "wb"), None),
    )
    out_specs = (
        P("seq", ("wa", "wb")),
        P("seq", None, ("wa", "wb")),
        P("seq", "wa", "wb", None),
        P("seq", "wa", None),
        P("seq", "wa"),
        P("seq", None, "wa"),
    )
    fused = mesh.shape["seq"] == 2 and mesh.shape["wa"] == 4 and mesh.shape["wb"] == 4
    layer = fused_body if fused else body
    return jax.shard_map(layer, mesh=mesh, in_specs=in_specs, out_specs=out_specs, check_vma=False)
```

```python
import functools

import jax
import jax.numpy as jnp
from jax import lax
from jax.experimental import pallas as pl
from jax.experimental.pallas import tpu as pltpu
from jax.sharding import PartitionSpec as P

MESH = pl.DeviceIdType.MESH
NEG_FILL = -1e30
EPSILON = 1e-05
exact_mode = lax.Precision.HIGHEST


def passed_along(array, axis, by):
    devices = lax.axis_size(axis)
    pairs = [(i, i + by) for i in range(devices) if 0 <= i + by < devices]
    return lax.ppermute(array, axis, pairs)


def entering(array, axis, combine, identity):
    devices, index = (lax.axis_size(axis), lax.axis_index(axis))
    everything = jax.tree.map(lambda part: lax.all_gather(part, axis), array)
    start = jax.tree.map(
        lambda part, zero: jnp.broadcast_to(jnp.asarray(zero, part.dtype), part.shape),
        array,
        identity,
    )

    def turn(k, before):
        reached = k < index
        new = combine(before, jax.tree.map(lambda part: part[k], everything))
        return jax.tree.map(lambda a, b: jnp.where(reached, a, b), new, before)

    return lax.fori_loop(0, devices, turn, start)


def block_diagonal(inputs, blocks):
    row_count = inputs.shape[0]
    grouped = inputs.reshape(row_count, blocks.shape[0], blocks.shape[1])
    combined = jnp.einsum("rni,nio->rno", grouped, blocks, precision=exact_mode)
    return combined.reshape(row_count, -1)


def causal_conv(mlstm_in, previous, conv_weight):
    extended = jnp.concatenate([previous.astype(jnp.float32), mlstm_in.astype(jnp.float32)], axis=0)
    row_count = mlstm_in.shape[0]
    running = jnp.zeros(mlstm_in.shape, jnp.float32)
    for offset in range(conv_weight.shape[0]):
        running = running + conv_weight[offset] * extended[offset : offset + row_count]
    return running


def running_sum(row):
    at = jnp.arange(row.shape[0])
    return jnp.sum(jnp.where(at[:, None] >= at[None, :], row[None, :], 0.0), axis=1)


def block_hidden(queries, key_rows, value_rows, in_gate, log_forget, is_valid, carried):
    scaling = key_rows.shape[1] ** (-0.5)
    row_count = queries.shape[0]
    forget_sum = running_sum(jnp.where(is_valid, log_forget, 0.0))
    positions = jnp.arange(row_count)
    causal = (positions[:, None] >= positions[None, :]) & is_valid[None, :]
    log_weight = jnp.where(
        causal, forget_sum[:, None] - forget_sum[None, :] + in_gate[None, :], NEG_FILL
    )
    row_max = jnp.max(log_weight, axis=1)
    if carried is not None:
        carry_log = forget_sum + carried[2]
        row_max = jnp.maximum(row_max, carry_log)
    weights = jnp.where(causal, jnp.exp(log_weight - row_max[:, None]), 0.0)
    scores = jnp.dot(queries, key_rows.T, preferred_element_type=jnp.float32) * scaling
    mixing = scores * weights
    denominator = jnp.sum(mixing, axis=1)
    numerator = jnp.dot(mixing.astype(jnp.bfloat16), value_rows, preferred_element_type=jnp.float32)
    if carried is not None:
        carry_weight = jnp.exp(carry_log - row_max)
        query_wide = queries.astype(jnp.float32)
        numerator = numerator + carry_weight[:, None] * jnp.dot(
            query_wide, carried[0].T, precision=exact_mode
        )
        denominator = denominator + carry_weight * jnp.dot(
            query_wide, carried[1], precision=exact_mode
        )
    return numerator / jnp.maximum(jnp.abs(denominator), jnp.exp(-row_max))[:, None]


def block_state(key_rows, value_rows, in_gate, log_forget, is_valid):
    scaling = key_rows.shape[1] ** (-0.5)
    forget_sum = running_sum(jnp.where(is_valid, log_forget, 0.0))
    forget_total = forget_sum[-1]
    end_log = jnp.where(is_valid, forget_total - forget_sum + in_gate, NEG_FILL)
    end_max = jnp.max(end_log)
    end_weight = jnp.where(is_valid, jnp.exp(end_log - end_max), 0.0)
    key_wide = key_rows.astype(jnp.float32) * scaling
    matrix_state = jnp.dot(
        (value_rows.astype(jnp.float32) * end_weight[:, None]).T, key_wide, precision=exact_mode
    )
    normalizer = jnp.dot(end_weight, key_wide, precision=exact_mode)
    return (matrix_state, normalizer, end_max, forget_total)


def merge_states(earlier, latter):
    state_a, normal_a, max_a, forget_a = earlier
    state_b, normal_b, max_b, forget_b = latter
    shifted = max_a + forget_b
    joined = jnp.maximum(shifted, max_b)
    weight_a = jnp.exp(shifted - joined)
    weight_b = jnp.exp(max_b - joined)
    return (
        weight_a * state_a + weight_b * state_b,
        weight_a * normal_a + weight_b * normal_b,
        joined,
        forget_a + forget_b,
    )


def edge_rows(rows, length, rim):
    select = (jnp.arange(rows.shape[0])[None, :] == length - rim + jnp.arange(rim)[:, None]).astype(
        jnp.float32
    )
    return jnp.dot(select, rows.astype(jnp.float32), precision=exact_mode).astype(jnp.bfloat16)


def body(
    long_x,
    short_x,
    short_len,
    w_in,
    w_outgate,
    w_gates,
    conv_weight,
    w_query,
    w_key,
    w_value,
    igate_bias,
    fgate_bias,
    norm_gain,
    skip_gain,
    w_down,
):
    long_rows = long_x.shape[0]
    slot_rows = short_x.shape[1]
    heads = igate_bias.shape[0]
    head_width = w_in.shape[1]
    value_width = w_outgate.shape[1]
    block_size = w_value.shape[1]
    rim = conv_weight.shape[0] - 1
    head_index = lax.axis_index("wa")
    column_index = lax.axis_index("wb")
    local_rows = jnp.concatenate([long_x, short_x[0]], axis=0)
    gathered = lax.all_gather(local_rows, "wb", axis=1, tiled=True)
    mlstm_full = jnp.dot(
        gathered, lax.all_gather(w_in, "wb", axis=0, tiled=True), preferred_element_type=jnp.float32
    )
    mlstm_in = mlstm_full.astype(jnp.bfloat16)
    gate_out = jnp.dot(gathered, w_outgate, preferred_element_type=jnp.float32)
    gate_pre = jnp.dot(gathered, w_gates, preferred_element_type=jnp.float32)
    pick = (jnp.arange(heads) == head_index).astype(jnp.float32)
    in_gate = jnp.sum(gate_pre[:, :heads] * pick, axis=1) + jnp.sum(igate_bias * pick)
    log_forget = jax.nn.log_sigmoid(
        jnp.sum(gate_pre[:, heads:] * pick, axis=1) + jnp.sum(fgate_bias * pick)
    )
    long_in = mlstm_in[:long_rows]
    slot_in = mlstm_in[long_rows:]
    previous = passed_along(long_in[long_rows - rim :], "seq", 1)
    long_conv = causal_conv(long_in, previous, conv_weight)
    slot_conv = causal_conv(slot_in, jnp.zeros((rim, head_width), jnp.bfloat16), conv_weight)
    activated = jax.nn.silu(jnp.concatenate([long_conv, slot_conv], axis=0))
    queries = block_diagonal(activated, w_query).astype(jnp.bfloat16)
    key_rows = block_diagonal(activated, w_key).astype(jnp.bfloat16)
    value_blocks = lax.dynamic_slice_in_dim(
        w_value, column_index * (value_width // block_size), value_width // block_size, 0
    )
    value_cols = lax.dynamic_slice_in_dim(mlstm_in, column_index * value_width, value_width, 1)
    value_rows = block_diagonal(value_cols.astype(jnp.float32), value_blocks).astype(jnp.bfloat16)
    long_valid = jnp.ones((long_rows,), bool)
    local_state = block_state(
        key_rows[:long_rows],
        value_rows[:long_rows],
        in_gate[:long_rows],
        log_forget[:long_rows],
        long_valid,
    )
    local_tuple = (
        local_state[0],
        local_state[1],
        jnp.reshape(local_state[2], (1,)),
        jnp.reshape(local_state[3], (1,)),
    )
    identity = (
        jnp.zeros_like(local_state[0]),
        jnp.zeros_like(local_state[1]),
        jnp.full((1,), NEG_FILL, jnp.float32),
        jnp.zeros((1,), jnp.float32),
    )
    prefix = entering(local_tuple, "seq", merge_states, identity)
    carried = (prefix[0], prefix[1], prefix[2][0])
    long_hidden = block_hidden(
        queries[:long_rows],
        key_rows[:long_rows],
        value_rows[:long_rows],
        in_gate[:long_rows],
        log_forget[:long_rows],
        long_valid,
        carried,
    )
    final = merge_states(prefix, local_tuple)
    slot_valid = jnp.arange(slot_rows) < short_len[0]
    slot_hidden = block_hidden(
        queries[long_rows:],
        key_rows[long_rows:],
        value_rows[long_rows:],
        in_gate[long_rows:],
        log_forget[long_rows:],
        slot_valid,
        None,
    )
    slot_state = block_state(
        key_rows[long_rows:],
        value_rows[long_rows:],
        in_gate[long_rows:],
        log_forget[long_rows:],
        slot_valid,
    )
    hidden = jnp.concatenate([long_hidden, slot_hidden], axis=0)
    sums = lax.psum((jnp.sum(hidden, axis=1), jnp.sum(hidden * hidden, axis=1)), "wb")
    mean = sums[0] / head_width
    square = sums[1] / head_width
    normed = (
        (hidden - mean[:, None]) * lax.rsqrt(square - mean * mean + EPSILON)[:, None] * norm_gain
    )
    act_cols = lax.dynamic_slice_in_dim(activated, column_index * value_width, value_width, 1)
    row_valid = jnp.concatenate([long_valid, slot_valid], axis=0).astype(jnp.float32)
    gated = ((normed + skip_gain * act_cols) * jax.nn.silu(gate_out) * row_valid[:, None]).astype(
        jnp.bfloat16
    )
    terms = jnp.dot(gated, w_down, preferred_element_type=jnp.float32)
    mixed = lax.psum_scatter(
        terms.astype(jnp.bfloat16), ("wa", "wb"), scatter_dimension=1, tiled=True
    )
    long_y = mixed[:long_rows]
    short_y = mixed[long_rows:][None]
    slot_edge = edge_rows(slot_in, short_len[0], rim)
    is_last = lax.axis_index("seq") == lax.axis_size("seq") - 1
    cache_c = jnp.where(is_last, final[0], slot_state[0])[None, None]
    cache_n = jnp.where(is_last, final[1], slot_state[1])[None, None]
    cache_m = jnp.reshape(jnp.where(is_last, final[2][0], slot_state[2]), (1, 1))
    cache_conv = jnp.where(is_last, long_in[long_rows - rim :], slot_edge)[None]
    return (long_y, short_y, cache_c, cache_n, cache_m, cache_conv)


def flipped(index, mask):
    out, bit = index, 1
    while bit <= mask:
        if mask & bit:
            out = out + bit - 2 * bit * lax.rem(lax.div(index, bit), 2)
        bit *= 2
    return out


def mega_kernel(
    nwa, nwb, nseq,
    len_hbm, ib_hbm, fb_hbm,
    lx_ref, sx_ref, w_in_hbm, wg_hbm, cw_hbm, wq_hbm, wk_hbm, wv_hbm, gain_hbm, skip_hbm, w_og_hbm, w_down_hbm,
    ly_ref, sy_ref, c_ref, n_ref, m_ref, cc_ref,
    xg, own_ref, psend, precv, gsend, grecv, mg, tail, ext_l, ext_s, act, qs, kb, vb, esend, erecv, hs,
    ga, wd, yacc, zsend, zrecv, wsq, wlo,
    w_in_ref, wg_ref, cw_ref, wq_ref, wk_ref, wv_ref, gain_ref, skip_ref, w_og_ref,
    len_ref, ib_ref, fb_ref,
    p_ss, p_rs, g_ss, g_rs, m_ss, m_rs, x_ss, x_rs, xa_ss, xa_rs, e_ss, e_rs,
    t_ss, t_rs, k_ss, k_rs, v_ss, v_rs, o_ss, o_rs, z_ss, z_rs, d_ss, d_rs, f_ss, f_rs, w_sem,
):
    f32, bf16 = jnp.float32, jnp.bfloat16
    seq, wa, wb = lax.axis_index("seq"), lax.axis_index("wa"), lax.axis_index("wb")
    rl, rs = lx_ref.shape[0], sx_ref.shape[0]
    rows = rl + rs
    kd = lx_ref.shape[1]
    gw = mg.shape[2]
    na, nb = nwa - 1, nwb - 1
    other = lax.rem(seq + 1, nseq)
    group_a = [flipped(wa, j) for j in range(nwa)]
    group_b = [flipped(wb, i) for i in range(nwb)]
    barrier = pltpu.get_barrier_semaphore()
    peers_a = [(seq, group_a[j], wb) for j in range(1, nwa)]
    peers_b = [(seq, wa, group_b[i]) for i in range(1, nwb)]
    cross_b = [(other, wa, group_b[i]) for i in range(nwb)]
    peer = cross_b[0]
    everyone = peers_a + peers_b + cross_b
    for p in everyone:
        pl.semaphore_signal(barrier, inc=1, device_id=p, device_id_type=MESH)
    loads = []

    def load(src, dst):
        copy = pltpu.make_async_copy(src, dst, w_sem.at[len(loads)])
        copy.start()
        loads.append(copy)
        return copy

    half = wd.shape[1] // 2
    quarter = wd.shape[2]

    def quarter_of(owner):
        return pl.ds(pl.multiple_of(owner * quarter, 128), quarter)

    first = [load(lx_ref, xg.at[0, 0:rl, :]), load(sx_ref, xg.at[0, rl:rows, :])]
    first += [load(wg_hbm, wg_ref), load(w_in_hbm, w_in_ref)]
    small = [(wq_hbm, wq_ref), (wk_hbm, wk_ref), (wv_hbm, wv_ref), (cw_hbm, cw_ref)]
    small += [(len_hbm, len_ref), (ib_hbm, ib_ref), (fb_hbm, fb_ref)]
    small = [load(src, dst) for src, dst in small]
    late = [load(src, dst) for src, dst in ((gain_hbm, gain_ref), (skip_hbm, skip_ref))]
    late += [load(w_og_hbm, w_og_ref), load(w_down_hbm.at[:, quarter_of(wa)], wd.at[0])]

    sent = []

    def send(src, dst, ssem, rsem, device):
        copy = pltpu.make_async_remote_copy(
            src_ref=src, dst_ref=dst, send_sem=ssem, recv_sem=rsem,
            device_id=device, device_id_type=MESH,
        )
        copy.start()
        sent.append(copy)
        return copy

    def edge_copy(i):
        return pltpu.make_async_remote_copy(
            src_ref=mg.at[0, rl - 16 : rl, :], dst_ref=tail.at[i], send_sem=t_ss.at[i],
            recv_sem=t_rs.at[i], device_id=cross_b[i], device_id_type=MESH,
        )

    def dot(a, b, dims=((1,), (0,))):
        return lax.dot_general(a, b, (dims, ((), ())), preferred_element_type=f32)

    def columns_of(owner):
        return pl.ds(pl.multiple_of(owner * gw, 128), gw)

    far_first = list(range(nb, 0, -1))

    @pl.when(seq == 0)
    def _():
        tail[...] = jnp.zeros_like(tail)

    for c in first:
        c.wait()
    x = xg[0]
    for i in far_first:
        psend[i - 1] = dot(x, w_in_ref[:, columns_of(group_b[i])]).astype(bf16)
    gp = dot(wg_ref[:, pl.ds(pl.multiple_of(wb * kd, 128), kd)], x, ((1,), (1,)))
    row_id = lax.broadcasted_iota(jnp.int32, gp.shape, 0)
    gsend[...] = jnp.zeros_like(gsend)
    for at, head in ((0, wa), (2, wa + gp.shape[0] // 2)):
        row = jnp.sum(jnp.where(row_id == head, gp, 0.0), axis=0, keepdims=True)
        gsend[at : at + 1, 0:rl] = row[:, 0:rl]
        gsend[at + 1 : at + 2, 0:rs] = row[:, rl:rows]
    pl.semaphore_wait(barrier, len(everyone))
    copies_p, copies_g, copies_x = [], [None] * nb, [None] * nb
    part = rows // nwa
    share = pl.ds(pl.multiple_of(wa * part, 16), part)
    cuts = [(0, rl), (rl, rows)]

    def send_x():
        for i in (2, 1):
            at = i - 1
            copies_x[at] = send(
                xg.at[0, share, :], xg.at[i, share, :], x_ss.at[at], x_rs.at[at], peers_b[at]
            )

    for c, (start, end) in enumerate(cuts):
        if c == 1:
            send_x()
        copies_p.append([None] * nb)
        for i in far_first:
            at, span = i - 1, slice(start, end)
            copies_p[c][at] = send(
                psend.at[at, span, :], precv.at[at, span, :],
                p_ss.at[c * nb + at], p_rs.at[c * nb + at], peers_b[at],
            )
        if c == 0:
            for i in far_first:
                at = i - 1
                copies_g[at] = send(gsend, grecv.at[at], g_ss.at[at], g_rs.at[at], peers_b[at])
    if 1 >= len(cuts):
        send_x()
    mine = pl.ds(pl.multiple_of(seq * half, 16), half)
    copies_d = []
    for j in range(1, nwa):
        copies_d.append(
            send(
                w_down_hbm.at[mine, quarter_of(group_a[j])], wd.at[j, mine, :],
                d_ss.at[j - 1], d_rs.at[j - 1], peers_a[j - 1],
            )
        )
    own_ref[...] = dot(x, w_in_ref[:, columns_of(wb)])

    def halves(a):
        top = a.astype(bf16)
        return top, (a - top.astype(f32)).astype(bf16)

    row_sq = lax.broadcasted_iota(jnp.int32, (gw, gw), 0)
    col_sq = lax.broadcasted_iota(jnp.int32, (gw, gw), 1)
    same = row_sq // 4 == col_sq // 4
    inner = lax.rem(row_sq, 4)
    blocks = wq_ref.shape[2]
    outer = lax.rem(lax.broadcasted_iota(jnp.int32, (4, gw), 1), 4) == lax.broadcasted_iota(
        jnp.int32, (4, gw), 0
    )
    block_at = lax.broadcasted_iota(jnp.int32, (blocks, gw), 0)
    block_of = lax.broadcasted_iota(jnp.int32, (blocks, gw), 1) // 4
    for c in small:
        c.wait()
    for n in range(nwb):
        spread = (block_at == group_b[n] * (gw // 4) + block_of).astype(bf16)
        for kind, ref in enumerate((wq_ref, wk_ref, wv_ref)):
            full = jnp.zeros((gw, gw), f32)
            for i in range(4):
                top, rest = halves(ref[i])
                wide = dot(top, spread) + dot(rest, spread)
                coef = jnp.sum(jnp.where(outer, wide, 0.0), axis=0, keepdims=True)
                full = jnp.where(inner == i, coef, full)
            wsq[kind * nwb + n], wlo[kind * nwb + n] = halves(jnp.where(same, full, 0.0))

    copies_m = []
    copies_xa = []

    def relay_x():
        copies_x[1].wait_recv()
        copies_x[2] = send(
            xg.at[2, share, :], xg.at[3, share, :], x_ss.at[2], x_rs.at[2], peers_b[0]
        )

    def spread_x(i):
        if i != 2:
            copies_x[i - 1].wait_recv()
        src = xg.at[i, share, :]
        for j in range(na):
            at = (i - 1) * na + j
            copies_xa.append(send(src, src, xa_ss.at[at], xa_rs.at[at], peers_a[j]))

    for c, (start, end) in enumerate(cuts):
        if c == 1:
            relay_x()
            spread_x(2)
            spread_x(1)
        span = slice(start, end)
        total = own_ref[span, :]
        for i in far_first:
            copies_p[c][i - 1].wait_recv()
            total = total + precv[i - 1, span, :].astype(f32)
        mg[0, span, :] = total.astype(bf16)
        if start < rl <= end:

            @pl.when(seq == 0)
            def _():
                for i in [0] + far_first:
                    edge_copy(i).start()

        copies_m.append([None] * nb)
        for i in far_first if c else (2, 1):
            at = i - 1
            copies_m[c][at] = send(
                mg.at[0, span, :], mg.at[i, span, :],
                m_ss.at[c * nb + at], m_rs.at[c * nb + at], peers_b[at],
            )

    for c in copies_g:
        c.wait_recv()
    sums = [gsend[...]] + [grecv[i] for i in range(nb)]
    while len(sums) > 1:
        sums = [sums[i] + sums[i + 1] for i in range(0, len(sums), 2)]
    gates = sums[0]
    ig = gates[0:2] + ib_ref[wa]
    fg = gates[2:4] + fb_ref[wa]
    lf = jnp.minimum(fg, 0.0) - jnp.log1p(jnp.exp(-jnp.abs(fg)))
    length = len_ref[0, 0]
    last = seq == nseq - 1

    def block_gates(i_row, f_row, size, limit):
        t = lax.broadcasted_iota(jnp.int32, (size, size), 0)
        s = lax.broadcasted_iota(jnp.int32, (size, size), 1)
        valid = lax.broadcasted_iota(jnp.int32, (1, size), 1) < limit
        f_row = jnp.where(valid, f_row, 0.0)
        b_col = jnp.sum(jnp.where(s <= t, f_row, 0.0), axis=1, keepdims=True)
        b_row = jnp.sum(jnp.where(s == t, b_col, 0.0), axis=0, keepdims=True)
        total = jnp.sum(f_row, axis=1, keepdims=True)
        e_row = jnp.where(valid, total - b_row + i_row, NEG_FILL)
        causal = (s <= t) & (s < limit)
        logw = jnp.where(causal, b_col - b_row + i_row, NEG_FILL)
        return b_col, total, e_row, causal, logw

    def to_col(row):
        size = row.shape[1]
        t = lax.broadcasted_iota(jnp.int32, (size, size), 0)
        s = lax.broadcasted_iota(jnp.int32, (size, size), 1)
        return jnp.sum(jnp.where(s == t, row, 0.0), axis=1, keepdims=True)

    bl, totl, el, causl, logl = block_gates(ig[0:1, 0:rl], lf[0:1, 0:rl], rl, rl)
    bs, tots, es, causs, logs = block_gates(ig[1:2, 0:rs], lf[1:2, 0:rs], rs, length)
    esend[...] = jnp.broadcast_to(el, esend.shape)
    ce = send(esend, erecv, e_ss.at[0], e_rs.at[0], peer)
    pick_row = lax.broadcasted_iota(jnp.int32, (8, rows), 0)
    pick_at = lax.broadcasted_iota(jnp.int32, (8, rows), 1)
    slot_at = length - 3 + pick_row
    target = jnp.where(last, rl - 3 + pick_row, jnp.where(slot_at >= 0, rl + slot_at, -1))
    pick = (pick_at == target).astype(bf16)
    first_keep = jnp.where(seq > 0, 1.0, 0.0)
    scale = (gw * nwb) ** (-0.5)
    copies_k, copies_v, copies_f, scores_l, scores_s = [], [], [], [], []

    def mixed(a, kind, n):
        top, rest = halves(a)
        wide = wsq[kind * nwb + n]
        return (dot(top, wide) + dot(rest, wide) + dot(top, wlo[kind * nwb + n])).astype(bf16)

    def convolved(ext, n, size):
        taps = cw_ref[:, columns_of(group_b[n])]
        conv = jnp.zeros((size, gw), f32)
        for j in range(4):
            conv = conv + taps[j : j + 1] * ext[5 + j : 5 + j + size, :]
        return conv / (1.0 + jnp.exp(-conv))

    def long_part(n):
        m = mg[n, 0:rl, :]
        v = (dot(m, wsq[2 * nwb + n]) + dot(m, wlo[2 * nwb + n])).astype(bf16)
        vb[n, rl : 2 * rl, :] = v
        copies_v.append(
            send(vb.at[n, rl : 2 * rl, :], vb.at[n, 0:rl, :], v_ss.at[n], v_rs.at[n], peer)
        )

        @pl.when(seq > 0)
        def _():
            edge_copy(n).wait_recv()

        ext_l[0:8, :] = tail[n].astype(f32)[8:16] * first_keep
        ext_l[8 : 8 + rl, :] = m.astype(f32)
        a = convolved(ext_l, n, rl)
        if n == 0:
            act[0:rl, :] = a
        k = mixed(a, 1, n)
        kb[n, rl : 2 * rl, :] = k
        copies_k.append(
            send(kb.at[n, rl : 2 * rl, :], kb.at[n, 0:rl, :], k_ss.at[n], k_rs.at[n], peer)
        )
        q = mixed(a, 0, n)
        qs[n] = q
        scores_l.append(dot(q, k, ((1,), (1,))))

    def short_part(n):
        m = mg[n, rl:rows, :]
        vb[n, 2 * rl : rl + rows, :] = (
            dot(m, wsq[2 * nwb + n]) + dot(m, wlo[2 * nwb + n])
        ).astype(bf16)
        ext_s[8 : 8 + rs, :] = m.astype(f32)
        a = convolved(ext_s, n, rs)
        if n == 0:
            act[rl:rows, :] = a
        k = mixed(a, 1, n)
        kb[n, 2 * rl : rl + rows, :] = k
        scores_s.append(dot(mixed(a, 0, n), k, ((1,), (1,))))

    ext_s[0:8, :] = jnp.zeros((8, gw), f32)
    long_part(0)
    short_part(0)
    spread_x(3)
    for j in range(na):
        copies_d[j].wait_recv()
        src = wd.at[j + 1, mine, :]
        copies_f.append(send(src, src, f_ss.at[j], f_rs.at[j], peer))
    copies_m[0][1].wait_recv()
    copies_m[0][2] = send(
        mg.at[2, 0:rl, :], mg.at[3, 0:rl, :], m_ss.at[2], m_rs.at[2], peers_b[0]
    )
    copies_m[0][0].wait_recv()
    long_part(1)
    long_part(2)
    copies_m[1][0].wait_recv()
    short_part(1)
    copies_m[0][2].wait_recv()
    long_part(3)
    for n in (2, 3):
        copies_m[1][n - 1].wait_recv()
        short_part(n)
    sl, ss = sum(scores_l[1:], scores_l[0]), sum(scores_s[1:], scores_s[0])

    for c in late:
        c.wait()
    for c in copies_xa:
        c.wait_recv()
    inv = 1.0 / (gw * nwb)
    gain, skip = gain_ref[...], skip_ref[...]
    gate = jnp.zeros((rows, gw), f32)
    for i in range(nwb):
        gate = gate + dot(xg[i], w_og_ref[pl.ds(pl.multiple_of(group_b[i] * kd, 128), kd), :])
    gate = gate / (1.0 + jnp.exp(-gate))
    copies_o = []

    def gated(start, size, hidden, total, square_sum, keep):
        mean = total * inv
        norm = lax.rsqrt(square_sum * inv - mean * mean + EPSILON)
        normed = (hidden - mean) * norm * gain
        out = (normed + skip * act[start : start + size, :]) * gate[start : start + size]
        return (out if keep is None else out * keep).astype(bf16)

    def share_out(start, size):
        span = slice(start, start + size)
        row = len(copies_o)
        copies_o.append([])
        for j in range(1, nwa):
            at = row * na + j - 1
            copies_o[-1].append(
                send(ga.at[0, span, :], ga.at[j, span, :], o_ss.at[at], o_rs.at[at], peers_a[j - 1])
            )

    rmax_s = jnp.max(logs, axis=1, keepdims=True)
    mix_s = ss * scale * jnp.where(causs, jnp.exp(logs - rmax_s), 0.0)
    den_s = jnp.sum(mix_s, axis=1, keepdims=True)
    div_s = jnp.maximum(jnp.abs(den_s), jnp.exp(-rmax_s))
    mix_s = mix_s.astype(bf16)
    sum_s = jnp.zeros((rs, 1), f32)
    sq_s = jnp.zeros((rs, 1), f32)
    for n in range(nwb):
        hh = dot(mix_s, vb[n, 2 * rl : rl + rows, :]) / div_s
        if n == 0:
            own_s = hh
        sum_s += jnp.sum(hh, axis=1, keepdims=True)
        sq_s += jnp.sum(hh * hh, axis=1, keepdims=True)
    ok_s = (lax.broadcasted_iota(jnp.int32, (rs, 1), 0) < length).astype(f32)
    ga[0, rl:rows, :] = gated(rl, rs, own_s, sum_s, sq_s, ok_s)
    share_out(rl, rs)

    ce.wait_recv()
    ep = erecv[0:1, :]
    mp = jnp.max(ep, axis=1, keepdims=True)
    carry_m = jnp.where(seq > 0, mp, NEG_FILL)
    carry_log = bl + carry_m
    rmax_l = jnp.maximum(jnp.max(logl, axis=1, keepdims=True), carry_log)
    mix_l = sl * scale * jnp.where(causl, jnp.exp(logl - rmax_l), 0.0)
    for c in copies_k + copies_v:
        c.wait_recv()
    sp = jnp.zeros((rl, rl), f32)
    for n in range(nwb):
        sp = sp + dot(qs[n], kb[n, 0:rl, :], ((1,), (1,)))
    mix_p = sp * scale * jnp.exp(ep - mp) * jnp.exp(carry_log - rmax_l)
    den_l = jnp.sum(mix_l, axis=1, keepdims=True) + jnp.sum(mix_p, axis=1, keepdims=True)
    div_l = jnp.maximum(jnp.abs(den_l), jnp.exp(-rmax_l))
    mix = jnp.concatenate([mix_p, mix_l], axis=1).astype(bf16)
    sum_l = jnp.zeros((rl, 1), f32)
    sq_l = jnp.zeros((rl, 1), f32)
    for n in range(nwb):
        hl = dot(mix, vb[n, 0 : 2 * rl, :]) / div_l
        if n == 0:
            hs[...] = hl
        sum_l += jnp.sum(hl, axis=1, keepdims=True)
        sq_l += jnp.sum(hl * hl, axis=1, keepdims=True)
    step = rl // 2
    for start in (0, step):
        span = slice(start, start + step)
        ga[0, span, :] = gated(start, step, hs[span, :], sum_l[span], sq_l[span], None)
        share_out(start, step)

    ml = jnp.max(el, axis=1, keepdims=True)
    shifted = carry_m + totl
    joined = jnp.maximum(shifted, ml)
    ms = jnp.max(es, axis=1, keepdims=True)
    m_ref[...] = jnp.where(last, joined, ms)
    keep_p = jnp.where(last & (seq > 0), 1.0, 0.0)
    keep_l = jnp.where(last, 1.0, 0.0)
    wp = to_col(jnp.exp(ep - mp) * jnp.exp(shifted - joined)) * (keep_p * scale)
    wl = to_col(jnp.exp(el - joined)) * (keep_l * scale)
    ws = to_col(jnp.where(es > 0.5 * NEG_FILL, jnp.exp(es - ms), 0.0)) * ((1.0 - keep_l) * scale)
    weight = jnp.concatenate([wp, wl, ws], axis=0)
    vw = (vb[0].astype(f32) * weight).astype(bf16)
    for n in range(nwb):
        lanes = columns_of(group_b[n])
        keys = kb[n]
        cc_ref[0, :, lanes] = dot(pick, mg[n])[0:3].astype(bf16)
        c_ref[0, 0, :, lanes] = dot(vw, keys, ((0,), (0,)))
        n_ref[0, :, lanes] = jnp.sum(keys.astype(f32) * weight, axis=0, keepdims=True)

    for c in copies_f:
        c.wait_recv()
    ow = zrecv.shape[2]
    copies_z = []
    spans = [(rl, rs), (0, step), (step, step)]

    def piece_of(owner):
        return pl.ds(pl.multiple_of(owner * ow, 128), ow)

    for row, (start, size) in enumerate(spans):
        span = slice(start, start + size)
        y = dot(ga[0, span, :], wd[0])
        for j in range(1, nwa):
            copies_o[row][j - 1].wait_recv()
            y = y + dot(ga[j, span, :], wd[j])
        yacc[span, :] = y
        copies_z.append([])
        for i in range(1, nwb):
            at = row * nb + i - 1
            zsend[i - 1, span, :] = yacc[span, piece_of(group_b[i])].astype(bf16)
            copies_z[-1].append(
                send(
                    zsend.at[i - 1, span, :], zrecv.at[i - 1, span, :],
                    z_ss.at[at], z_rs.at[at], peers_b[i - 1],
                )
            )
    for row, (start, size) in enumerate(spans):
        span = slice(start, start + size)
        y = yacc[span, piece_of(wb)]
        for i in range(nb):
            copies_z[row][i].wait_recv()
            y = y + zrecv[i, span, :].astype(f32)
        if start == rl:
            sy_ref[0] = y.astype(bf16)
        else:
            ly_ref[span, :] = y.astype(bf16)
    for c in sent:
        c.wait_send()

    @pl.when(seq == 0)
    def _():
        for i in range(nwb):
            edge_copy(i).wait_send()


def write_kernel(*refs):
    sources, targets, sem = refs[:6], refs[6:12], refs[12]
    copies = [
        pltpu.make_async_copy(src, dst, sem.at[i])
        for i, (src, dst) in enumerate(zip(sources, targets))
    ]
    for c in copies:
        c.start()
    for c in copies:
        c.wait()


def fused_body(
    long_x, short_x, short_len, w_in, w_outgate, w_gates, conv_weight, w_query, w_key, w_value,
    igate_bias, fgate_bias, norm_gain, skip_gain, w_down,
):
    nseq, nwa, nwb = (lax.axis_size(a) for a in ("seq", "wa", "wb"))
    f32, bf16 = jnp.float32, jnp.bfloat16
    rl, kd = long_x.shape
    rs = short_x.shape[1]
    rows = rl + rs
    gw = w_outgate.shape[1]
    hw = w_in.shape[1]
    ow = w_down.shape[1] // (nwa * nwb)
    turned = [w.transpose(1, 2, 0) for w in (w_query, w_key, w_value)]
    vm = pl.BlockSpec(memory_space=pltpu.VMEM)
    hbm = pl.BlockSpec(memory_space=pl.ANY)
    nb, na = nwb - 1, nwa - 1
    dma = pltpu.SemaphoreType.DMA
    shapes = (
        jax.ShapeDtypeStruct((rl, ow), bf16),
        jax.ShapeDtypeStruct((1, rs, ow), bf16),
        jax.ShapeDtypeStruct((1, 1, gw, hw), f32),
        jax.ShapeDtypeStruct((1, 1, hw), f32),
        jax.ShapeDtypeStruct((1, 1), f32),
        jax.ShapeDtypeStruct((1, 3, hw), bf16),
    )
    inputs = (
        short_len[:, None], igate_bias, fgate_bias, long_x, short_x[0], w_in, w_gates.T,
        conv_weight, *turned, norm_gain[None], skip_gain[None], w_outgate, w_down,
    )
    outs = pl.pallas_call(
        functools.partial(mega_kernel, nwa, nwb, nseq),
        out_shape=tuple(pltpu.VMEM(a.shape, a.dtype) for a in shapes),
        in_specs=[pl.BlockSpec(memory_space=pltpu.HBM)] * 15,
        out_specs=(vm,) * 6,
        scratch_shapes=[
            pltpu.VMEM((nwb, rows, kd), bf16),
            pltpu.VMEM((rows, gw), f32),
            pltpu.VMEM((nb, rows, gw), bf16),
            pltpu.VMEM((nb, rows, gw), bf16),
            pltpu.VMEM((8, max(rl, rs)), f32),
            pltpu.VMEM((nb, 8, max(rl, rs)), f32),
            pltpu.VMEM((nwb, rows, gw), bf16),
            pltpu.VMEM((nwb, 16, gw), bf16),
            pltpu.VMEM((8 + rl, gw), f32),
            pltpu.VMEM((8 + rs, gw), f32),
            pltpu.VMEM((rows, gw), f32),
            pltpu.VMEM((nwb, rl, gw), bf16),
            pltpu.VMEM((nwb, rl + rows, gw), bf16),
            pltpu.VMEM((nwb, rl + rows, gw), bf16),
            pltpu.VMEM((8, rl), f32),
            pltpu.VMEM((8, rl), f32),
            pltpu.VMEM((rl, gw), f32),
            pltpu.VMEM((nwa, rows, gw), bf16),
            pltpu.VMEM((nwa, gw, nwb * ow), bf16),
            pltpu.VMEM((rows, nwb * ow), f32),
            pltpu.VMEM((nb, rows, ow), bf16),
            pltpu.VMEM((nb, rows, ow), bf16),
            pltpu.VMEM((3 * nwb, gw, gw), bf16),
            pltpu.VMEM((3 * nwb, gw, gw), bf16),
            pltpu.VMEM(w_in.shape, bf16),
            pltpu.VMEM(w_gates.shape[::-1], bf16),
            pltpu.VMEM(conv_weight.shape, f32),
            pltpu.VMEM(turned[0].shape, f32),
            pltpu.VMEM(turned[1].shape, f32),
            pltpu.VMEM(turned[2].shape, f32),
            pltpu.VMEM((1, gw), f32),
            pltpu.VMEM((1, gw), f32),
            pltpu.VMEM(w_outgate.shape, bf16),
            pltpu.SMEM((1, 1), jnp.int32),
            pltpu.SMEM(igate_bias.shape, f32),
            pltpu.SMEM(fgate_bias.shape, f32),
        ]
        + [dma((3 * nb,))] * 2
        + [dma((nb,))] * 2
        + [dma((3 * nb,))] * 2
        + [dma((nb,))] * 2
        + [dma((nb * na,))] * 2
        + [dma((1,))] * 2
        + [dma((nwb,))] * 6
        + [dma((3 * na,))] * 2
        + [dma((3 * nb,))] * 2
        + [dma((na,))] * 4
        + [dma((15,))],
        compiler_params=pltpu.CompilerParams(
            collective_id=0, has_side_effects=True, vmem_limit_bytes=48 * 2**20
        ),
        name="mlstm_layer",
    )(*(a if a.size == 1 else pltpu.with_memory_space_constraint(a, pltpu.HBM) for a in inputs))
    return pl.pallas_call(
        write_kernel,
        out_shape=shapes,
        in_specs=[vm] * 6,
        out_specs=(pl.BlockSpec(memory_space=pltpu.HBM),) * 6,
        scratch_shapes=[dma((6,))],
        name="write_out",
    )(*(pltpu.with_memory_space_constraint(out, pltpu.VMEM) for out in outs))


def solution(mesh):
    in_specs = (
        P("seq", "wb"),
        P("seq", None, "wb"),
        P("seq"),
        P("wb", "wa"),
        P(None, ("wa", "wb")),
        P(),
        P(None, "wa"),
        P("wa", None, None),
        P("wa", None, None),
        P("wa", None, None),
        P(),
        P(),
        P(("wa", "wb")),
        P(("wa", "wb")),
        P(("wa", "wb"), None),
    )
    out_specs = (
        P("seq", ("wa", "wb")),
        P("seq", None, ("wa", "wb")),
        P("seq", "wa", "wb", None),
        P("seq", "wa", None),
        P("seq", "wa"),
        P("seq", None, "wa"),
    )
    fused = mesh.shape["seq"] == 2 and mesh.shape["wa"] == 4 and mesh.shape["wb"] == 4
    layer = fused_body if fused else body
    return jax.shard_map(layer, mesh=mesh, in_specs=in_specs, out_specs=out_specs, check_vma=False)
```

```python
import functools

import jax
import jax.numpy as jnp
from jax import lax
from jax.experimental import pallas as pl
from jax.experimental.pallas import tpu as pltpu
from jax.sharding import PartitionSpec as P

MESH = pl.DeviceIdType.MESH
NEG_FILL = -1e30
EPSILON = 1e-05
exact_mode = lax.Precision.HIGHEST


def passed_along(array, axis, by):
    devices = lax.axis_size(axis)
    pairs = [(i, i + by) for i in range(devices) if 0 <= i + by < devices]
    return lax.ppermute(array, axis, pairs)


def entering(array, axis, combine, identity):
    devices, index = (lax.axis_size(axis), lax.axis_index(axis))
    everything = jax.tree.map(lambda part: lax.all_gather(part, axis), array)
    start = jax.tree.map(
        lambda part, zero: jnp.broadcast_to(jnp.asarray(zero, part.dtype), part.shape),
        array,
        identity,
    )

    def turn(k, before):
        reached = k < index
        new = combine(before, jax.tree.map(lambda part: part[k], everything))
        return jax.tree.map(lambda a, b: jnp.where(reached, a, b), new, before)

    return lax.fori_loop(0, devices, turn, start)


def block_diagonal(inputs, blocks):
    row_count = inputs.shape[0]
    grouped = inputs.reshape(row_count, blocks.shape[0], blocks.shape[1])
    combined = jnp.einsum("rni,nio->rno", grouped, blocks, precision=exact_mode)
    return combined.reshape(row_count, -1)


def causal_conv(mlstm_in, previous, conv_weight):
    extended = jnp.concatenate([previous.astype(jnp.float32), mlstm_in.astype(jnp.float32)], axis=0)
    row_count = mlstm_in.shape[0]
    running = jnp.zeros(mlstm_in.shape, jnp.float32)
    for offset in range(conv_weight.shape[0]):
        running = running + conv_weight[offset] * extended[offset : offset + row_count]
    return running


def running_sum(row):
    at = jnp.arange(row.shape[0])
    return jnp.sum(jnp.where(at[:, None] >= at[None, :], row[None, :], 0.0), axis=1)


def block_hidden(queries, key_rows, value_rows, in_gate, log_forget, is_valid, carried):
    scaling = key_rows.shape[1] ** (-0.5)
    row_count = queries.shape[0]
    forget_sum = running_sum(jnp.where(is_valid, log_forget, 0.0))
    positions = jnp.arange(row_count)
    causal = (positions[:, None] >= positions[None, :]) & is_valid[None, :]
    log_weight = jnp.where(
        causal, forget_sum[:, None] - forget_sum[None, :] + in_gate[None, :], NEG_FILL
    )
    row_max = jnp.max(log_weight, axis=1)
    if carried is not None:
        carry_log = forget_sum + carried[2]
        row_max = jnp.maximum(row_max, carry_log)
    weights = jnp.where(causal, jnp.exp(log_weight - row_max[:, None]), 0.0)
    scores = jnp.dot(queries, key_rows.T, preferred_element_type=jnp.float32) * scaling
    mixing = scores * weights
    denominator = jnp.sum(mixing, axis=1)
    numerator = jnp.dot(mixing.astype(jnp.bfloat16), value_rows, preferred_element_type=jnp.float32)
    if carried is not None:
        carry_weight = jnp.exp(carry_log - row_max)
        query_wide = queries.astype(jnp.float32)
        numerator = numerator + carry_weight[:, None] * jnp.dot(
            query_wide, carried[0].T, precision=exact_mode
        )
        denominator = denominator + carry_weight * jnp.dot(
            query_wide, carried[1], precision=exact_mode
        )
    return numerator / jnp.maximum(jnp.abs(denominator), jnp.exp(-row_max))[:, None]


def block_state(key_rows, value_rows, in_gate, log_forget, is_valid):
    scaling = key_rows.shape[1] ** (-0.5)
    forget_sum = running_sum(jnp.where(is_valid, log_forget, 0.0))
    forget_total = forget_sum[-1]
    end_log = jnp.where(is_valid, forget_total - forget_sum + in_gate, NEG_FILL)
    end_max = jnp.max(end_log)
    end_weight = jnp.where(is_valid, jnp.exp(end_log - end_max), 0.0)
    key_wide = key_rows.astype(jnp.float32) * scaling
    matrix_state = jnp.dot(
        (value_rows.astype(jnp.float32) * end_weight[:, None]).T, key_wide, precision=exact_mode
    )
    normalizer = jnp.dot(end_weight, key_wide, precision=exact_mode)
    return (matrix_state, normalizer, end_max, forget_total)


def merge_states(earlier, latter):
    state_a, normal_a, max_a, forget_a = earlier
    state_b, normal_b, max_b, forget_b = latter
    shifted = max_a + forget_b
    joined = jnp.maximum(shifted, max_b)
    weight_a = jnp.exp(shifted - joined)
    weight_b = jnp.exp(max_b - joined)
    return (
        weight_a * state_a + weight_b * state_b,
        weight_a * normal_a + weight_b * normal_b,
        joined,
        forget_a + forget_b,
    )


def edge_rows(rows, length, rim):
    select = (jnp.arange(rows.shape[0])[None, :] == length - rim + jnp.arange(rim)[:, None]).astype(
        jnp.float32
    )
    return jnp.dot(select, rows.astype(jnp.float32), precision=exact_mode).astype(jnp.bfloat16)


def body(
    long_x,
    short_x,
    short_len,
    w_in,
    w_outgate,
    w_gates,
    conv_weight,
    w_query,
    w_key,
    w_value,
    igate_bias,
    fgate_bias,
    norm_gain,
    skip_gain,
    w_down,
):
    long_rows = long_x.shape[0]
    slot_rows = short_x.shape[1]
    heads = igate_bias.shape[0]
    head_width = w_in.shape[1]
    value_width = w_outgate.shape[1]
    block_size = w_value.shape[1]
    rim = conv_weight.shape[0] - 1
    head_index = lax.axis_index("wa")
    column_index = lax.axis_index("wb")
    local_rows = jnp.concatenate([long_x, short_x[0]], axis=0)
    gathered = lax.all_gather(local_rows, "wb", axis=1, tiled=True)
    mlstm_full = jnp.dot(
        gathered, lax.all_gather(w_in, "wb", axis=0, tiled=True), preferred_element_type=jnp.float32
    )
    mlstm_in = mlstm_full.astype(jnp.bfloat16)
    gate_out = jnp.dot(gathered, w_outgate, preferred_element_type=jnp.float32)
    gate_pre = jnp.dot(gathered, w_gates, preferred_element_type=jnp.float32)
    pick = (jnp.arange(heads) == head_index).astype(jnp.float32)
    in_gate = jnp.sum(gate_pre[:, :heads] * pick, axis=1) + jnp.sum(igate_bias * pick)
    log_forget = jax.nn.log_sigmoid(
        jnp.sum(gate_pre[:, heads:] * pick, axis=1) + jnp.sum(fgate_bias * pick)
    )
    long_in = mlstm_in[:long_rows]
    slot_in = mlstm_in[long_rows:]
    previous = passed_along(long_in[long_rows - rim :], "seq", 1)
    long_conv = causal_conv(long_in, previous, conv_weight)
    slot_conv = causal_conv(slot_in, jnp.zeros((rim, head_width), jnp.bfloat16), conv_weight)
    activated = jax.nn.silu(jnp.concatenate([long_conv, slot_conv], axis=0))
    queries = block_diagonal(activated, w_query).astype(jnp.bfloat16)
    key_rows = block_diagonal(activated, w_key).astype(jnp.bfloat16)
    value_blocks = lax.dynamic_slice_in_dim(
        w_value, column_index * (value_width // block_size), value_width // block_size, 0
    )
    value_cols = lax.dynamic_slice_in_dim(mlstm_in, column_index * value_width, value_width, 1)
    value_rows = block_diagonal(value_cols.astype(jnp.float32), value_blocks).astype(jnp.bfloat16)
    long_valid = jnp.ones((long_rows,), bool)
    local_state = block_state(
        key_rows[:long_rows],
        value_rows[:long_rows],
        in_gate[:long_rows],
        log_forget[:long_rows],
        long_valid,
    )
    local_tuple = (
        local_state[0],
        local_state[1],
        jnp.reshape(local_state[2], (1,)),
        jnp.reshape(local_state[3], (1,)),
    )
    identity = (
        jnp.zeros_like(local_state[0]),
        jnp.zeros_like(local_state[1]),
        jnp.full((1,), NEG_FILL, jnp.float32),
        jnp.zeros((1,), jnp.float32),
    )
    prefix = entering(local_tuple, "seq", merge_states, identity)
    carried = (prefix[0], prefix[1], prefix[2][0])
    long_hidden = block_hidden(
        queries[:long_rows],
        key_rows[:long_rows],
        value_rows[:long_rows],
        in_gate[:long_rows],
        log_forget[:long_rows],
        long_valid,
        carried,
    )
    final = merge_states(prefix, local_tuple)
    slot_valid = jnp.arange(slot_rows) < short_len[0]
    slot_hidden = block_hidden(
        queries[long_rows:],
        key_rows[long_rows:],
        value_rows[long_rows:],
        in_gate[long_rows:],
        log_forget[long_rows:],
        slot_valid,
        None,
    )
    slot_state = block_state(
        key_rows[long_rows:],
        value_rows[long_rows:],
        in_gate[long_rows:],
        log_forget[long_rows:],
        slot_valid,
    )
    hidden = jnp.concatenate([long_hidden, slot_hidden], axis=0)
    sums = lax.psum((jnp.sum(hidden, axis=1), jnp.sum(hidden * hidden, axis=1)), "wb")
    mean = sums[0] / head_width
    square = sums[1] / head_width
    normed = (
        (hidden - mean[:, None]) * lax.rsqrt(square - mean * mean + EPSILON)[:, None] * norm_gain
    )
    act_cols = lax.dynamic_slice_in_dim(activated, column_index * value_width, value_width, 1)
    row_valid = jnp.concatenate([long_valid, slot_valid], axis=0).astype(jnp.float32)
    gated = ((normed + skip_gain * act_cols) * jax.nn.silu(gate_out) * row_valid[:, None]).astype(
        jnp.bfloat16
    )
    terms = jnp.dot(gated, w_down, preferred_element_type=jnp.float32)
    mixed = lax.psum_scatter(
        terms.astype(jnp.bfloat16), ("wa", "wb"), scatter_dimension=1, tiled=True
    )
    long_y = mixed[:long_rows]
    short_y = mixed[long_rows:][None]
    slot_edge = edge_rows(slot_in, short_len[0], rim)
    is_last = lax.axis_index("seq") == lax.axis_size("seq") - 1
    cache_c = jnp.where(is_last, final[0], slot_state[0])[None, None]
    cache_n = jnp.where(is_last, final[1], slot_state[1])[None, None]
    cache_m = jnp.reshape(jnp.where(is_last, final[2][0], slot_state[2]), (1, 1))
    cache_conv = jnp.where(is_last, long_in[long_rows - rim :], slot_edge)[None]
    return (long_y, short_y, cache_c, cache_n, cache_m, cache_conv)


def flipped(index, mask):
    out, bit = index, 1
    while bit <= mask:
        if mask & bit:
            out = out + bit - 2 * bit * lax.rem(lax.div(index, bit), 2)
        bit *= 2
    return out


def mega_kernel(
    nwa, nwb, nseq,
    len_hbm, ib_hbm, fb_hbm,
    lx_ref, sx_ref, w_in_hbm, wg_hbm, cw_hbm, wq_hbm, wk_hbm, wv_hbm, gain_hbm, skip_hbm, w_og_hbm, w_down_hbm,
    ly_ref, sy_ref, c_ref, n_ref, m_ref, cc_ref,
    xg, own_ref, psend, precv, gsend, grecv, mg, tail, ext_l, ext_s, act, qs, kb, vb, esend, erecv, hs,
    ga, wd, yacc, zsend, zrecv, wsq, wlo,
    w_in_ref, wg_ref, cw_ref, wq_ref, wk_ref, wv_ref, gain_ref, skip_ref, w_og_ref,
    len_ref, ib_ref, fb_ref,
    p_ss, p_rs, g_ss, g_rs, m_ss, m_rs, x_ss, x_rs, xa_ss, xa_rs, e_ss, e_rs,
    t_ss, t_rs, k_ss, k_rs, v_ss, v_rs, o_ss, o_rs, z_ss, z_rs, d_ss, d_rs, f_ss, f_rs, w_sem,
):
    f32, bf16 = jnp.float32, jnp.bfloat16
    seq, wa, wb = lax.axis_index("seq"), lax.axis_index("wa"), lax.axis_index("wb")
    rl, rs = lx_ref.shape[0], sx_ref.shape[0]
    rows = rl + rs
    kd = lx_ref.shape[1]
    gw = mg.shape[2]
    na, nb = nwa - 1, nwb - 1
    other = lax.rem(seq + 1, nseq)
    group_a = [flipped(wa, j) for j in range(nwa)]
    group_b = [flipped(wb, i) for i in range(nwb)]
    barrier = pltpu.get_barrier_semaphore()
    peers_a = [(seq, group_a[j], wb) for j in range(1, nwa)]
    peers_b = [(seq, wa, group_b[i]) for i in range(1, nwb)]
    cross_b = [(other, wa, group_b[i]) for i in range(nwb)]
    peer = cross_b[0]
    everyone = peers_a + peers_b + cross_b
    for p in everyone:
        pl.semaphore_signal(barrier, inc=1, device_id=p, device_id_type=MESH)
    loads = []

    def load(src, dst):
        copy = pltpu.make_async_copy(src, dst, w_sem.at[len(loads)])
        copy.start()
        loads.append(copy)
        return copy

    half = wd.shape[1] // 2
    quarter = wd.shape[2]

    def quarter_of(owner):
        return pl.ds(pl.multiple_of(owner * quarter, 128), quarter)

    first = [load(lx_ref, xg.at[0, 0:rl, :]), load(sx_ref, xg.at[0, rl:rows, :])]
    first += [load(wg_hbm, wg_ref), load(w_in_hbm, w_in_ref)]
    small = [(wq_hbm, wq_ref), (wk_hbm, wk_ref), (wv_hbm, wv_ref), (cw_hbm, cw_ref)]
    small += [(len_hbm, len_ref), (ib_hbm, ib_ref), (fb_hbm, fb_ref)]
    small = [load(src, dst) for src, dst in small]
    late = [load(src, dst) for src, dst in ((gain_hbm, gain_ref), (skip_hbm, skip_ref))]
    late += [load(w_og_hbm, w_og_ref), load(w_down_hbm.at[:, quarter_of(wa)], wd.at[0])]

    sent = []

    def send(src, dst, ssem, rsem, device):
        copy = pltpu.make_async_remote_copy(
            src_ref=src, dst_ref=dst, send_sem=ssem, recv_sem=rsem,
            device_id=device, device_id_type=MESH,
        )
        copy.start()
        sent.append(copy)
        return copy

    def edge_copy(i):
        return pltpu.make_async_remote_copy(
            src_ref=mg.at[0, rl - 16 : rl, :], dst_ref=tail.at[i], send_sem=t_ss.at[i],
            recv_sem=t_rs.at[i], device_id=cross_b[i], device_id_type=MESH,
        )

    def dot(a, b, dims=((1,), (0,))):
        return lax.dot_general(a, b, (dims, ((), ())), preferred_element_type=f32)

    def columns_of(owner):
        return pl.ds(pl.multiple_of(owner * gw, 128), gw)

    far_first = list(range(nb, 0, -1))

    @pl.when(seq == 0)
    def _():
        tail[...] = jnp.zeros_like(tail)
        kb[:, 0:rl, :] = jnp.zeros((nwb, rl, gw), bf16)
        vb[:, 0:rl, :] = jnp.zeros((nwb, rl, gw), bf16)

    for c in first:
        c.wait()
    x = xg[0]
    for i in far_first:
        psend[i - 1] = dot(x, w_in_ref[:, columns_of(group_b[i])]).astype(bf16)
    gp = dot(wg_ref[:, pl.ds(pl.multiple_of(wb * kd, 128), kd)], x, ((1,), (1,)))
    row_id = lax.broadcasted_iota(jnp.int32, gp.shape, 0)
    gsend[...] = jnp.zeros_like(gsend)
    for at, head in ((0, wa), (2, wa + gp.shape[0] // 2)):
        row = jnp.sum(jnp.where(row_id == head, gp, 0.0), axis=0, keepdims=True)
        gsend[at : at + 1, 0:rl] = row[:, 0:rl]
        gsend[at + 1 : at + 2, 0:rs] = row[:, rl:rows]
    pl.semaphore_wait(barrier, len(everyone))
    copies_p, copies_g, copies_x = [], [None] * nb, [None] * nb
    part = rows // nwa
    share = pl.ds(pl.multiple_of(wa * part, 16), part)
    cuts = [(0, rl), (rl, rows)]

    def send_x():
        for i in (2, 1):
            at = i - 1
            copies_x[at] = send(
                xg.at[0, share, :], xg.at[i, share, :], x_ss.at[at], x_rs.at[at], peers_b[at]
            )

    for c, (start, end) in enumerate(cuts):
        if c == 1:
            send_x()
        copies_p.append([None] * nb)
        for i in far_first:
            at, span = i - 1, slice(start, end)
            copies_p[c][at] = send(
                psend.at[at, span, :], precv.at[at, span, :],
                p_ss.at[c * nb + at], p_rs.at[c * nb + at], peers_b[at],
            )
        if c == 0:
            for i in far_first:
                at = i - 1
                copies_g[at] = send(gsend, grecv.at[at], g_ss.at[at], g_rs.at[at], peers_b[at])
    if 1 >= len(cuts):
        send_x()
    mine = pl.ds(pl.multiple_of(seq * half, 16), half)
    copies_d = []
    for j in range(1, nwa):
        copies_d.append(
            send(
                w_down_hbm.at[mine, quarter_of(group_a[j])], wd.at[j, mine, :],
                d_ss.at[j - 1], d_rs.at[j - 1], peers_a[j - 1],
            )
        )
    own_ref[...] = dot(x, w_in_ref[:, columns_of(wb)])

    def halves(a):
        top = a.astype(bf16)
        return top, (a - top.astype(f32)).astype(bf16)

    row_sq = lax.broadcasted_iota(jnp.int32, (gw, gw), 0)
    col_sq = lax.broadcasted_iota(jnp.int32, (gw, gw), 1)
    same = row_sq // 4 == col_sq // 4
    inner = lax.rem(row_sq, 4)
    blocks = wq_ref.shape[2]
    outer = lax.rem(lax.broadcasted_iota(jnp.int32, (4, gw), 1), 4) == lax.broadcasted_iota(
        jnp.int32, (4, gw), 0
    )
    block_at = lax.broadcasted_iota(jnp.int32, (blocks, gw), 0)
    block_of = lax.broadcasted_iota(jnp.int32, (blocks, gw), 1) // 4
    for c in small:
        c.wait()
    for n in range(nwb):
        spread = (block_at == group_b[n] * (gw // 4) + block_of).astype(bf16)
        for kind, ref in enumerate((wq_ref, wk_ref, wv_ref)):
            full = jnp.zeros((gw, gw), f32)
            for i in range(4):
                top, rest = halves(ref[i])
                wide = dot(top, spread) + dot(rest, spread)
                coef = jnp.sum(jnp.where(outer, wide, 0.0), axis=0, keepdims=True)
                full = jnp.where(inner == i, coef, full)
            wsq[kind * nwb + n], wlo[kind * nwb + n] = halves(jnp.where(same, full, 0.0))

    copies_m = []
    copies_xa = []

    def relay_x():
        copies_x[1].wait_recv()
        copies_x[2] = send(
            xg.at[2, share, :], xg.at[3, share, :], x_ss.at[2], x_rs.at[2], peers_b[0]
        )

    def spread_x(i):
        if i != 2:
            copies_x[i - 1].wait_recv()
        src = xg.at[i, share, :]
        for j in range(na):
            at = (i - 1) * na + j
            copies_xa.append(send(src, src, xa_ss.at[at], xa_rs.at[at], peers_a[j]))

    for c, (start, end) in enumerate(cuts):
        if c == 1:
            relay_x()
            spread_x(2)
            spread_x(1)
        span = slice(start, end)
        total = own_ref[span, :]
        for i in far_first:
            copies_p[c][i - 1].wait_recv()
            total = total + precv[i - 1, span, :].astype(f32)
        mg[0, span, :] = total.astype(bf16)
        if start < rl <= end:

            @pl.when(seq == 0)
            def _():
                for i in [0] + far_first:
                    edge_copy(i).start()

        copies_m.append([None] * nb)
        for i in (2, 1):
            at = i - 1
            copies_m[c][at] = send(
                mg.at[0, span, :], mg.at[i, span, :],
                m_ss.at[c * nb + at], m_rs.at[c * nb + at], peers_b[at],
            )

    for c in copies_g:
        c.wait_recv()
    sums = [gsend[...]] + [grecv[i] for i in range(nb)]
    while len(sums) > 1:
        sums = [sums[i] + sums[i + 1] for i in range(0, len(sums), 2)]
    gates = sums[0]
    ig = gates[0:2] + ib_ref[wa]
    fg = gates[2:4] + fb_ref[wa]
    lf = jnp.minimum(fg, 0.0) - jnp.log1p(jnp.exp(-jnp.abs(fg)))
    length = len_ref[0, 0]
    last = seq == nseq - 1

    def block_gates(i_row, f_row, size, limit):
        t = lax.broadcasted_iota(jnp.int32, (size, size), 0)
        s = lax.broadcasted_iota(jnp.int32, (size, size), 1)
        valid = lax.broadcasted_iota(jnp.int32, (1, size), 1) < limit
        f_row = jnp.where(valid, f_row, 0.0)
        b_col = jnp.sum(jnp.where(s <= t, f_row, 0.0), axis=1, keepdims=True)
        b_row = jnp.sum(jnp.where(s == t, b_col, 0.0), axis=0, keepdims=True)
        total = jnp.sum(f_row, axis=1, keepdims=True)
        e_row = jnp.where(valid, total - b_row + i_row, NEG_FILL)
        causal = (s <= t) & (s < limit)
        logw = jnp.where(causal, b_col - b_row + i_row, NEG_FILL)
        return b_col, total, e_row, causal, logw

    def to_col(row):
        size = row.shape[1]
        t = lax.broadcasted_iota(jnp.int32, (size, size), 0)
        s = lax.broadcasted_iota(jnp.int32, (size, size), 1)
        return jnp.sum(jnp.where(s == t, row, 0.0), axis=1, keepdims=True)

    bl, totl, el, causl, logl = block_gates(ig[0:1, 0:rl], lf[0:1, 0:rl], rl, rl)
    bs, tots, es, causs, logs = block_gates(ig[1:2, 0:rs], lf[1:2, 0:rs], rs, length)
    esend[...] = jnp.broadcast_to(el, esend.shape)
    ce = send(esend, erecv, e_ss.at[0], e_rs.at[0], peer)
    pick_row = lax.broadcasted_iota(jnp.int32, (8, rows), 0)
    pick_at = lax.broadcasted_iota(jnp.int32, (8, rows), 1)
    slot_at = length - 3 + pick_row
    target = jnp.where(last, rl - 3 + pick_row, jnp.where(slot_at >= 0, rl + slot_at, -1))
    pick = (pick_at == target).astype(bf16)
    first_keep = jnp.where(seq > 0, 1.0, 0.0)
    scale = (gw * nwb) ** (-0.5)
    copies_f, scores_l, scores_s = [], [], []

    def mixed(a, kind, n):
        top, rest = halves(a)
        wide = wsq[kind * nwb + n]
        return (dot(top, wide) + dot(rest, wide) + dot(top, wlo[kind * nwb + n])).astype(bf16)

    def convolved(ext, n, size):
        taps = cw_ref[:, columns_of(group_b[n])]
        conv = jnp.zeros((size, gw), f32)
        for j in range(4):
            conv = conv + taps[j : j + 1] * ext[5 + j : 5 + j + size, :]
        return conv / (1.0 + jnp.exp(-conv))

    def hand_on(rows_ref, ssem, rsem, n):
        return pltpu.make_async_remote_copy(
            src_ref=rows_ref.at[n, rl : 2 * rl, :], dst_ref=rows_ref.at[n, 0:rl, :],
            send_sem=ssem.at[n], recv_sem=rsem.at[n], device_id=peer, device_id_type=MESH,
        )

    def long_part(n):
        m = mg[n, 0:rl, :]
        v = (dot(m, wsq[2 * nwb + n]) + dot(m, wlo[2 * nwb + n])).astype(bf16)
        vb[n, rl : 2 * rl, :] = v

        @pl.when(seq == 0)
        def _():
            hand_on(vb, v_ss, v_rs, n).start()

        @pl.when(seq > 0)
        def _():
            edge_copy(n).wait_recv()

        ext_l[0:8, :] = tail[n].astype(f32)[8:16] * first_keep
        ext_l[8 : 8 + rl, :] = m.astype(f32)
        a = convolved(ext_l, n, rl)
        if n == 0:
            act[0:rl, :] = a
        k = mixed(a, 1, n)
        kb[n, rl : 2 * rl, :] = k

        @pl.when(seq == 0)
        def _():
            hand_on(kb, k_ss, k_rs, n).start()

        q = mixed(a, 0, n)
        qs[n] = q
        scores_l.append(dot(q, k, ((1,), (1,))))

    def short_part(n):
        m = mg[n, rl:rows, :]
        vb[n, 2 * rl : rl + rows, :] = (
            dot(m, wsq[2 * nwb + n]) + dot(m, wlo[2 * nwb + n])
        ).astype(bf16)
        ext_s[8 : 8 + rs, :] = m.astype(f32)
        a = convolved(ext_s, n, rs)
        if n == 0:
            act[rl:rows, :] = a
        k = mixed(a, 1, n)
        kb[n, 2 * rl : rl + rows, :] = k
        scores_s.append(dot(mixed(a, 0, n), k, ((1,), (1,))))

    ext_s[0:8, :] = jnp.zeros((8, gw), f32)
    long_part(0)
    short_part(0)
    copies_m[0][1].wait_recv()
    copies_m[0][2] = send(
        mg.at[2, 0:rl, :], mg.at[3, 0:rl, :], m_ss.at[2], m_rs.at[2], peers_b[0]
    )
    spread_x(3)
    for j in range(na):
        copies_d[j].wait_recv()
        src = wd.at[j + 1, mine, :]
        copies_f.append(send(src, src, f_ss.at[j], f_rs.at[j], peer))
    copies_m[0][0].wait_recv()
    long_part(1)
    copies_m[1][1].wait_recv()
    copies_m[1][2] = send(
        mg.at[2, rl:rows, :], mg.at[3, rl:rows, :], m_ss.at[nb + 2], m_rs.at[nb + 2], peers_b[0]
    )
    long_part(2)
    copies_m[1][0].wait_recv()
    short_part(1)
    copies_m[0][2].wait_recv()
    long_part(3)
    for c in late:
        c.wait()
    for c in copies_xa:
        c.wait_recv()
    inv = 1.0 / (gw * nwb)
    gain, skip = gain_ref[...], skip_ref[...]
    gate = jnp.zeros((rows, gw), f32)
    for i in range(nwb):
        gate = gate + dot(xg[i], w_og_ref[pl.ds(pl.multiple_of(group_b[i] * kd, 128), kd), :])
    gate = gate / (1.0 + jnp.exp(-gate))
    short_part(2)
    copies_m[1][2].wait_recv()
    short_part(3)
    sl, ss = sum(scores_l[1:], scores_l[0]), sum(scores_s[1:], scores_s[0])

    copies_o = []

    def gated(start, size, hidden, total, square_sum, keep):
        mean = total * inv
        norm = lax.rsqrt(square_sum * inv - mean * mean + EPSILON)
        normed = (hidden - mean) * norm * gain
        out = (normed + skip * act[start : start + size, :]) * gate[start : start + size]
        return (out if keep is None else out * keep).astype(bf16)

    def share_out(start, size):
        span = slice(start, start + size)
        row = len(copies_o)
        copies_o.append([])
        for j in range(1, nwa):
            at = row * na + j - 1
            copies_o[-1].append(
                send(ga.at[0, span, :], ga.at[j, span, :], o_ss.at[at], o_rs.at[at], peers_a[j - 1])
            )

    rmax_s = jnp.max(logs, axis=1, keepdims=True)
    mix_s = ss * scale * jnp.where(causs, jnp.exp(logs - rmax_s), 0.0)
    den_s = jnp.sum(mix_s, axis=1, keepdims=True)
    div_s = jnp.maximum(jnp.abs(den_s), jnp.exp(-rmax_s))
    mix_s = mix_s.astype(bf16)
    sum_s = jnp.zeros((rs, 1), f32)
    sq_s = jnp.zeros((rs, 1), f32)
    for n in range(nwb):
        hh = dot(mix_s, vb[n, 2 * rl : rl + rows, :]) / div_s
        if n == 0:
            own_s = hh
        sum_s += jnp.sum(hh, axis=1, keepdims=True)
        sq_s += jnp.sum(hh * hh, axis=1, keepdims=True)
    ok_s = (lax.broadcasted_iota(jnp.int32, (rs, 1), 0) < length).astype(f32)
    ga[0, rl:rows, :] = gated(rl, rs, own_s, sum_s, sq_s, ok_s)
    share_out(rl, rs)

    ce.wait_recv()
    ep = erecv[0:1, :]
    mp = jnp.max(ep, axis=1, keepdims=True)
    carry_m = jnp.where(seq > 0, mp, NEG_FILL)
    carry_log = bl + carry_m
    rmax_l = jnp.maximum(jnp.max(logl, axis=1, keepdims=True), carry_log)
    mix_l = sl * scale * jnp.where(causl, jnp.exp(logl - rmax_l), 0.0)

    @pl.when(seq > 0)
    def _():
        for n in range(nwb):
            hand_on(vb, v_ss, v_rs, n).wait_recv()
            hand_on(kb, k_ss, k_rs, n).wait_recv()

    sp = jnp.zeros((rl, rl), f32)
    for n in range(nwb):
        sp = sp + dot(qs[n], kb[n, 0:rl, :], ((1,), (1,)))
    mix_p = sp * scale * jnp.exp(ep - mp) * jnp.exp(carry_log - rmax_l)
    den_l = jnp.sum(mix_l, axis=1, keepdims=True) + jnp.sum(mix_p, axis=1, keepdims=True)
    div_l = jnp.maximum(jnp.abs(den_l), jnp.exp(-rmax_l))
    mix = jnp.concatenate([mix_p, mix_l], axis=1).astype(bf16)
    sum_l = jnp.zeros((rl, 1), f32)
    sq_l = jnp.zeros((rl, 1), f32)
    for n in range(nwb):
        hl = dot(mix, vb[n, 0 : 2 * rl, :]) / div_l
        if n == 0:
            hs[...] = hl
        sum_l += jnp.sum(hl, axis=1, keepdims=True)
        sq_l += jnp.sum(hl * hl, axis=1, keepdims=True)
    step = rl // 2
    for start in (0, step):
        span = slice(start, start + step)
        ga[0, span, :] = gated(start, step, hs[span, :], sum_l[span], sq_l[span], None)
        share_out(start, step)

    ml = jnp.max(el, axis=1, keepdims=True)
    shifted = carry_m + totl
    joined = jnp.maximum(shifted, ml)
    ms = jnp.max(es, axis=1, keepdims=True)
    m_ref[...] = jnp.where(last, joined, ms)
    keep_p = jnp.where(last & (seq > 0), 1.0, 0.0)
    keep_l = jnp.where(last, 1.0, 0.0)
    wp = to_col(jnp.exp(ep - mp) * jnp.exp(shifted - joined)) * (keep_p * scale)
    wl = to_col(jnp.exp(el - joined)) * (keep_l * scale)
    ws = to_col(jnp.where(es > 0.5 * NEG_FILL, jnp.exp(es - ms), 0.0)) * ((1.0 - keep_l) * scale)
    weight = jnp.concatenate([wp, wl, ws], axis=0)
    vw = (vb[0].astype(f32) * weight).astype(bf16)
    for n in range(nwb):
        lanes = columns_of(group_b[n])
        keys = kb[n]
        cc_ref[0, :, lanes] = dot(pick, mg[n])[0:3].astype(bf16)
        c_ref[0, 0, :, lanes] = dot(vw, keys, ((0,), (0,)))
        n_ref[0, :, lanes] = jnp.sum(keys.astype(f32) * weight, axis=0, keepdims=True)

    for c in copies_f:
        c.wait_recv()
    ow = zrecv.shape[2]
    copies_z = []
    spans = [(rl, rs), (0, step), (step, step)]

    def piece_of(owner):
        return pl.ds(pl.multiple_of(owner * ow, 128), ow)

    for row, (start, size) in enumerate(spans):
        span = slice(start, start + size)
        y = dot(ga[0, span, :], wd[0])
        for j in range(1, nwa):
            copies_o[row][j - 1].wait_recv()
            y = y + dot(ga[j, span, :], wd[j])
        yacc[span, :] = y
        copies_z.append([])
        for i in range(1, nwb):
            at = row * nb + i - 1
            zsend[i - 1, span, :] = yacc[span, piece_of(group_b[i])].astype(bf16)
            copies_z[-1].append(
                send(
                    zsend.at[i - 1, span, :], zrecv.at[i - 1, span, :],
                    z_ss.at[at], z_rs.at[at], peers_b[i - 1],
                )
            )
    for c in sent[: -3 * nb]:
        c.wait_send()

    @pl.when(seq == 0)
    def _():
        for i in range(nwb):
            edge_copy(i).wait_send()
            hand_on(vb, v_ss, v_rs, i).wait_send()
            hand_on(kb, k_ss, k_rs, i).wait_send()

    for row, (start, size) in enumerate(spans):
        span = slice(start, start + size)
        y = yacc[span, piece_of(wb)]
        for i in range(nb):
            copies_z[row][i].wait_recv()
            y = y + zrecv[i, span, :].astype(f32)
        if start == rl:
            sy_ref[0] = y.astype(bf16)
        else:
            ly_ref[span, :] = y.astype(bf16)
    for c in sent[-3 * nb :]:
        c.wait_send()


def write_kernel(*refs):
    sources, targets, sem = refs[:6], refs[6:12], refs[12]
    copies = [
        pltpu.make_async_copy(src, dst, sem.at[i])
        for i, (src, dst) in enumerate(zip(sources, targets))
    ]
    for c in copies:
        c.start()
    for c in copies:
        c.wait()


def fused_body(
    long_x, short_x, short_len, w_in, w_outgate, w_gates, conv_weight, w_query, w_key, w_value,
    igate_bias, fgate_bias, norm_gain, skip_gain, w_down,
):
    nseq, nwa, nwb = (lax.axis_size(a) for a in ("seq", "wa", "wb"))
    f32, bf16 = jnp.float32, jnp.bfloat16
    rl, kd = long_x.shape
    rs = short_x.shape[1]
    rows = rl + rs
    gw = w_outgate.shape[1]
    hw = w_in.shape[1]
    ow = w_down.shape[1] // (nwa * nwb)
    turned = [w.transpose(1, 2, 0) for w in (w_query, w_key, w_value)]
    vm = pl.BlockSpec(memory_space=pltpu.VMEM)
    hbm = pl.BlockSpec(memory_space=pl.ANY)
    nb, na = nwb - 1, nwa - 1
    dma = pltpu.SemaphoreType.DMA
    shapes = (
        jax.ShapeDtypeStruct((rl, ow), bf16),
        jax.ShapeDtypeStruct((1, rs, ow), bf16),
        jax.ShapeDtypeStruct((1, 1, gw, hw), f32),
        jax.ShapeDtypeStruct((1, 1, hw), f32),
        jax.ShapeDtypeStruct((1, 1), f32),
        jax.ShapeDtypeStruct((1, 3, hw), bf16),
    )
    inputs = (
        short_len[:, None], igate_bias, fgate_bias, long_x, short_x[0], w_in, w_gates.T,
        conv_weight, *turned, norm_gain[None], skip_gain[None], w_outgate, w_down,
    )
    outs = pl.pallas_call(
        functools.partial(mega_kernel, nwa, nwb, nseq),
        out_shape=tuple(pltpu.VMEM(a.shape, a.dtype) for a in shapes),
        in_specs=[pl.BlockSpec(memory_space=pltpu.HBM)] * 15,
        out_specs=(vm,) * 6,
        scratch_shapes=[
            pltpu.VMEM((nwb, rows, kd), bf16),
            pltpu.VMEM((rows, gw), f32),
            pltpu.VMEM((nb, rows, gw), bf16),
            pltpu.VMEM((nb, rows, gw), bf16),
            pltpu.VMEM((8, max(rl, rs)), f32),
            pltpu.VMEM((nb, 8, max(rl, rs)), f32),
            pltpu.VMEM((nwb, rows, gw), bf16),
            pltpu.VMEM((nwb, 16, gw), bf16),
            pltpu.VMEM((8 + rl, gw), f32),
            pltpu.VMEM((8 + rs, gw), f32),
            pltpu.VMEM((rows, gw), f32),
            pltpu.VMEM((nwb, rl, gw), bf16),
            pltpu.VMEM((nwb, rl + rows, gw), bf16),
            pltpu.VMEM((nwb, rl + rows, gw), bf16),
            pltpu.VMEM((8, rl), f32),
            pltpu.VMEM((8, rl), f32),
            pltpu.VMEM((rl, gw), f32),
            pltpu.VMEM((nwa, rows, gw), bf16),
            pltpu.VMEM((nwa, gw, nwb * ow), bf16),
            pltpu.VMEM((rows, nwb * ow), f32),
            pltpu.VMEM((nb, rows, ow), bf16),
            pltpu.VMEM((nb, rows, ow), bf16),
            pltpu.VMEM((3 * nwb, gw, gw), bf16),
            pltpu.VMEM((3 * nwb, gw, gw), bf16),
            pltpu.VMEM(w_in.shape, bf16),
            pltpu.VMEM(w_gates.shape[::-1], bf16),
            pltpu.VMEM(conv_weight.shape, f32),
            pltpu.VMEM(turned[0].shape, f32),
            pltpu.VMEM(turned[1].shape, f32),
            pltpu.VMEM(turned[2].shape, f32),
            pltpu.VMEM((1, gw), f32),
            pltpu.VMEM((1, gw), f32),
            pltpu.VMEM(w_outgate.shape, bf16),
            pltpu.SMEM((1, 1), jnp.int32),
            pltpu.SMEM(igate_bias.shape, f32),
            pltpu.SMEM(fgate_bias.shape, f32),
        ]
        + [dma((3 * nb,))] * 2
        + [dma((nb,))] * 2
        + [dma((3 * nb,))] * 2
        + [dma((nb,))] * 2
        + [dma((nb * na,))] * 2
        + [dma((1,))] * 2
        + [dma((nwb,))] * 6
        + [dma((3 * na,))] * 2
        + [dma((3 * nb,))] * 2
        + [dma((na,))] * 4
        + [dma((15,))],
        compiler_params=pltpu.CompilerParams(
            collective_id=0, has_side_effects=True, vmem_limit_bytes=48 * 2**20
        ),
        name="mlstm_layer",
    )(*(a if a.size == 1 else pltpu.with_memory_space_constraint(a, pltpu.HBM) for a in inputs))
    return pl.pallas_call(
        write_kernel,
        out_shape=shapes,
        in_specs=[vm] * 6,
        out_specs=(pl.BlockSpec(memory_space=pltpu.HBM),) * 6,
        scratch_shapes=[dma((6,))],
        name="write_out",
    )(*(pltpu.with_memory_space_constraint(out, pltpu.VMEM) for out in outs))


def solution(mesh):
    in_specs = (
        P("seq", "wb"),
        P("seq", None, "wb"),
        P("seq"),
        P("wb", "wa"),
        P(None, ("wa", "wb")),
        P(),
        P(None, "wa"),
        P("wa", None, None),
        P("wa", None, None),
        P("wa", None, None),
        P(),
        P(),
        P(("wa", "wb")),
        P(("wa", "wb")),
        P(("wa", "wb"), None),
    )
    out_specs = (
        P("seq", ("wa", "wb")),
        P("seq", None, ("wa", "wb")),
        P("seq", "wa", "wb", None),
        P("seq", "wa", None),
        P("seq", "wa"),
        P("seq", None, "wa"),
    )
    fused = mesh.shape["seq"] == 2 and mesh.shape["wa"] == 4 and mesh.shape["wb"] == 4
    layer = fused_body if fused else body
    return jax.shard_map(layer, mesh=mesh, in_specs=in_specs, out_specs=out_specs, check_vma=False)
```

```python
import functools

import jax
import jax.numpy as jnp
from jax import lax
from jax.experimental import pallas as pl
from jax.experimental.pallas import tpu as pltpu
from jax.sharding import PartitionSpec as P

MESH = pl.DeviceIdType.MESH
NEG_FILL = -1e30
EPSILON = 1e-05
exact_mode = lax.Precision.HIGHEST


def passed_along(array, axis, by):
    devices = lax.axis_size(axis)
    pairs = [(i, i + by) for i in range(devices) if 0 <= i + by < devices]
    return lax.ppermute(array, axis, pairs)


def entering(array, axis, combine, identity):
    devices, index = (lax.axis_size(axis), lax.axis_index(axis))
    everything = jax.tree.map(lambda part: lax.all_gather(part, axis), array)
    start = jax.tree.map(
        lambda part, zero: jnp.broadcast_to(jnp.asarray(zero, part.dtype), part.shape),
        array,
        identity,
    )

    def turn(k, before):
        reached = k < index
        new = combine(before, jax.tree.map(lambda part: part[k], everything))
        return jax.tree.map(lambda a, b: jnp.where(reached, a, b), new, before)

    return lax.fori_loop(0, devices, turn, start)


def block_diagonal(inputs, blocks):
    row_count = inputs.shape[0]
    grouped = inputs.reshape(row_count, blocks.shape[0], blocks.shape[1])
    combined = jnp.einsum("rni,nio->rno", grouped, blocks, precision=exact_mode)
    return combined.reshape(row_count, -1)


def causal_conv(mlstm_in, previous, conv_weight):
    extended = jnp.concatenate([previous.astype(jnp.float32), mlstm_in.astype(jnp.float32)], axis=0)
    row_count = mlstm_in.shape[0]
    running = jnp.zeros(mlstm_in.shape, jnp.float32)
    for offset in range(conv_weight.shape[0]):
        running = running + conv_weight[offset] * extended[offset : offset + row_count]
    return running


def running_sum(row):
    at = jnp.arange(row.shape[0])
    return jnp.sum(jnp.where(at[:, None] >= at[None, :], row[None, :], 0.0), axis=1)


def block_hidden(queries, key_rows, value_rows, in_gate, log_forget, is_valid, carried):
    scaling = key_rows.shape[1] ** (-0.5)
    row_count = queries.shape[0]
    forget_sum = running_sum(jnp.where(is_valid, log_forget, 0.0))
    positions = jnp.arange(row_count)
    causal = (positions[:, None] >= positions[None, :]) & is_valid[None, :]
    log_weight = jnp.where(
        causal, forget_sum[:, None] - forget_sum[None, :] + in_gate[None, :], NEG_FILL
    )
    row_max = jnp.max(log_weight, axis=1)
    if carried is not None:
        carry_log = forget_sum + carried[2]
        row_max = jnp.maximum(row_max, carry_log)
    weights = jnp.where(causal, jnp.exp(log_weight - row_max[:, None]), 0.0)
    scores = jnp.dot(queries, key_rows.T, preferred_element_type=jnp.float32) * scaling
    mixing = scores * weights
    denominator = jnp.sum(mixing, axis=1)
    numerator = jnp.dot(mixing.astype(jnp.bfloat16), value_rows, preferred_element_type=jnp.float32)
    if carried is not None:
        carry_weight = jnp.exp(carry_log - row_max)
        query_wide = queries.astype(jnp.float32)
        numerator = numerator + carry_weight[:, None] * jnp.dot(
            query_wide, carried[0].T, precision=exact_mode
        )
        denominator = denominator + carry_weight * jnp.dot(
            query_wide, carried[1], precision=exact_mode
        )
    return numerator / jnp.maximum(jnp.abs(denominator), jnp.exp(-row_max))[:, None]


def block_state(key_rows, value_rows, in_gate, log_forget, is_valid):
    scaling = key_rows.shape[1] ** (-0.5)
    forget_sum = running_sum(jnp.where(is_valid, log_forget, 0.0))
    forget_total = forget_sum[-1]
    end_log = jnp.where(is_valid, forget_total - forget_sum + in_gate, NEG_FILL)
    end_max = jnp.max(end_log)
    end_weight = jnp.where(is_valid, jnp.exp(end_log - end_max), 0.0)
    key_wide = key_rows.astype(jnp.float32) * scaling
    matrix_state = jnp.dot(
        (value_rows.astype(jnp.float32) * end_weight[:, None]).T, key_wide, precision=exact_mode
    )
    normalizer = jnp.dot(end_weight, key_wide, precision=exact_mode)
    return (matrix_state, normalizer, end_max, forget_total)


def merge_states(earlier, latter):
    state_a, normal_a, max_a, forget_a = earlier
    state_b, normal_b, max_b, forget_b = latter
    shifted = max_a + forget_b
    joined = jnp.maximum(shifted, max_b)
    weight_a = jnp.exp(shifted - joined)
    weight_b = jnp.exp(max_b - joined)
    return (
        weight_a * state_a + weight_b * state_b,
        weight_a * normal_a + weight_b * normal_b,
        joined,
        forget_a + forget_b,
    )


def edge_rows(rows, length, rim):
    select = (jnp.arange(rows.shape[0])[None, :] == length - rim + jnp.arange(rim)[:, None]).astype(
        jnp.float32
    )
    return jnp.dot(select, rows.astype(jnp.float32), precision=exact_mode).astype(jnp.bfloat16)


def body(
    long_x,
    short_x,
    short_len,
    w_in,
    w_outgate,
    w_gates,
    conv_weight,
    w_query,
    w_key,
    w_value,
    igate_bias,
    fgate_bias,
    norm_gain,
    skip_gain,
    w_down,
):
    long_rows = long_x.shape[0]
    slot_rows = short_x.shape[1]
    heads = igate_bias.shape[0]
    head_width = w_in.shape[1]
    value_width = w_outgate.shape[1]
    block_size = w_value.shape[1]
    rim = conv_weight.shape[0] - 1
    head_index = lax.axis_index("wa")
    column_index = lax.axis_index("wb")
    local_rows = jnp.concatenate([long_x, short_x[0]], axis=0)
    gathered = lax.all_gather(local_rows, "wb", axis=1, tiled=True)
    mlstm_full = jnp.dot(
        gathered, lax.all_gather(w_in, "wb", axis=0, tiled=True), preferred_element_type=jnp.float32
    )
    mlstm_in = mlstm_full.astype(jnp.bfloat16)
    gate_out = jnp.dot(gathered, w_outgate, preferred_element_type=jnp.float32)
    gate_pre = jnp.dot(gathered, w_gates, preferred_element_type=jnp.float32)
    pick = (jnp.arange(heads) == head_index).astype(jnp.float32)
    in_gate = jnp.sum(gate_pre[:, :heads] * pick, axis=1) + jnp.sum(igate_bias * pick)
    log_forget = jax.nn.log_sigmoid(
        jnp.sum(gate_pre[:, heads:] * pick, axis=1) + jnp.sum(fgate_bias * pick)
    )
    long_in = mlstm_in[:long_rows]
    slot_in = mlstm_in[long_rows:]
    previous = passed_along(long_in[long_rows - rim :], "seq", 1)
    long_conv = causal_conv(long_in, previous, conv_weight)
    slot_conv = causal_conv(slot_in, jnp.zeros((rim, head_width), jnp.bfloat16), conv_weight)
    activated = jax.nn.silu(jnp.concatenate([long_conv, slot_conv], axis=0))
    queries = block_diagonal(activated, w_query).astype(jnp.bfloat16)
    key_rows = block_diagonal(activated, w_key).astype(jnp.bfloat16)
    value_blocks = lax.dynamic_slice_in_dim(
        w_value, column_index * (value_width // block_size), value_width // block_size, 0
    )
    value_cols = lax.dynamic_slice_in_dim(mlstm_in, column_index * value_width, value_width, 1)
    value_rows = block_diagonal(value_cols.astype(jnp.float32), value_blocks).astype(jnp.bfloat16)
    long_valid = jnp.ones((long_rows,), bool)
    local_state = block_state(
        key_rows[:long_rows],
        value_rows[:long_rows],
        in_gate[:long_rows],
        log_forget[:long_rows],
        long_valid,
    )
    local_tuple = (
        local_state[0],
        local_state[1],
        jnp.reshape(local_state[2], (1,)),
        jnp.reshape(local_state[3], (1,)),
    )
    identity = (
        jnp.zeros_like(local_state[0]),
        jnp.zeros_like(local_state[1]),
        jnp.full((1,), NEG_FILL, jnp.float32),
        jnp.zeros((1,), jnp.float32),
    )
    prefix = entering(local_tuple, "seq", merge_states, identity)
    carried = (prefix[0], prefix[1], prefix[2][0])
    long_hidden = block_hidden(
        queries[:long_rows],
        key_rows[:long_rows],
        value_rows[:long_rows],
        in_gate[:long_rows],
        log_forget[:long_rows],
        long_valid,
        carried,
    )
    final = merge_states(prefix, local_tuple)
    slot_valid = jnp.arange(slot_rows) < short_len[0]
    slot_hidden = block_hidden(
        queries[long_rows:],
        key_rows[long_rows:],
        value_rows[long_rows:],
        in_gate[long_rows:],
        log_forget[long_rows:],
        slot_valid,
        None,
    )
    slot_state = block_state(
        key_rows[long_rows:],
        value_rows[long_rows:],
        in_gate[long_rows:],
        log_forget[long_rows:],
        slot_valid,
    )
    hidden = jnp.concatenate([long_hidden, slot_hidden], axis=0)
    sums = lax.psum((jnp.sum(hidden, axis=1), jnp.sum(hidden * hidden, axis=1)), "wb")
    mean = sums[0] / head_width
    square = sums[1] / head_width
    normed = (
        (hidden - mean[:, None]) * lax.rsqrt(square - mean * mean + EPSILON)[:, None] * norm_gain
    )
    act_cols = lax.dynamic_slice_in_dim(activated, column_index * value_width, value_width, 1)
    row_valid = jnp.concatenate([long_valid, slot_valid], axis=0).astype(jnp.float32)
    gated = ((normed + skip_gain * act_cols) * jax.nn.silu(gate_out) * row_valid[:, None]).astype(
        jnp.bfloat16
    )
    terms = jnp.dot(gated, w_down, preferred_element_type=jnp.float32)
    mixed = lax.psum_scatter(
        terms.astype(jnp.bfloat16), ("wa", "wb"), scatter_dimension=1, tiled=True
    )
    long_y = mixed[:long_rows]
    short_y = mixed[long_rows:][None]
    slot_edge = edge_rows(slot_in, short_len[0], rim)
    is_last = lax.axis_index("seq") == lax.axis_size("seq") - 1
    cache_c = jnp.where(is_last, final[0], slot_state[0])[None, None]
    cache_n = jnp.where(is_last, final[1], slot_state[1])[None, None]
    cache_m = jnp.reshape(jnp.where(is_last, final[2][0], slot_state[2]), (1, 1))
    cache_conv = jnp.where(is_last, long_in[long_rows - rim :], slot_edge)[None]
    return (long_y, short_y, cache_c, cache_n, cache_m, cache_conv)


def flipped(index, mask):
    out, bit = index, 1
    while bit <= mask:
        if mask & bit:
            out = out + bit - 2 * bit * lax.rem(lax.div(index, bit), 2)
        bit *= 2
    return out


def mega_kernel(
    nwa, nwb, nseq,
    len_hbm, ib_hbm, fb_hbm,
    lx_ref, sx_ref, w_in_hbm, wg_hbm, cw_hbm, wq_hbm, wk_hbm, wv_hbm, gain_hbm, skip_hbm, w_og_hbm, w_down_hbm,
    ly_ref, sy_ref, c_ref, n_ref, m_ref, cc_ref,
    xg, own_ref, psend, precv, gsend, grecv, mg, tail, ext_l, ext_s, act, qs, kb, vb, esend, erecv, hs,
    ga, wd, yacc, zsend, zrecv, wsq, wlo,
    w_in_ref, wg_ref, cw_ref, wq_ref, wk_ref, wv_ref, gain_ref, skip_ref, w_og_ref,
    len_ref, ib_ref, fb_ref,
    p_ss, p_rs, g_ss, g_rs, m_ss, m_rs, x_ss, x_rs, xa_ss, xa_rs, e_ss, e_rs,
    t_ss, t_rs, k_ss, k_rs, v_ss, v_rs, o_ss, o_rs, z_ss, z_rs, d_ss, d_rs, f_ss, f_rs, w_sem,
):
    f32, bf16 = jnp.float32, jnp.bfloat16
    seq, wa, wb = lax.axis_index("seq"), lax.axis_index("wa"), lax.axis_index("wb")
    rl, rs = lx_ref.shape[0], sx_ref.shape[0]
    rows = rl + rs
    kd = lx_ref.shape[1]
    gw = mg.shape[2]
    na, nb = nwa - 1, nwb - 1
    other = lax.rem(seq + 1, nseq)
    group_a = [flipped(wa, j) for j in range(nwa)]
    group_b = [flipped(wb, i) for i in range(nwb)]
    barrier = pltpu.get_barrier_semaphore()
    peers_a = [(seq, group_a[j], wb) for j in range(1, nwa)]
    peers_b = [(seq, wa, group_b[i]) for i in range(1, nwb)]
    cross_b = [(other, wa, group_b[i]) for i in range(nwb)]
    peer = cross_b[0]
    everyone = peers_a + peers_b + cross_b
    for p in everyone:
        pl.semaphore_signal(barrier, inc=1, device_id=p, device_id_type=MESH)
    loads = []

    def load(src, dst):
        copy = pltpu.make_async_copy(src, dst, w_sem.at[len(loads)])
        copy.start()
        loads.append(copy)
        return copy

    half = wd.shape[1] // 2
    quarter = wd.shape[2]

    def quarter_of(owner):
        return pl.ds(pl.multiple_of(owner * quarter, 128), quarter)

    first = [load(lx_ref, xg.at[0, 0:rl, :]), load(sx_ref, xg.at[0, rl:rows, :])]
    first += [load(wg_hbm, wg_ref), load(w_in_hbm, w_in_ref)]
    small = [(wq_hbm, wq_ref), (wk_hbm, wk_ref), (wv_hbm, wv_ref), (cw_hbm, cw_ref)]
    small += [(len_hbm, len_ref), (ib_hbm, ib_ref), (fb_hbm, fb_ref)]
    small = [load(src, dst) for src, dst in small]
    late = [load(src, dst) for src, dst in ((gain_hbm, gain_ref), (skip_hbm, skip_ref))]
    late += [load(w_og_hbm, w_og_ref), load(w_down_hbm.at[:, quarter_of(wa)], wd.at[0])]

    sent = []

    def send(src, dst, ssem, rsem, device):
        copy = pltpu.make_async_remote_copy(
            src_ref=src, dst_ref=dst, send_sem=ssem, recv_sem=rsem,
            device_id=device, device_id_type=MESH,
        )
        copy.start()
        sent.append(copy)
        return copy

    def edge_copy(i):
        return pltpu.make_async_remote_copy(
            src_ref=mg.at[0, rl - 16 : rl, :], dst_ref=tail.at[i], send_sem=t_ss.at[i],
            recv_sem=t_rs.at[i], device_id=cross_b[i], device_id_type=MESH,
        )

    def dot(a, b, dims=((1,), (0,))):
        return lax.dot_general(a, b, (dims, ((), ())), preferred_element_type=f32)

    def columns_of(owner):
        return pl.ds(pl.multiple_of(owner * gw, 128), gw)

    far_first = list(range(nb, 0, -1))

    @pl.when(seq == 0)
    def _():
        tail[...] = jnp.zeros_like(tail)
        kb[:, 0:rl, :] = jnp.zeros((nwb, rl, gw), bf16)
        vb[:, 0:rl, :] = jnp.zeros((nwb, rl, gw), bf16)

    for c in first:
        c.wait()
    x = xg[0]
    for i in far_first:
        psend[i - 1] = dot(x, w_in_ref[:, columns_of(group_b[i])]).astype(bf16)
    gp = dot(wg_ref[:, pl.ds(pl.multiple_of(wb * kd, 128), kd)], x, ((1,), (1,)))
    row_id = lax.broadcasted_iota(jnp.int32, gp.shape, 0)
    gsend[...] = jnp.zeros_like(gsend)
    for at, head in ((0, wa), (2, wa + gp.shape[0] // 2)):
        row = jnp.sum(jnp.where(row_id == head, gp, 0.0), axis=0, keepdims=True)
        gsend[at : at + 1, 0:rl] = row[:, 0:rl]
        gsend[at + 1 : at + 2, 0:rs] = row[:, rl:rows]
    pl.semaphore_wait(barrier, len(everyone))
    copies_p, copies_g, copies_x = [], [None] * nb, [None] * nb
    part = rows // nwa
    share = pl.ds(pl.multiple_of(wa * part, 16), part)
    cuts = [(0, rl), (rl, rows)]

    def send_x():
        for i in (2, 1):
            at = i - 1
            copies_x[at] = send(
                xg.at[0, share, :], xg.at[i, share, :], x_ss.at[at], x_rs.at[at], peers_b[at]
            )

    for c, (start, end) in enumerate(cuts):
        if c == 1:
            send_x()
        copies_p.append([None] * nb)
        for i in far_first:
            at, span = i - 1, slice(start, end)
            copies_p[c][at] = send(
                psend.at[at, span, :], precv.at[at, span, :],
                p_ss.at[c * nb + at], p_rs.at[c * nb + at], peers_b[at],
            )
        if c == 0:
            for i in far_first:
                at = i - 1
                copies_g[at] = send(gsend, grecv.at[at], g_ss.at[at], g_rs.at[at], peers_b[at])
    if 1 >= len(cuts):
        send_x()
    mine = pl.ds(pl.multiple_of(seq * half, 16), half)
    copies_d = []
    for j in range(1, nwa):
        copies_d.append(
            send(
                w_down_hbm.at[mine, quarter_of(group_a[j])], wd.at[j, mine, :],
                d_ss.at[j - 1], d_rs.at[j - 1], peers_a[j - 1],
            )
        )
    own_ref[...] = dot(x, w_in_ref[:, columns_of(wb)])

    def halves(a):
        top = a.astype(bf16)
        return top, (a - top.astype(f32)).astype(bf16)

    row_sq = lax.broadcasted_iota(jnp.int32, (gw, gw), 0)
    col_sq = lax.broadcasted_iota(jnp.int32, (gw, gw), 1)
    same = row_sq // 4 == col_sq // 4
    inner = lax.rem(row_sq, 4)
    blocks = wq_ref.shape[2]
    outer = lax.rem(lax.broadcasted_iota(jnp.int32, (4, gw), 1), 4) == lax.broadcasted_iota(
        jnp.int32, (4, gw), 0
    )
    block_at = lax.broadcasted_iota(jnp.int32, (blocks, gw), 0)
    block_of = lax.broadcasted_iota(jnp.int32, (blocks, gw), 1) // 4
    for c in small:
        c.wait()
    for n in range(nwb):
        spread = (block_at == group_b[n] * (gw // 4) + block_of).astype(bf16)
        for kind, ref in enumerate((wq_ref, wk_ref, wv_ref)):
            full = jnp.zeros((gw, gw), f32)
            for i in range(4):
                top, rest = halves(ref[i])
                wide = dot(top, spread) + dot(rest, spread)
                coef = jnp.sum(jnp.where(outer, wide, 0.0), axis=0, keepdims=True)
                full = jnp.where(inner == i, coef, full)
            wsq[kind * nwb + n], wlo[kind * nwb + n] = halves(jnp.where(same, full, 0.0))

    copies_m = []
    copies_xa = []

    def relay_x():
        copies_x[1].wait_recv()
        copies_x[2] = send(
            xg.at[2, share, :], xg.at[3, share, :], x_ss.at[2], x_rs.at[2], peers_b[0]
        )

    def spread_x(i):
        if i != 2:
            copies_x[i - 1].wait_recv()
        src = xg.at[i, share, :]
        for j in range(na - 1, -1, -1):
            at = (i - 1) * na + j
            copies_xa.append(send(src, src, xa_ss.at[at], xa_rs.at[at], peers_a[j]))

    for c, (start, end) in enumerate(cuts):
        if c == 1:
            relay_x()
            spread_x(2)
            spread_x(1)
        span = slice(start, end)
        total = own_ref[span, :]
        for i in far_first:
            copies_p[c][i - 1].wait_recv()
            total = total + precv[i - 1, span, :].astype(f32)
        mg[0, span, :] = total.astype(bf16)
        if start < rl <= end:

            @pl.when(seq == 0)
            def _():
                for i in [0] + far_first:
                    edge_copy(i).start()

        copies_m.append([None] * nb)
        for i in (2, 1):
            at = i - 1
            copies_m[c][at] = send(
                mg.at[0, span, :], mg.at[i, span, :],
                m_ss.at[c * nb + at], m_rs.at[c * nb + at], peers_b[at],
            )

    for c in copies_g:
        c.wait_recv()
    sums = [gsend[...]] + [grecv[i] for i in range(nb)]
    while len(sums) > 1:
        sums = [sums[i] + sums[i + 1] for i in range(0, len(sums), 2)]
    gates = sums[0]
    ig = gates[0:2] + ib_ref[wa]
    fg = gates[2:4] + fb_ref[wa]
    lf = jnp.minimum(fg, 0.0) - jnp.log1p(jnp.exp(-jnp.abs(fg)))
    length = len_ref[0, 0]
    last = seq == nseq - 1

    def block_gates(i_row, f_row, size, limit):
        t = lax.broadcasted_iota(jnp.int32, (size, size), 0)
        s = lax.broadcasted_iota(jnp.int32, (size, size), 1)
        valid = lax.broadcasted_iota(jnp.int32, (1, size), 1) < limit
        f_row = jnp.where(valid, f_row, 0.0)
        b_col = jnp.sum(jnp.where(s <= t, f_row, 0.0), axis=1, keepdims=True)
        b_row = jnp.sum(jnp.where(s == t, b_col, 0.0), axis=0, keepdims=True)
        total = jnp.sum(f_row, axis=1, keepdims=True)
        e_row = jnp.where(valid, total - b_row + i_row, NEG_FILL)
        causal = (s <= t) & (s < limit)
        logw = jnp.where(causal, b_col - b_row + i_row, NEG_FILL)
        return b_col, total, e_row, causal, logw

    def to_col(row):
        size = row.shape[1]
        t = lax.broadcasted_iota(jnp.int32, (size, size), 0)
        s = lax.broadcasted_iota(jnp.int32, (size, size), 1)
        return jnp.sum(jnp.where(s == t, row, 0.0), axis=1, keepdims=True)

    bl, totl, el, causl, logl = block_gates(ig[0:1, 0:rl], lf[0:1, 0:rl], rl, rl)
    bs, tots, es, causs, logs = block_gates(ig[1:2, 0:rs], lf[1:2, 0:rs], rs, length)
    esend[...] = jnp.broadcast_to(el, esend.shape)
    ce = send(esend, erecv, e_ss.at[0], e_rs.at[0], peer)
    pick_row = lax.broadcasted_iota(jnp.int32, (8, rows), 0)
    pick_at = lax.broadcasted_iota(jnp.int32, (8, rows), 1)
    slot_at = length - 3 + pick_row
    target = jnp.where(last, rl - 3 + pick_row, jnp.where(slot_at >= 0, rl + slot_at, -1))
    pick = (pick_at == target).astype(bf16)
    first_keep = jnp.where(seq > 0, 1.0, 0.0)
    scale = (gw * nwb) ** (-0.5)
    copies_f, scores_l, scores_s = [], [], []

    def mixed(a, kind, n):
        top, rest = halves(a)
        wide = wsq[kind * nwb + n]
        return (dot(top, wide) + dot(rest, wide) + dot(top, wlo[kind * nwb + n])).astype(bf16)

    def convolved(ext, n, size):
        taps = cw_ref[:, columns_of(group_b[n])]
        conv = jnp.zeros((size, gw), f32)
        for j in range(4):
            conv = conv + taps[j : j + 1] * ext[5 + j : 5 + j + size, :]
        return conv / (1.0 + jnp.exp(-conv))

    def hand_on(rows_ref, ssem, rsem, n):
        return pltpu.make_async_remote_copy(
            src_ref=rows_ref.at[n, rl : 2 * rl, :], dst_ref=rows_ref.at[n, 0:rl, :],
            send_sem=ssem.at[n], recv_sem=rsem.at[n], device_id=peer, device_id_type=MESH,
        )

    def long_part(n):
        m = mg[n, 0:rl, :]
        v = (dot(m, wsq[2 * nwb + n]) + dot(m, wlo[2 * nwb + n])).astype(bf16)
        vb[n, rl : 2 * rl, :] = v

        @pl.when(seq == 0)
        def _():
            hand_on(vb, v_ss, v_rs, n).start()

        @pl.when(seq > 0)
        def _():
            edge_copy(n).wait_recv()

        ext_l[0:8, :] = tail[n].astype(f32)[8:16] * first_keep
        ext_l[8 : 8 + rl, :] = m.astype(f32)
        a = convolved(ext_l, n, rl)
        if n == 0:
            act[0:rl, :] = a
        k = mixed(a, 1, n)
        kb[n, rl : 2 * rl, :] = k

        @pl.when(seq == 0)
        def _():
            hand_on(kb, k_ss, k_rs, n).start()

        q = mixed(a, 0, n)
        qs[n] = q
        scores_l.append(dot(q, k, ((1,), (1,))))

    def short_part(n):
        m = mg[n, rl:rows, :]
        vb[n, 2 * rl : rl + rows, :] = (
            dot(m, wsq[2 * nwb + n]) + dot(m, wlo[2 * nwb + n])
        ).astype(bf16)
        ext_s[8 : 8 + rs, :] = m.astype(f32)
        a = convolved(ext_s, n, rs)
        if n == 0:
            act[rl:rows, :] = a
        k = mixed(a, 1, n)
        kb[n, 2 * rl : rl + rows, :] = k
        scores_s.append(dot(mixed(a, 0, n), k, ((1,), (1,))))

    ext_s[0:8, :] = jnp.zeros((8, gw), f32)
    long_part(0)
    short_part(0)
    copies_m[0][1].wait_recv()
    copies_m[0][2] = send(
        mg.at[2, 0:rl, :], mg.at[3, 0:rl, :], m_ss.at[2], m_rs.at[2], peers_b[0]
    )
    spread_x(3)
    for j in range(na):
        copies_d[j].wait_recv()
        src = wd.at[j + 1, mine, :]
        copies_f.append(send(src, src, f_ss.at[j], f_rs.at[j], peer))
    copies_m[0][0].wait_recv()
    long_part(1)
    copies_m[1][1].wait_recv()
    copies_m[1][2] = send(
        mg.at[2, rl:rows, :], mg.at[3, rl:rows, :], m_ss.at[nb + 2], m_rs.at[nb + 2], peers_b[0]
    )
    long_part(2)
    copies_m[1][0].wait_recv()
    short_part(1)
    copies_m[0][2].wait_recv()
    long_part(3)
    for c in late:
        c.wait()
    for c in copies_xa:
        c.wait_recv()
    inv = 1.0 / (gw * nwb)
    gain, skip = gain_ref[...], skip_ref[...]
    gate = jnp.zeros((rows, gw), f32)
    for i in range(nwb):
        gate = gate + dot(xg[i], w_og_ref[pl.ds(pl.multiple_of(group_b[i] * kd, 128), kd), :])
    gate = gate / (1.0 + jnp.exp(-gate))
    short_part(2)
    copies_m[1][2].wait_recv()
    short_part(3)
    sl, ss = sum(scores_l[1:], scores_l[0]), sum(scores_s[1:], scores_s[0])

    copies_o = []

    def gated(start, size, hidden, total, square_sum, keep):
        mean = total * inv
        norm = lax.rsqrt(square_sum * inv - mean * mean + EPSILON)
        normed = (hidden - mean) * norm * gain
        out = (normed + skip * act[start : start + size, :]) * gate[start : start + size]
        return (out if keep is None else out * keep).astype(bf16)

    def share_out(start, size):
        span = slice(start, start + size)
        row = len(copies_o)
        copies_o.append([])
        for j in range(na, 0, -1):
            at = row * na + j - 1
            copies_o[-1].insert(
                0,
                send(ga.at[0, span, :], ga.at[j, span, :], o_ss.at[at], o_rs.at[at], peers_a[j - 1])
            )

    rmax_s = jnp.max(logs, axis=1, keepdims=True)
    mix_s = ss * scale * jnp.where(causs, jnp.exp(logs - rmax_s), 0.0)
    den_s = jnp.sum(mix_s, axis=1, keepdims=True)
    div_s = jnp.maximum(jnp.abs(den_s), jnp.exp(-rmax_s))
    mix_s = mix_s.astype(bf16)
    sum_s = jnp.zeros((rs, 1), f32)
    sq_s = jnp.zeros((rs, 1), f32)
    for n in range(nwb):
        hh = dot(mix_s, vb[n, 2 * rl : rl + rows, :]) / div_s
        if n == 0:
            own_s = hh
        sum_s += jnp.sum(hh, axis=1, keepdims=True)
        sq_s += jnp.sum(hh * hh, axis=1, keepdims=True)
    ok_s = (lax.broadcasted_iota(jnp.int32, (rs, 1), 0) < length).astype(f32)
    ga[0, rl:rows, :] = gated(rl, rs, own_s, sum_s, sq_s, ok_s)
    share_out(rl, rs)

    ce.wait_recv()
    ep = erecv[0:1, :]
    mp = jnp.max(ep, axis=1, keepdims=True)
    carry_m = jnp.where(seq > 0, mp, NEG_FILL)
    carry_log = bl + carry_m
    rmax_l = jnp.maximum(jnp.max(logl, axis=1, keepdims=True), carry_log)
    mix_l = sl * scale * jnp.where(causl, jnp.exp(logl - rmax_l), 0.0)

    @pl.when(seq > 0)
    def _():
        for n in range(nwb):
            hand_on(vb, v_ss, v_rs, n).wait_recv()
            hand_on(kb, k_ss, k_rs, n).wait_recv()

    sp = jnp.zeros((rl, rl), f32)
    for n in range(nwb):
        sp = sp + dot(qs[n], kb[n, 0:rl, :], ((1,), (1,)))
    mix_p = sp * scale * jnp.exp(ep - mp) * jnp.exp(carry_log - rmax_l)
    den_l = jnp.sum(mix_l, axis=1, keepdims=True) + jnp.sum(mix_p, axis=1, keepdims=True)
    div_l = jnp.maximum(jnp.abs(den_l), jnp.exp(-rmax_l))
    mix = jnp.concatenate([mix_p, mix_l], axis=1).astype(bf16)
    sum_l = jnp.zeros((rl, 1), f32)
    sq_l = jnp.zeros((rl, 1), f32)
    for n in range(nwb):
        hl = dot(mix, vb[n, 0 : 2 * rl, :]) / div_l
        if n == 0:
            hs[...] = hl
        sum_l += jnp.sum(hl, axis=1, keepdims=True)
        sq_l += jnp.sum(hl * hl, axis=1, keepdims=True)
    step = rl // 2
    for start in (0, step):
        span = slice(start, start + step)
        ga[0, span, :] = gated(start, step, hs[span, :], sum_l[span], sq_l[span], None)
        share_out(start, step)

    ml = jnp.max(el, axis=1, keepdims=True)
    shifted = carry_m + totl
    joined = jnp.maximum(shifted, ml)
    ms = jnp.max(es, axis=1, keepdims=True)
    m_ref[...] = jnp.where(last, joined, ms)
    keep_p = jnp.where(last & (seq > 0), 1.0, 0.0)
    keep_l = jnp.where(last, 1.0, 0.0)
    wp = to_col(jnp.exp(ep - mp) * jnp.exp(shifted - joined)) * (keep_p * scale)
    wl = to_col(jnp.exp(el - joined)) * (keep_l * scale)
    ws = to_col(jnp.where(es > 0.5 * NEG_FILL, jnp.exp(es - ms), 0.0)) * ((1.0 - keep_l) * scale)
    weight = jnp.concatenate([wp, wl, ws], axis=0)
    vw = (vb[0].astype(f32) * weight).astype(bf16)
    for n in range(nwb):
        lanes = columns_of(group_b[n])
        keys = kb[n]
        cc_ref[0, :, lanes] = dot(pick, mg[n])[0:3].astype(bf16)
        c_ref[0, 0, :, lanes] = dot(vw, keys, ((0,), (0,)))
        n_ref[0, :, lanes] = jnp.sum(keys.astype(f32) * weight, axis=0, keepdims=True)

    for c in copies_f:
        c.wait_recv()
    ow = zrecv.shape[2]
    copies_z = []
    spans = [(rl, rs), (0, step), (step, step)]

    def piece_of(owner):
        return pl.ds(pl.multiple_of(owner * ow, 128), ow)

    for row, (start, size) in enumerate(spans):
        span = slice(start, start + size)
        y = dot(ga[0, span, :], wd[0])
        for j in range(1, nwa):
            copies_o[row][j - 1].wait_recv()
            y = y + dot(ga[j, span, :], wd[j])
        yacc[span, :] = y
        copies_z.append([])
        for i in far_first:
            at = row * nb + i - 1
            zsend[i - 1, span, :] = yacc[span, piece_of(group_b[i])].astype(bf16)
            copies_z[-1].insert(
                0,
                send(
                    zsend.at[i - 1, span, :], zrecv.at[i - 1, span, :],
                    z_ss.at[at], z_rs.at[at], peers_b[i - 1],
                ),
            )
    for c in sent[: -3 * nb]:
        c.wait_send()

    @pl.when(seq == 0)
    def _():
        for i in range(nwb):
            edge_copy(i).wait_send()
            hand_on(vb, v_ss, v_rs, i).wait_send()
            hand_on(kb, k_ss, k_rs, i).wait_send()

    for row, (start, size) in enumerate(spans):
        span = slice(start, start + size)
        y = yacc[span, piece_of(wb)]
        for i in range(nb):
            copies_z[row][i].wait_recv()
            y = y + zrecv[i, span, :].astype(f32)
        if start == rl:
            sy_ref[0] = y.astype(bf16)
        else:
            ly_ref[span, :] = y.astype(bf16)
    for c in sent[-3 * nb :]:
        c.wait_send()


def write_kernel(*refs):
    sources, targets, sem = refs[:6], refs[6:12], refs[12]
    copies = [
        pltpu.make_async_copy(src, dst, sem.at[i])
        for i, (src, dst) in enumerate(zip(sources, targets))
    ]
    for c in copies:
        c.start()
    for c in copies:
        c.wait()


def fused_body(
    long_x, short_x, short_len, w_in, w_outgate, w_gates, conv_weight, w_query, w_key, w_value,
    igate_bias, fgate_bias, norm_gain, skip_gain, w_down,
):
    nseq, nwa, nwb = (lax.axis_size(a) for a in ("seq", "wa", "wb"))
    f32, bf16 = jnp.float32, jnp.bfloat16
    rl, kd = long_x.shape
    rs = short_x.shape[1]
    rows = rl + rs
    gw = w_outgate.shape[1]
    hw = w_in.shape[1]
    ow = w_down.shape[1] // (nwa * nwb)
    turned = [w.transpose(1, 2, 0) for w in (w_query, w_key, w_value)]
    vm = pl.BlockSpec(memory_space=pltpu.VMEM)
    hbm = pl.BlockSpec(memory_space=pl.ANY)
    nb, na = nwb - 1, nwa - 1
    dma = pltpu.SemaphoreType.DMA
    shapes = (
        jax.ShapeDtypeStruct((rl, ow), bf16),
        jax.ShapeDtypeStruct((1, rs, ow), bf16),
        jax.ShapeDtypeStruct((1, 1, gw, hw), f32),
        jax.ShapeDtypeStruct((1, 1, hw), f32),
        jax.ShapeDtypeStruct((1, 1), f32),
        jax.ShapeDtypeStruct((1, 3, hw), bf16),
    )
    inputs = (
        short_len[:, None], igate_bias, fgate_bias, long_x, short_x[0], w_in, w_gates.T,
        conv_weight, *turned, norm_gain[None], skip_gain[None], w_outgate, w_down,
    )
    outs = pl.pallas_call(
        functools.partial(mega_kernel, nwa, nwb, nseq),
        out_shape=tuple(pltpu.VMEM(a.shape, a.dtype) for a in shapes),
        in_specs=[pl.BlockSpec(memory_space=pltpu.HBM)] * 15,
        out_specs=(vm,) * 6,
        scratch_shapes=[
            pltpu.VMEM((nwb, rows, kd), bf16),
            pltpu.VMEM((rows, gw), f32),
            pltpu.VMEM((nb, rows, gw), bf16),
            pltpu.VMEM((nb, rows, gw), bf16),
            pltpu.VMEM((8, max(rl, rs)), f32),
            pltpu.VMEM((nb, 8, max(rl, rs)), f32),
            pltpu.VMEM((nwb, rows, gw), bf16),
            pltpu.VMEM((nwb, 16, gw), bf16),
            pltpu.VMEM((8 + rl, gw), f32),
            pltpu.VMEM((8 + rs, gw), f32),
            pltpu.VMEM((rows, gw), f32),
            pltpu.VMEM((nwb, rl, gw), bf16),
            pltpu.VMEM((nwb, rl + rows, gw), bf16),
            pltpu.VMEM((nwb, rl + rows, gw), bf16),
            pltpu.VMEM((8, rl), f32),
            pltpu.VMEM((8, rl), f32),
            pltpu.VMEM((rl, gw), f32),
            pltpu.VMEM((nwa, rows, gw), bf16),
            pltpu.VMEM((nwa, gw, nwb * ow), bf16),
            pltpu.VMEM((rows, nwb * ow), f32),
            pltpu.VMEM((nb, rows, ow), bf16),
            pltpu.VMEM((nb, rows, ow), bf16),
            pltpu.VMEM((3 * nwb, gw, gw), bf16),
            pltpu.VMEM((3 * nwb, gw, gw), bf16),
            pltpu.VMEM(w_in.shape, bf16),
            pltpu.VMEM(w_gates.shape[::-1], bf16),
            pltpu.VMEM(conv_weight.shape, f32),
            pltpu.VMEM(turned[0].shape, f32),
            pltpu.VMEM(turned[1].shape, f32),
            pltpu.VMEM(turned[2].shape, f32),
            pltpu.VMEM((1, gw), f32),
            pltpu.VMEM((1, gw), f32),
            pltpu.VMEM(w_outgate.shape, bf16),
            pltpu.SMEM((1, 1), jnp.int32),
            pltpu.SMEM(igate_bias.shape, f32),
            pltpu.SMEM(fgate_bias.shape, f32),
        ]
        + [dma((3 * nb,))] * 2
        + [dma((nb,))] * 2
        + [dma((3 * nb,))] * 2
        + [dma((nb,))] * 2
        + [dma((nb * na,))] * 2
        + [dma((1,))] * 2
        + [dma((nwb,))] * 6
        + [dma((3 * na,))] * 2
        + [dma((3 * nb,))] * 2
        + [dma((na,))] * 4
        + [dma((15,))],
        compiler_params=pltpu.CompilerParams(
            collective_id=0, has_side_effects=True, vmem_limit_bytes=48 * 2**20
        ),
        name="mlstm_layer",
    )(*(a if a.size == 1 else pltpu.with_memory_space_constraint(a, pltpu.HBM) for a in inputs))
    return pl.pallas_call(
        write_kernel,
        out_shape=shapes,
        in_specs=[vm] * 6,
        out_specs=(pl.BlockSpec(memory_space=pltpu.HBM),) * 6,
        scratch_shapes=[dma((6,))],
        name="write_out",
    )(*(pltpu.with_memory_space_constraint(out, pltpu.VMEM) for out in outs))


def solution(mesh):
    in_specs = (
        P("seq", "wb"),
        P("seq", None, "wb"),
        P("seq"),
        P("wb", "wa"),
        P(None, ("wa", "wb")),
        P(),
        P(None, "wa"),
        P("wa", None, None),
        P("wa", None, None),
        P("wa", None, None),
        P(),
        P(),
        P(("wa", "wb")),
        P(("wa", "wb")),
        P(("wa", "wb"), None),
    )
    out_specs = (
        P("seq", ("wa", "wb")),
        P("seq", None, ("wa", "wb")),
        P("seq", "wa", "wb", None),
        P("seq", "wa", None),
        P("seq", "wa"),
        P("seq", None, "wa"),
    )
    fused = mesh.shape["seq"] == 2 and mesh.shape["wa"] == 4 and mesh.shape["wb"] == 4
    layer = fused_body if fused else body
    return jax.shard_map(layer, mesh=mesh, in_specs=in_specs, out_specs=out_specs, check_vma=False)
```
